32 devices in a mesh: dp: 8 (over z, x), seq: 4 (over y, core).
Axes of the slice: x: 2, y: 2, z: 4, core: 2. Of those that a mesh axis runs over, the one named last changes fastest.
Arguments:
- caption_tokens: bfloat16 [128, 128, 768], P(('dp', 'seq')), may hold values from -6 to 6
- image_tokens: bfloat16 [128, 196, 768], P(('dp', 'seq')), may hold values from -6 to 6
- caption_lengths: int32 [128], P(('dp', 'seq')), may hold values from 8 to 128, as said below
- caption_image: int32 [128], P('dp'), may hold values from 0 to 127, as said below
- norm_gain: bfloat16 [768, 3], P(('dp', 'seq')), may hold values from 0.099609375 to 1.8984375
- norm_bias: bfloat16 [768, 3], P(('dp', 'seq')), may hold values from -1.25 to 1.25
- self_packed: bfloat16 [768, 2304], P(('dp', 'seq')), may hold values from -0.21875 to 0.21875
- self_output: bfloat16 [768, 768], P(('dp', 'seq')), may hold values from -0.625 to 0.625
- cross_query: bfloat16 [768, 768], P(('dp', 'seq')), may hold values from -0.21875 to 0.21875
- cross_pair: bfloat16 [768, 1536], P(('dp', 'seq')), may hold values from -0.21875 to 0.21875
- cross_output: bfloat16 [768, 768], P(('dp', 'seq')), may hold values from -0.75 to 0.75
- expand_weight: bfloat16 [768, 3072], P(('dp', 'seq')), may hold values from -0.21875 to 0.21875
- reduce_weight: bfloat16 [3072, 768], P(('dp', 'seq')), may hold values from -0.109375 to 0.109375
- cotangent: bfloat16 [128, 128, 768], P(('dp', 'seq')), may hold values from -6 to 6
Outputs:
- caption_out: bfloat16 [128, 128, 768], P(('dp', 'seq'))
- caption_grad: bfloat16 [128, 128, 768], P(('dp', 'seq'))
- image_grad: bfloat16 [128, 196, 768], P(('dp', 'seq'))
- gain_grad: float32 [768, 3], P(('dp', 'seq'))
- bias_grad: float32 [768, 3], P(('dp', 'seq'))
- self_packed_grad: float32 [768, 2304], P(('dp', 'seq'))
- self_output_grad: float32 [768, 768], P(('dp', 'seq'))
- cross_query_grad: float32 [768, 768], P(('dp', 'seq'))
- cross_pair_grad: float32 [768, 1536], P(('dp', 'seq'))
- cross_output_grad: float32 [768, 768], P(('dp', 'seq'))
- expand_grad: float32 [768, 3072], P(('dp', 'seq'))
- reduce_grad: float32 [3072, 768], P(('dp', 'seq'))
The draws below stay inside these ranges and needn't reach their ends.
Inputs may be any that keep to these rules, and one draw needn't show every extreme that they name: `caption_lengths`: each aligned block of 4 captions holds at least one caption of length 128. `caption_image`: A permutation of the image indices. Caption c and its image lie in the same aligned block of 16; of each aligned block of 4 captions exactly 1 has its image in each aligned block of 4 images of that group.
All inputs are finite; a program needn't handle non-finite values.
Results may differ from the reference program's by a relative error of at most 0.022.
Values may be sent and summed in bfloat16 or wider, within the bound.
No kernel may reach another device: no remote copies, remote signals or barrier semaphores. Data moves between devices by JAX's collectives and lax.ppermute only.
A program may use at most 192 MiB of HBM per device.

```python
import math
import jax
import jax.numpy as jnp
from jax import lax

D = 768
HEADS = 12
HEAD_DIM = 64
FF = 3072
PATCH = 196
LEN = 128
MIN_LEN = 8
CAP_DEV = 4
GROUP_CAPS = 16
PER_PEER = 1
CAPTIONS = 128


def draw_caption_lengths(key, part):
    base_key, top_key = jax.random.split(key)
    sampled = jax.random.randint(base_key, (CAPTIONS,), MIN_LEN, LEN + 1)
    chosen = jax.random.randint(top_key, (CAPTIONS // CAP_DEV,), 0, CAP_DEV)
    offsets = jnp.arange(CAPTIONS) % CAP_DEV
    longest = offsets == jnp.repeat(chosen, CAP_DEV)
    return jnp.where(longest, LEN, sampled).astype(jnp.int32)


def draw_caption_image(key, part):
    groups = CAPTIONS // GROUP_CAPS
    peer_count = GROUP_CAPS // CAP_DEV
    send_key, place_key = jax.random.split(key)
    ordinal = jnp.broadcast_to(jnp.arange(CAP_DEV, dtype=jnp.int32), (groups * peer_count, CAP_DEV))
    sending = jax.random.permutation(send_key, ordinal, axis=1, independent=True).reshape(groups, peer_count, CAP_DEV)
    target = sending // PER_PEER
    arrival = jnp.arange(peer_count, dtype=jnp.int32)[None, :, None] * PER_PEER + sending % PER_PEER
    placing = jax.random.permutation(place_key, ordinal, axis=1, independent=True).reshape(groups, peer_count * CAP_DEV)
    flat_index = (target * CAP_DEV + arrival).reshape(groups, peer_count * CAP_DEV)
    image_slot = jnp.take_along_axis(placing, flat_index, axis=1).reshape(groups, peer_count, CAP_DEV)
    owner_index = jnp.arange(groups, dtype=jnp.int32)[:, None, None] * peer_count + target
    return (owner_index * CAP_DEV + image_slot).reshape(CAPTIONS).astype(jnp.int32)


def shard_levels(key, dims, cuts, smallest, high):
    factor_of, own = 1.0, jax.random.fold_in(key, 6)
    for dim, shards_of in cuts:
        steps = jnp.exp(jax.random.uniform(jax.random.fold_in(own, dim), (shards_of,), jnp.float32, smallest / len(cuts), high / len(cuts)))
        factor_of = factor_of * jnp.repeat(steps, dims[dim] // shards_of).reshape([-1 if axis == dim else 1 for axis in range(len(dims))])
    return factor_of


def gaussian(rng, dims, scale, most, cuts=(), held_as=jnp.bfloat16):
    level = shard_levels(rng, dims, cuts, -0.22, 0.18) if cuts else 1.0
    values = jax.random.normal(rng, dims, jnp.float32) * scale * level
    return jnp.minimum(jnp.maximum(values, -most), most).astype(held_as)


def setup_inputs(seed: int = 0) -> dict:
    key_list = jax.random.split(jax.random.key(seed), 15)
    caption_tokens = gaussian(key_list[0], (CAPTIONS, LEN, D), 1.0, 6.0, ((0, 32),))
    image_tokens = gaussian(key_list[1], (CAPTIONS, PATCH, D), 1.0, 6.0, ((0, 32),))
    caption_lengths = draw_caption_lengths(jax.random.fold_in(key_list[14], 71), 0)
    caption_image = draw_caption_image(jax.random.fold_in(key_list[14], 71), 0)
    norm_gain = jnp.clip(1.0 + 0.18 * jax.random.normal(key_list[4], (D, 3), jnp.float32), 0.099609375, 1.8984375).astype(jnp.bfloat16)
    norm_bias = gaussian(key_list[5], (D, 3), 0.2, 1.25, ((0, 32),))
    self_packed = gaussian(key_list[6], (D, 3 * D), D ** -0.5, 0.21875, ((0, 32),))
    self_output = gaussian(key_list[7], (D, D), (D // 8) ** -0.5, 0.625, ((0, 32),))
    cross_query = gaussian(key_list[8], (D, D), D ** -0.5, 0.21875, ((0, 32),))
    cross_pair = gaussian(key_list[9], (D, 2 * D), D ** -0.5, 0.21875, ((0, 32),))
    cross_output = gaussian(key_list[10], (D, D), (D // 12) ** -0.5, 0.75, ((0, 32),))
    expand_weight = gaussian(key_list[11], (D, FF), D ** -0.5, 0.21875, ((0, 32),))
    reduce_weight = gaussian(key_list[12], (FF, D), FF ** -0.5, 0.109375, ((0, 32),))
    cotangent = gaussian(key_list[13], (CAPTIONS, LEN, D), 1.0, 6.0, ((0, 32),))
    return {"caption_tokens": caption_tokens, "image_tokens": image_tokens, "caption_lengths": caption_lengths, "caption_image": caption_image, "norm_gain": norm_gain, "norm_bias": norm_bias, "self_packed": self_packed, "self_output": self_output, "cross_query": cross_query, "cross_pair": cross_pair, "cross_output": cross_output, "expand_weight": expand_weight, "reduce_weight": reduce_weight, "cotangent": cotangent}


@jax.custom_vjp
def low(v):
    return lax.optimization_barrier(v.astype(jnp.bfloat16)).astype(jnp.float32)

@jax.custom_vjp
def low_back(v):
    return v

def low_keep(v):
    return (low(v), None)

def low_pass(kept, grad):
    return (grad,)

def back_keep(v):
    return (v, None)

def back_low(kept, grad):
    return (low(grad),)
low.defvjp(low_keep, low_pass)
low_back.defvjp(back_keep, back_low)

def project(values, weight):
    return jnp.einsum('...d,de->...e', values, weight, precision=lax.Precision.HIGHEST)

def layer_norm(values, gain, shift):
    centred = values - lax.optimization_barrier(jnp.mean(values, axis=-1, keepdims=True))
    spread = lax.optimization_barrier(jnp.mean(centred * centred, axis=-1, keepdims=True))
    return centred * lax.rsqrt(spread + 1e-05) * gain + shift

def split_heads(values):
    return values.reshape(values.shape[:-1] + (HEADS, HEAD_DIM))

def attention(query_rows, key_rows, value_rows, score_mask):
    scores = jnp.einsum('bqhe,bkhe->bhqk', split_heads(query_rows), split_heads(key_rows), precision=lax.Precision.HIGHEST) * (1.0 / math.sqrt(HEAD_DIM))
    scores = low_back(scores)
    if score_mask is not None:
        scores = jnp.where(score_mask[:, None], scores, -1e+30)
    row_probs = low(jax.nn.softmax(scores, axis=-1))
    mixed = jnp.einsum('bhqk,bkhe->bqhe', row_probs, split_heads(value_rows), precision=lax.Precision.HIGHEST)
    return mixed.reshape(query_rows.shape)

def block_forward(weights, tokens, paired, lengths_part):
    norm_gain, norm_bias, packed_weight, output_weight, query_weight, pair_weight, cross_weight, expand_weight, reduce_weight = weights
    positions = jnp.arange(LEN)
    live_rows = positions[None, :] < lengths_part[:, None]
    score_mask = (positions[:, None] >= positions[None, :])[None] & live_rows[:, None, :]
    normed_one = low(layer_norm(tokens, norm_gain[:, 0], norm_bias[:, 0]))
    packed = low_back(low(project(normed_one, packed_weight)))
    attended = low_back(low(attention(packed[..., :D], packed[..., D:2 * D], packed[..., 2 * D:], score_mask)))
    after_self = tokens + low_back(project(attended, output_weight))
    normed_two = low_back(low(layer_norm(after_self, norm_gain[:, 1], norm_bias[:, 1])))
    cross_rows = low_back(low(project(normed_two, query_weight)))
    image_pair = low_back(low(project(paired, pair_weight)))
    cross_mixed = low_back(low(attention(cross_rows, image_pair[..., :D], image_pair[..., D:], None)))
    after_cross = after_self + low_back(low(project(cross_mixed, cross_weight)))
    normed_three = low(layer_norm(after_cross, norm_gain[:, 2], norm_bias[:, 2]))
    gate_rows = low_back(project(normed_three, expand_weight))
    hidden = low(jax.nn.gelu(gate_rows, approximate=False))
    return jnp.where(live_rows[..., None], after_cross + project(hidden, reduce_weight), 0.0)

def reference(caption_tokens, image_tokens, caption_lengths, caption_image, norm_gain, norm_bias, self_packed, self_output, cross_query, cross_pair, cross_output, expand_weight, reduce_weight, cotangent):
    floats = [member.astype(jnp.float32) for member in (caption_tokens, image_tokens, norm_gain, norm_bias, self_packed, self_output, cross_query, cross_pair, cross_output, expand_weight, reduce_weight)]
    block_count = CAPTIONS // 32
    length_blocks = caption_lengths.reshape(block_count, 32)
    step_block = jax.checkpoint(block_forward)

    def forward(tokens, patches, *weights):
        paired = jnp.take(patches, caption_image, axis=0)

        def scan_step(carry, pieces):
            return (carry, step_block(weights, pieces[0], pieces[1], pieces[2]))
        _, outputs = lax.scan(scan_step, jnp.zeros((), jnp.float32), (tokens.reshape(block_count, 32, LEN, D), paired.reshape(block_count, 32, PATCH, D), length_blocks))
        return outputs.reshape(CAPTIONS, LEN, D)
    result, pullback = jax.vjp(forward, *floats)
    grads = pullback(cotangent.astype(jnp.float32))
    return (result.astype(jnp.bfloat16), grads[0].astype(jnp.bfloat16), grads[1].astype(jnp.bfloat16), grads[2], grads[3], grads[4], grads[5], grads[6], grads[7], grads[8], grads[9], grads[10])
```

```python
import math

import jax
import jax.numpy as jnp
from jax import lax
from jax.sharding import PartitionSpec as P

HEADS = 12
HEAD_DIM = 64


epsilon = 1e-05


def split_heads(values):
    return values.reshape(values.shape[:-1] + (HEADS, HEAD_DIM))


def project(values, weight):
    flat_rows = values.reshape(-1, values.shape[-1])
    return jnp.dot(flat_rows, weight, preferred_element_type=jnp.float32).reshape(
        values.shape[:-1] + (weight.shape[1],)
    )


def project_back(values, weight):
    flat_rows = values.reshape(-1, values.shape[-1])
    result = lax.dot_general(
        flat_rows, weight, (((1,), (1,)), ((), ())), preferred_element_type=jnp.float32
    )
    return result.reshape(values.shape[:-1] + (weight.shape[0],))


def weight_grad(left_rows, right_rows):
    return lax.dot_general(
        left_rows.reshape(-1, left_rows.shape[-1]),
        right_rows.reshape(-1, right_rows.shape[-1]),
        (((0,), (0,)), ((), ())),
        preferred_element_type=jnp.float32,
    )


def layer_norm(values, gain, shift):
    centred = values - jnp.mean(values, axis=-1, keepdims=True)
    spread = jnp.mean(centred * centred, axis=-1, keepdims=True)
    inverse = lax.rsqrt(spread + epsilon)
    scaled = centred * inverse
    return (scaled * gain + shift, scaled, inverse)


def norm_back(grad_rows, scaled, inverse, gain):
    weighted = grad_rows * gain
    result = inverse * (
        weighted
        - jnp.mean(weighted, axis=-1, keepdims=True)
        - scaled * jnp.mean(weighted * scaled, axis=-1, keepdims=True)
    )
    flat_grad = grad_rows.reshape(-1, grad_rows.shape[-1])
    flat_scaled = scaled.reshape(-1, scaled.shape[-1])
    return (result, jnp.sum(flat_grad * flat_scaled, axis=0), jnp.sum(flat_grad, axis=0))


def gelu_exact(values):
    return jax.nn.gelu(values, approximate=False)


def causal_mask(lengths_part, seq_len):
    positions = jnp.arange(seq_len)
    live_rows = positions[None, :] < lengths_part[:, None]
    return (positions[:, None] >= positions[None, :])[None] & live_rows[:, None, :]


def score_block(query_rows, key_rows, score_mask):
    score_scale = 1.0 / math.sqrt(HEAD_DIM)
    scores = (
        jnp.einsum(
            "bqhe,bkhe->bhqk",
            split_heads(query_rows),
            split_heads(key_rows),
            preferred_element_type=jnp.float32,
        )
        * score_scale
    )
    if score_mask is not None:
        scores = jnp.where(score_mask[:, None], scores, -1e30)
    return scores


def attend(query_rows, key_rows, value_rows, score_mask):
    scores = score_block(query_rows, key_rows, score_mask)
    row_peak = jnp.max(scores, axis=-1, keepdims=True)
    expanded = jnp.exp(scores - row_peak)
    row_total = jnp.sum(expanded, axis=-1, keepdims=True)
    row_probs = (expanded / row_total).astype(jnp.bfloat16)
    mixed = jnp.einsum(
        "bhqk,bkhe->bqhe", row_probs, split_heads(value_rows), preferred_element_type=jnp.float32
    )
    return (
        mixed.reshape(query_rows.shape).astype(jnp.bfloat16),
        (row_peak + jnp.log(row_total))[..., 0],
    )


def attend_back(query_rows, key_rows, value_rows, score_mask, logsum, grad_rows):
    score_scale = 1.0 / math.sqrt(HEAD_DIM)
    scores = score_block(query_rows, key_rows, score_mask)
    row_probs = jnp.exp(scores - logsum[..., None])
    grad_heads = split_heads(grad_rows)
    grad_value = jnp.einsum(
        "bhqk,bqhe->bkhe",
        row_probs.astype(jnp.bfloat16),
        grad_heads,
        preferred_element_type=jnp.float32,
    )
    grad_probs = jnp.einsum(
        "bqhe,bkhe->bhqk", grad_heads, split_heads(value_rows), preferred_element_type=jnp.float32
    )
    grad_scores = (
        row_probs * (grad_probs - jnp.sum(grad_probs * row_probs, axis=-1, keepdims=True))
    ).astype(jnp.bfloat16)
    grad_query = (
        jnp.einsum(
            "bhqk,bkhe->bqhe",
            grad_scores,
            split_heads(key_rows),
            preferred_element_type=jnp.float32,
        )
        * score_scale
    )
    grad_key = (
        jnp.einsum(
            "bhqk,bqhe->bkhe",
            grad_scores,
            split_heads(query_rows),
            preferred_element_type=jnp.float32,
        )
        * score_scale
    )
    return (
        grad_query.reshape(query_rows.shape).astype(jnp.bfloat16),
        grad_key.reshape(key_rows.shape).astype(jnp.bfloat16),
        grad_value.reshape(value_rows.shape).astype(jnp.bfloat16),
    )


def self_forward(query_rows, key_rows, value_rows, lengths_part):
    return attend(query_rows, key_rows, value_rows, causal_mask(lengths_part, query_rows.shape[1]))


def cross_forward(query_rows, key_rows, value_rows):
    return attend(query_rows, key_rows, value_rows, None)


def self_backward(query_rows, key_rows, value_rows, lengths_part, logsum, grad_rows):
    return attend_back(
        query_rows,
        key_rows,
        value_rows,
        causal_mask(lengths_part, query_rows.shape[1]),
        logsum,
        grad_rows,
    )


def cross_backward(query_rows, key_rows, value_rows, logsum, grad_rows):
    return attend_back(query_rows, key_rows, value_rows, None, logsum, grad_rows)


def index_bits():
    found = []
    for axis in ("dp", "seq"):
        count = lax.axis_size(axis)
        found += [(axis, bit) for bit in reversed(range(count.bit_length() - 1))]
    return found


def swap_pairs(axis, bit):
    return [(i, i ^ (1 << bit)) for i in range(lax.axis_size(axis))]


def own_bit(axis, bit):
    return (lax.axis_index(axis) >> bit) & 1


def gather_order(flip):
    far = [("dp", bit) for bit in range(1, lax.axis_size("dp").bit_length() - 1)]
    near = [[("dp", 0)], [("seq", bit) for bit in range(1, lax.axis_size("seq").bit_length() - 1)]]
    if flip:
        near = near[::-1]
    return far + near[0] + near[1] + [("seq", 0)]


def gather_rows(part, flip):
    bits = index_bits()
    state = part.reshape((1,) * len(bits) + part.shape)
    for place in gather_order(flip):
        dim = bits.index(place)
        other = lax.ppermute(state, place[0], swap_pairs(*place))
        state = jnp.where(
            own_bit(*place) == 0,
            jnp.concatenate([state, other], dim),
            jnp.concatenate([other, state], dim),
        )
    return state.reshape((-1,) + part.shape[1:])


def scatter_rows(whole, flip):
    bits = index_bits()
    rows = whole.shape[0] >> len(bits)
    state = whole.reshape((2,) * len(bits) + (rows,) + whole.shape[1:])
    order = gather_order(flip)
    for place in [order[-1]] + order[:-1][::-1]:
        dim = bits.index(place)
        mine = own_bit(*place)
        given = lax.dynamic_slice_in_dim(state, 1 - mine, 1, dim)
        kept = lax.dynamic_slice_in_dim(state, mine, 1, dim)
        state = kept + lax.ppermute(given, place[0], swap_pairs(*place))
    return state.reshape((rows,) + whole.shape[1:])


def route(table_rows, pick, place):
    peers = lax.axis_size("seq")
    position = lax.axis_index("seq")
    arrived = []
    for k in range(peers):
        rows = jnp.take(table_rows, pick[position ^ k], axis=0)
        if k:
            rows = lax.ppermute(rows, "seq", [(i, i ^ k) for i in range(peers)])
        arrived.append(rows)
    return jnp.take(jnp.concatenate(arrived, axis=0), place, axis=0)


def shards(
    caption_tokens,
    image_tokens,
    caption_lengths,
    caption_image,
    norm_gain,
    norm_bias,
    self_packed,
    self_output,
    cross_query,
    cross_pair,
    cross_output,
    expand_weight,
    reduce_weight,
    cotangent,
):
    captions, seq_len, model_width = caption_tokens.shape
    peer_count = lax.axis_size("seq")
    position = lax.axis_index("seq")
    per_peer = captions // peer_count

    owner = (caption_image // captions % peer_count).reshape(peer_count, captions)
    slot = (caption_image % captions).reshape(peer_count, captions)
    by_owner = jnp.argsort(owner, axis=1, stable=True).reshape(peer_count, peer_count, per_peer)
    slot_by_owner = jnp.take_along_axis(
        slot, by_owner.reshape(peer_count, captions), axis=1
    ).reshape(peer_count, peer_count, per_peer)
    asked = slot_by_owner[:, position]
    held = by_owner[position]
    turns = position ^ jnp.arange(peer_count)
    image_place = jnp.argsort(held[turns].reshape(-1))
    home_place = jnp.argsort(asked[turns].reshape(-1))
    paired = route(image_tokens, asked, image_place)

    norm_columns = jnp.pad(jnp.concatenate([norm_gain, norm_bias], axis=1), ((0, 0), (0, 122)))
    first_group = gather_rows(jnp.concatenate([self_packed, norm_columns], axis=1), False)
    second_group = gather_rows(
        jnp.concatenate([cross_pair, self_output, cross_query, cross_output], axis=1), True
    )
    expand_full = gather_rows(expand_weight, False)
    reduce_full = gather_rows(reduce_weight, True)
    packed_weight = first_group[:, : 3 * model_width]
    norm_values = first_group[:, 3 * model_width : 3 * model_width + 6].astype(jnp.float32)
    norm_gains, norm_shifts = norm_values[:, :3], norm_values[:, 3:]
    pair_weight = second_group[:, : 2 * model_width]
    output_weight = second_group[:, 2 * model_width : 3 * model_width]
    query_weight = second_group[:, 3 * model_width : 4 * model_width]
    cross_weight = second_group[:, 4 * model_width :]

    live_rows = jnp.arange(seq_len)[None, :] < caption_lengths[:, None]
    inputs = caption_tokens.astype(jnp.float32)
    normed_full, scaled_one, inverse_one = layer_norm(inputs, norm_gains[:, 0], norm_shifts[:, 0])
    normed_one = normed_full.astype(jnp.bfloat16)
    packed = project(normed_one, packed_weight).astype(jnp.bfloat16)
    query_part = packed[..., :model_width]
    key_part = packed[..., model_width : 2 * model_width]
    value_part = packed[..., 2 * model_width :]
    attended, logsum_one = self_forward(query_part, key_part, value_part, caption_lengths)
    after_self = inputs + project(attended, output_weight)
    normed_full_two, scaled_two, inverse_two = layer_norm(
        after_self, norm_gains[:, 1], norm_shifts[:, 1]
    )
    normed_two = normed_full_two.astype(jnp.bfloat16)
    image_pair = project(paired, pair_weight).astype(jnp.bfloat16)
    image_key = image_pair[..., :model_width]
    image_value = image_pair[..., model_width:]
    query_rows = project(normed_two, query_weight).astype(jnp.bfloat16)
    mixed_rows, logsum_two = cross_forward(query_rows, image_key, image_value)
    branch = project(mixed_rows, cross_weight).astype(jnp.bfloat16)
    after_cross = after_self + branch.astype(jnp.float32)
    normed_full_three, scaled_three, inverse_three = layer_norm(
        after_cross, norm_gains[:, 2], norm_shifts[:, 2]
    )
    normed_three = normed_full_three.astype(jnp.bfloat16)
    gate_rows = project(normed_three, expand_full)
    hidden = gelu_exact(gate_rows).astype(jnp.bfloat16)
    caption_out = jnp.where(
        live_rows[..., None], after_cross + project(hidden, reduce_full), 0.0
    ).astype(jnp.bfloat16)

    grad_out = jnp.where(live_rows[..., None], cotangent, jnp.zeros_like(cotangent))
    reduce_grad = scatter_rows(weight_grad(hidden, grad_out).astype(jnp.bfloat16), True)
    _, gelu_pull = jax.vjp(gelu_exact, gate_rows)
    grad_gate = gelu_pull(project_back(grad_out, reduce_full))[0].astype(jnp.bfloat16)
    expand_grad = scatter_rows(weight_grad(normed_three, grad_gate).astype(jnp.bfloat16), False)
    grad_norm_three, gain_three, shift_three = norm_back(
        project_back(grad_gate, expand_full), scaled_three, inverse_three, norm_gains[:, 2]
    )
    grad_second = grad_out.astype(jnp.float32) + grad_norm_three
    grad_branch = grad_second.astype(jnp.bfloat16)
    cross_output_grad = weight_grad(mixed_rows, grad_branch)
    grad_cross_mixed = project_back(grad_branch, cross_weight).astype(jnp.bfloat16)
    grad_cross_rows, grad_image_key, grad_image_value = cross_backward(
        query_rows, image_key, image_value, logsum_two, grad_cross_mixed
    )
    grad_pair = jnp.concatenate([grad_image_key, grad_image_value], axis=-1)
    cross_pair_grad = weight_grad(paired, grad_pair)
    image_grad = route(
        project_back(grad_pair, pair_weight).astype(jnp.bfloat16), held, home_place
    )
    cross_query_grad = weight_grad(normed_two, grad_cross_rows)
    cross_sums = scatter_rows(
        jnp.concatenate([cross_pair_grad, cross_query_grad, cross_output_grad], axis=1).astype(
            jnp.bfloat16
        ),
        True,
    )
    grad_norm_two, gain_two, shift_two = norm_back(
        project_back(grad_cross_rows, query_weight).astype(jnp.bfloat16).astype(jnp.float32),
        scaled_two,
        inverse_two,
        norm_gains[:, 1],
    )
    grad_first = grad_second + grad_norm_two
    grad_self = grad_first.astype(jnp.bfloat16)
    self_output_grad = weight_grad(attended, grad_self)
    grad_attended = project_back(grad_self, output_weight).astype(jnp.bfloat16)
    grad_query, grad_key, grad_value = self_backward(
        query_part, key_part, value_part, caption_lengths, logsum_one, grad_attended
    )
    grad_packed = jnp.concatenate([grad_query, grad_key, grad_value], axis=-1)
    self_packed_grad = weight_grad(normed_one, grad_packed)
    grad_norm_one, gain_one, shift_one = norm_back(
        project_back(grad_packed, packed_weight), scaled_one, inverse_one, norm_gains[:, 0]
    )
    caption_grad = (grad_first + grad_norm_one).astype(jnp.bfloat16)
    norm_sums = jnp.stack([gain_one, gain_two, gain_three, shift_one, shift_two, shift_three], axis=1)
    self_sums = scatter_rows(
        jnp.concatenate(
            [self_packed_grad, self_output_grad, jnp.pad(norm_sums, ((0, 0), (0, 122)))], axis=1
        ).astype(jnp.bfloat16),
        False,
    )
    widen = lambda member: member.astype(jnp.float32)
    cross_sums, self_sums = widen(cross_sums), widen(self_sums)
    return (
        caption_out,
        caption_grad,
        image_grad,
        self_sums[:, 4 * model_width : 4 * model_width + 3],
        self_sums[:, 4 * model_width + 3 : 4 * model_width + 6],
        self_sums[:, : 3 * model_width],
        self_sums[:, 3 * model_width : 4 * model_width],
        cross_sums[:, 2 * model_width : 3 * model_width],
        cross_sums[:, : 2 * model_width],
        cross_sums[:, 3 * model_width :],
        widen(expand_grad),
        widen(reduce_grad),
    )


def solution(mesh):
    placed = (
        P(("dp", "seq"), None, None),
        P(("dp", "seq"), None, None),
        P(("dp", "seq")),
        P("dp"),
        P(("dp", "seq"), None),
        P(("dp", "seq"), None),
        P(("dp", "seq"), None),
        P(("dp", "seq"), None),
        P(("dp", "seq"), None),
        P(("dp", "seq"), None),
        P(("dp", "seq"), None),
        P(("dp", "seq"), None),
        P(("dp", "seq"), None),
        P(("dp", "seq"), None, None),
    )
    return jax.shard_map(
        shards,
        mesh=mesh,
        in_specs=placed,
        out_specs=(
            P(("dp", "seq"), None, None),
            P(("dp", "seq"), None, None),
            P(("dp", "seq"), None, None),
            P(("dp", "seq"), None),
            P(("dp", "seq"), None),
            P(("dp", "seq"), None),
            P(("dp", "seq"), None),
            P(("dp", "seq"), None),
            P(("dp", "seq"), None),
            P(("dp", "seq"), None),
            P(("dp", "seq"), None),
            P(("dp", "seq"), None),
        ),
        check_vma=False,
    )
```

```python
import math

import jax
import jax.numpy as jnp
from jax import lax
from jax.sharding import PartitionSpec as P

HEADS = 12
HEAD_DIM = 64


epsilon = 1e-05


def split_heads(values):
    return values.reshape(values.shape[:-1] + (HEADS, HEAD_DIM))


def project(values, weight):
    flat_rows = values.reshape(-1, values.shape[-1])
    return jnp.dot(flat_rows, weight, preferred_element_type=jnp.float32).reshape(
        values.shape[:-1] + (weight.shape[1],)
    )


def project_back(values, weight):
    flat_rows = values.reshape(-1, values.shape[-1])
    result = lax.dot_general(
        flat_rows, weight, (((1,), (1,)), ((), ())), preferred_element_type=jnp.float32
    )
    return result.reshape(values.shape[:-1] + (weight.shape[0],))


def weight_grad(left_rows, right_rows):
    return lax.dot_general(
        left_rows.reshape(-1, left_rows.shape[-1]),
        right_rows.reshape(-1, right_rows.shape[-1]),
        (((0,), (0,)), ((), ())),
        preferred_element_type=jnp.float32,
    )


def layer_norm(values, gain, shift):
    centred = values - jnp.mean(values, axis=-1, keepdims=True)
    spread = jnp.mean(centred * centred, axis=-1, keepdims=True)
    inverse = lax.rsqrt(spread + epsilon)
    scaled = centred * inverse
    return (scaled * gain + shift, scaled, inverse)


def norm_back(grad_rows, scaled, inverse, gain):
    weighted = grad_rows * gain
    result = inverse * (
        weighted
        - jnp.mean(weighted, axis=-1, keepdims=True)
        - scaled * jnp.mean(weighted * scaled, axis=-1, keepdims=True)
    )
    flat_grad = grad_rows.reshape(-1, grad_rows.shape[-1])
    flat_scaled = scaled.reshape(-1, scaled.shape[-1])
    return (result, jnp.sum(flat_grad * flat_scaled, axis=0), jnp.sum(flat_grad, axis=0))


def gelu_exact(values):
    return jax.nn.gelu(values, approximate=False)


def causal_mask(lengths_part, seq_len):
    positions = jnp.arange(seq_len)
    live_rows = positions[None, :] < lengths_part[:, None]
    return (positions[:, None] >= positions[None, :])[None] & live_rows[:, None, :]


def score_block(query_rows, key_rows, score_mask):
    score_scale = 1.0 / math.sqrt(HEAD_DIM)
    scores = (
        jnp.einsum(
            "bqhe,bkhe->bhqk",
            split_heads(query_rows),
            split_heads(key_rows),
            preferred_element_type=jnp.float32,
        )
        * score_scale
    )
    if score_mask is not None:
        scores = jnp.where(score_mask[:, None], scores, -1e30)
    return scores


def attend(query_rows, key_rows, value_rows, score_mask):
    scores = score_block(query_rows, key_rows, score_mask)
    row_peak = jnp.max(scores, axis=-1, keepdims=True)
    expanded = jnp.exp(scores - row_peak)
    row_total = jnp.sum(expanded, axis=-1, keepdims=True)
    row_probs = (expanded / row_total).astype(jnp.bfloat16)
    mixed = jnp.einsum(
        "bhqk,bkhe->bqhe", row_probs, split_heads(value_rows), preferred_element_type=jnp.float32
    )
    return (
        mixed.reshape(query_rows.shape).astype(jnp.bfloat16),
        (row_peak + jnp.log(row_total))[..., 0],
    )


def attend_back(query_rows, key_rows, value_rows, score_mask, logsum, grad_rows):
    score_scale = 1.0 / math.sqrt(HEAD_DIM)
    scores = score_block(query_rows, key_rows, score_mask)
    row_probs = jnp.exp(scores - logsum[..., None])
    grad_heads = split_heads(grad_rows)
    grad_value = jnp.einsum(
        "bhqk,bqhe->bkhe",
        row_probs.astype(jnp.bfloat16),
        grad_heads,
        preferred_element_type=jnp.float32,
    )
    grad_probs = jnp.einsum(
        "bqhe,bkhe->bhqk", grad_heads, split_heads(value_rows), preferred_element_type=jnp.float32
    )
    grad_scores = (
        row_probs * (grad_probs - jnp.sum(grad_probs * row_probs, axis=-1, keepdims=True))
    ).astype(jnp.bfloat16)
    grad_query = (
        jnp.einsum(
            "bhqk,bkhe->bqhe",
            grad_scores,
            split_heads(key_rows),
            preferred_element_type=jnp.float32,
        )
        * score_scale
    )
    grad_key = (
        jnp.einsum(
            "bhqk,bqhe->bkhe",
            grad_scores,
            split_heads(query_rows),
            preferred_element_type=jnp.float32,
        )
        * score_scale
    )
    return (
        grad_query.reshape(query_rows.shape).astype(jnp.bfloat16),
        grad_key.reshape(key_rows.shape).astype(jnp.bfloat16),
        grad_value.reshape(value_rows.shape).astype(jnp.bfloat16),
    )


def self_forward(query_rows, key_rows, value_rows, lengths_part):
    return attend(query_rows, key_rows, value_rows, causal_mask(lengths_part, query_rows.shape[1]))


def cross_forward(query_rows, key_rows, value_rows):
    return attend(query_rows, key_rows, value_rows, None)


def self_backward(query_rows, key_rows, value_rows, lengths_part, logsum, grad_rows):
    return attend_back(
        query_rows,
        key_rows,
        value_rows,
        causal_mask(lengths_part, query_rows.shape[1]),
        logsum,
        grad_rows,
    )


def cross_backward(query_rows, key_rows, value_rows, logsum, grad_rows):
    return attend_back(query_rows, key_rows, value_rows, None, logsum, grad_rows)


def index_bits():
    found = []
    for axis in ("dp", "seq"):
        count = lax.axis_size(axis)
        found += [(axis, bit) for bit in reversed(range(count.bit_length() - 1))]
    return found


def swap_pairs(axis, bit):
    return [(i, i ^ (1 << bit)) for i in range(lax.axis_size(axis))]


def own_bit(axis, bit):
    return (lax.axis_index(axis) >> bit) & 1


def gather_order(flip):
    far = [("dp", bit) for bit in range(1, lax.axis_size("dp").bit_length() - 1)]
    near = [[("dp", 0)], [("seq", bit) for bit in range(1, lax.axis_size("seq").bit_length() - 1)]]
    if flip:
        near = near[::-1]
    return far + near[0] + near[1] + [("seq", 0)]


def gather_rows(part, flip):
    bits = index_bits()
    own = [own_bit(*place) for place in bits]
    rest = [0] * part.ndim
    known = [1] * len(bits)
    piece = part.reshape((1,) * len(bits) + part.shape)
    whole = jnp.zeros((2,) * len(bits) + part.shape, part.dtype)
    whole = lax.dynamic_update_slice(whole, piece, own + rest)
    for place in gather_order(flip):
        dim = bits.index(place)
        starts = [0 if size == 2 else bit for size, bit in zip(known, own)]
        if max(known) == 2:
            piece = lax.dynamic_slice(whole, starts + rest, known + list(part.shape))
        other = lax.ppermute(piece, place[0], swap_pairs(*place))
        starts[dim] = 1 - own[dim]
        whole = lax.dynamic_update_slice(whole, other, starts + rest)
        known[dim] = 2
    return whole.reshape((-1,) + part.shape[1:])


class Scatter:
    def __init__(self, whole, flip):
        bits = index_bits()
        self.rows = whole.shape[0] >> len(bits)
        self.tail = whole.shape[1:]
        self.state = whole.reshape((2,) * len(bits) + (self.rows,) + self.tail)
        order = gather_order(flip)
        self.left = [order[-1]] + order[:-1][::-1]

    def step(self):
        place = self.left.pop(0)
        dim = index_bits().index(place)
        mine = own_bit(*place)
        given = lax.dynamic_slice_in_dim(self.state, 1 - mine, 1, dim)
        kept = lax.dynamic_slice_in_dim(self.state, mine, 1, dim)
        self.state = kept + lax.ppermute(given, place[0], swap_pairs(*place))

    def finish(self):
        while self.left:
            self.step()
        return self.state.reshape((self.rows,) + self.tail).astype(jnp.float32)


def tie(scatters, *values):
    held = lax.optimization_barrier(tuple(one.state for one in scatters) + values)
    for one, state in zip(scatters, held):
        one.state = state
    return held[len(scatters):] if len(values) > 1 else held[-1]


def route(table_rows, pick, place):
    peers = lax.axis_size("seq")
    position = lax.axis_index("seq")
    arrived = []
    for k in range(peers):
        rows = jnp.take(table_rows, pick[position ^ k], axis=0)
        if k:
            rows = lax.ppermute(rows, "seq", [(i, i ^ k) for i in range(peers)])
        arrived.append(rows)
    return jnp.take(jnp.concatenate(arrived, axis=0), place, axis=0)


def shards(
    caption_tokens,
    image_tokens,
    caption_lengths,
    caption_image,
    norm_gain,
    norm_bias,
    self_packed,
    self_output,
    cross_query,
    cross_pair,
    cross_output,
    expand_weight,
    reduce_weight,
    cotangent,
):
    captions, seq_len, model_width = caption_tokens.shape
    peer_count = lax.axis_size("seq")
    position = lax.axis_index("seq")
    per_peer = captions // peer_count

    owner = (caption_image // captions % peer_count).reshape(peer_count, captions)
    slot = (caption_image % captions).reshape(peer_count, captions)
    by_owner = jnp.argsort(owner, axis=1, stable=True).reshape(peer_count, peer_count, per_peer)
    slot_by_owner = jnp.take_along_axis(
        slot, by_owner.reshape(peer_count, captions), axis=1
    ).reshape(peer_count, peer_count, per_peer)
    asked = slot_by_owner[:, position]
    held = by_owner[position]
    turns = position ^ jnp.arange(peer_count)
    image_place = jnp.argsort(held[turns].reshape(-1))
    home_place = jnp.argsort(asked[turns].reshape(-1))
    paired = route(image_tokens, asked, image_place)

    norm_columns = jnp.pad(jnp.concatenate([norm_gain, norm_bias], axis=1), ((0, 0), (0, 122)))
    first_group = gather_rows(jnp.concatenate([self_packed, norm_columns], axis=1), False)
    rows = self_packed.shape[0]
    ratio = reduce_weight.shape[0] // rows
    reduce_blocks = [reduce_weight[k * rows : (k + 1) * rows] for k in range(ratio)]
    others = lax.all_gather(
        jnp.concatenate(
            [cross_pair, self_output, cross_query, cross_output, expand_weight] + reduce_blocks,
            axis=1,
        ),
        ("dp", "seq"),
        axis=0,
        tiled=True,
    )
    packed_weight = first_group[:, : 3 * model_width]
    norm_values = first_group[:, 3 * model_width : 3 * model_width + 6].astype(jnp.float32)
    norm_gains, norm_shifts = norm_values[:, :3], norm_values[:, 3:]
    pair_weight = others[:, : 2 * model_width]
    output_weight = others[:, 2 * model_width : 3 * model_width]
    query_weight = others[:, 3 * model_width : 4 * model_width]
    cross_weight = others[:, 4 * model_width : 5 * model_width]
    hidden_width = expand_weight.shape[1]
    expand_full = others[:, 5 * model_width : 5 * model_width + hidden_width]
    reduce_full = (
        others[:, 5 * model_width + hidden_width :]
        .reshape(-1, rows, ratio, model_width)
        .transpose(0, 2, 1, 3)
        .reshape(-1, model_width)
    )

    live_rows = jnp.arange(seq_len)[None, :] < caption_lengths[:, None]
    inputs = caption_tokens.astype(jnp.float32)
    normed_full, scaled_one, inverse_one = layer_norm(inputs, norm_gains[:, 0], norm_shifts[:, 0])
    normed_one = normed_full.astype(jnp.bfloat16)
    packed = project(normed_one, packed_weight).astype(jnp.bfloat16)
    query_part = packed[..., :model_width]
    key_part = packed[..., model_width : 2 * model_width]
    value_part = packed[..., 2 * model_width :]
    attended, logsum_one = self_forward(query_part, key_part, value_part, caption_lengths)
    after_self = inputs + project(attended, output_weight)
    normed_full_two, scaled_two, inverse_two = layer_norm(
        after_self, norm_gains[:, 1], norm_shifts[:, 1]
    )
    normed_two = normed_full_two.astype(jnp.bfloat16)
    image_pair = project(paired, pair_weight).astype(jnp.bfloat16)
    image_key = image_pair[..., :model_width]
    image_value = image_pair[..., model_width:]
    query_rows = project(normed_two, query_weight).astype(jnp.bfloat16)
    mixed_rows, logsum_two = cross_forward(query_rows, image_key, image_value)
    branch = project(mixed_rows, cross_weight).astype(jnp.bfloat16)
    after_cross = after_self + branch.astype(jnp.float32)
    normed_full_three, scaled_three, inverse_three = layer_norm(
        after_cross, norm_gains[:, 2], norm_shifts[:, 2]
    )
    normed_three = normed_full_three.astype(jnp.bfloat16)
    gate_rows = project(normed_three, expand_full)
    hidden = gelu_exact(gate_rows).astype(jnp.bfloat16)
    caption_out = jnp.where(
        live_rows[..., None], after_cross + project(hidden, reduce_full), 0.0
    ).astype(jnp.bfloat16)

    grad_out = jnp.where(live_rows[..., None], cotangent, jnp.zeros_like(cotangent))
    narrow = lambda member: member.astype(jnp.bfloat16)
    reduce_sums = Scatter(narrow(weight_grad(hidden, grad_out)), True)
    grad_late = tie([reduce_sums], grad_out)
    reduce_sums.step()
    _, gelu_pull = jax.vjp(gelu_exact, gate_rows)
    grad_gate = gelu_pull(project_back(grad_late, reduce_full))[0].astype(jnp.bfloat16)
    expand_sums = Scatter(narrow(weight_grad(normed_three, grad_gate)), False)
    grad_gate = tie([reduce_sums, expand_sums], grad_gate)
    reduce_sums.step()
    expand_sums.step()
    grad_norm_three, gain_three, shift_three = norm_back(
        project_back(grad_gate, expand_full), scaled_three, inverse_three, norm_gains[:, 2]
    )
    grad_second = grad_out.astype(jnp.float32) + grad_norm_three
    grad_branch = grad_second.astype(jnp.bfloat16)
    cross_output_grad = weight_grad(mixed_rows, grad_branch)
    grad_cross_mixed = project_back(grad_branch, cross_weight).astype(jnp.bfloat16)
    grad_cross_mixed = tie([expand_sums], grad_cross_mixed)
    expand_sums.step()
    grad_cross_rows, grad_image_key, grad_image_value = cross_backward(
        query_rows, image_key, image_value, logsum_two, grad_cross_mixed
    )
    grad_pair = jnp.concatenate([grad_image_key, grad_image_value], axis=-1)
    grad_cross_rows, grad_pair = tie([reduce_sums, expand_sums], grad_cross_rows, grad_pair)
    reduce_sums.step()
    expand_sums.step()
    image_grad = route(
        project_back(grad_pair, pair_weight).astype(jnp.bfloat16), held, home_place
    )
    cross_pair_grad = weight_grad(paired, grad_pair)
    cross_query_grad = weight_grad(normed_two, grad_cross_rows)
    grad_norm_two, gain_two, shift_two = norm_back(
        project_back(grad_cross_rows, query_weight).astype(jnp.bfloat16).astype(jnp.float32),
        scaled_two,
        inverse_two,
        norm_gains[:, 1],
    )
    grad_first = grad_second + grad_norm_two
    grad_self = grad_first.astype(jnp.bfloat16)
    self_output_grad = weight_grad(attended, grad_self)
    cross_sums = Scatter(
        narrow(
            jnp.concatenate(
                [cross_pair_grad, cross_query_grad, cross_output_grad, self_output_grad], axis=1
            )
        ),
        True,
    )
    grad_self = tie([reduce_sums, expand_sums, cross_sums], grad_self)
    reduce_sums.step()
    expand_sums.step()
    cross_sums.step()
    grad_attended = project_back(grad_self, output_weight).astype(jnp.bfloat16)
    grad_query, grad_key, grad_value = self_backward(
        query_part, key_part, value_part, caption_lengths, logsum_one, grad_attended
    )
    grad_packed = jnp.concatenate([grad_query, grad_key, grad_value], axis=-1)
    grad_packed = tie([reduce_sums, expand_sums, cross_sums], grad_packed)
    cross_sums.step()
    self_packed_grad = weight_grad(normed_one, grad_packed)
    grad_norm_one, gain_one, shift_one = norm_back(
        project_back(grad_packed, packed_weight), scaled_one, inverse_one, norm_gains[:, 0]
    )
    caption_grad = (grad_first + grad_norm_one).astype(jnp.bfloat16)
    norm_sums = jnp.stack([gain_one, gain_two, gain_three, shift_one, shift_two, shift_three], axis=1)
    half = 3 * model_width // 2
    first_sums = Scatter(narrow(self_packed_grad[:, :half]), False)
    second_sums = Scatter(
        narrow(
            jnp.concatenate(
                [self_packed_grad[:, half:], jnp.pad(norm_sums, ((0, 0), (0, 122)))], axis=1
            )
        ),
        True,
    )
    reduce_grad, expand_grad = reduce_sums.finish(), expand_sums.finish()
    first_sums, second_sums = first_sums.finish(), second_sums.finish()
    cross_sums = cross_sums.finish()
    return (
        caption_out,
        caption_grad,
        image_grad,
        second_sums[:, half : half + 3],
        second_sums[:, half + 3 : half + 6],
        jnp.concatenate([first_sums, second_sums[:, :half]], axis=1),
        cross_sums[:, 4 * model_width :],
        cross_sums[:, 2 * model_width : 3 * model_width],
        cross_sums[:, : 2 * model_width],
        cross_sums[:, 3 * model_width : 4 * model_width],
        expand_grad,
        reduce_grad,
    )


def solution(mesh):
    placed = (
        P(("dp", "seq"), None, None),
        P(("dp", "seq"), None, None),
        P(("dp", "seq")),
        P("dp"),
        P(("dp", "seq"), None),
        P(("dp", "seq"), None),
        P(("dp", "seq"), None),
        P(("dp", "seq"), None),
        P(("dp", "seq"), None),
        P(("dp", "seq"), None),
        P(("dp", "seq"), None),
        P(("dp", "seq"), None),
        P(("dp", "seq"), None),
        P(("dp", "seq"), None, None),
    )
    return jax.shard_map(
        shards,
        mesh=mesh,
        in_specs=placed,
        out_specs=(
            P(("dp", "seq"), None, None),
            P(("dp", "seq"), None, None),
            P(("dp", "seq"), None, None),
            P(("dp", "seq"), None),
            P(("dp", "seq"), None),
            P(("dp", "seq"), None),
            P(("dp", "seq"), None),
            P(("dp", "seq"), None),
            P(("dp", "seq"), None),
            P(("dp", "seq"), None),
            P(("dp", "seq"), None),
            P(("dp", "seq"), None),
        ),
        check_vma=False,
    )
```

```python
import functools
import math

import jax
import jax.numpy as jnp
from jax import lax
from jax.experimental import pallas as pl
from jax.experimental.pallas import tpu as pltpu
from jax.sharding import PartitionSpec as P

HEADS = 12
HEAD_DIM = 64


epsilon = 1e-05


TILE = 384


def split_heads(values):
    return values.reshape(values.shape[:-1] + (HEADS, HEAD_DIM))


def project(values, weight):
    flat_rows = values.reshape(-1, values.shape[-1])
    return jnp.dot(flat_rows, weight, preferred_element_type=jnp.float32).reshape(
        values.shape[:-1] + (weight.shape[1],)
    )


def project_back(values, weight):
    flat_rows = values.reshape(-1, values.shape[-1])
    result = lax.dot_general(
        flat_rows, weight, (((1,), (1,)), ((), ())), preferred_element_type=jnp.float32
    )
    return result.reshape(values.shape[:-1] + (weight.shape[0],))


def weight_grad(left_rows, right_rows):
    return lax.dot_general(
        left_rows.reshape(-1, left_rows.shape[-1]),
        right_rows.reshape(-1, right_rows.shape[-1]),
        (((0,), (0,)), ((), ())),
        preferred_element_type=jnp.float32,
    )


def layer_norm(values, gain, shift):
    centred = values - jnp.mean(values, axis=-1, keepdims=True)
    spread = jnp.mean(centred * centred, axis=-1, keepdims=True)
    inverse = lax.rsqrt(spread + epsilon)
    scaled = centred * inverse
    return (scaled * gain + shift, scaled, inverse)


def norm_back(grad_rows, scaled, inverse, gain):
    weighted = grad_rows * gain
    result = inverse * (
        weighted
        - jnp.mean(weighted, axis=-1, keepdims=True)
        - scaled * jnp.mean(weighted * scaled, axis=-1, keepdims=True)
    )
    flat_grad = grad_rows.reshape(-1, grad_rows.shape[-1])
    flat_scaled = scaled.reshape(-1, scaled.shape[-1])
    return (result, jnp.sum(flat_grad * flat_scaled, axis=0), jnp.sum(flat_grad, axis=0))


def causal_mask(lengths_part, seq_len):
    positions = jnp.arange(seq_len)
    live_rows = positions[None, :] < lengths_part[:, None]
    return (positions[:, None] >= positions[None, :])[None] & live_rows[:, None, :]


def score_block(query_rows, key_rows, score_mask):
    score_scale = 1.0 / math.sqrt(HEAD_DIM)
    scores = (
        jnp.einsum(
            "bqhe,bkhe->bhqk",
            split_heads(query_rows),
            split_heads(key_rows),
            preferred_element_type=jnp.float32,
        )
        * score_scale
    )
    if score_mask is not None:
        scores = jnp.where(score_mask[:, None], scores, -1e30)
    return scores


def attend(query_rows, key_rows, value_rows, score_mask):
    scores = score_block(query_rows, key_rows, score_mask)
    row_peak = jnp.max(scores, axis=-1, keepdims=True)
    expanded = jnp.exp(scores - row_peak)
    row_total = jnp.sum(expanded, axis=-1, keepdims=True)
    row_probs = (expanded / row_total).astype(jnp.bfloat16)
    mixed = jnp.einsum(
        "bhqk,bkhe->bqhe", row_probs, split_heads(value_rows), preferred_element_type=jnp.float32
    )
    return (
        mixed.reshape(query_rows.shape).astype(jnp.bfloat16),
        (row_peak + jnp.log(row_total))[..., 0],
    )


def attend_back(query_rows, key_rows, value_rows, score_mask, logsum, grad_rows):
    score_scale = 1.0 / math.sqrt(HEAD_DIM)
    scores = score_block(query_rows, key_rows, score_mask)
    row_probs = jnp.exp(scores - logsum[..., None])
    grad_heads = split_heads(grad_rows)
    grad_value = jnp.einsum(
        "bhqk,bqhe->bkhe",
        row_probs.astype(jnp.bfloat16),
        grad_heads,
        preferred_element_type=jnp.float32,
    )
    grad_probs = jnp.einsum(
        "bqhe,bkhe->bhqk", grad_heads, split_heads(value_rows), preferred_element_type=jnp.float32
    )
    grad_scores = (
        row_probs * (grad_probs - jnp.sum(grad_probs * row_probs, axis=-1, keepdims=True))
    ).astype(jnp.bfloat16)
    grad_query = (
        jnp.einsum(
            "bhqk,bkhe->bqhe",
            grad_scores,
            split_heads(key_rows),
            preferred_element_type=jnp.float32,
        )
        * score_scale
    )
    grad_key = (
        jnp.einsum(
            "bhqk,bqhe->bkhe",
            grad_scores,
            split_heads(query_rows),
            preferred_element_type=jnp.float32,
        )
        * score_scale
    )
    return (
        grad_query.reshape(query_rows.shape).astype(jnp.bfloat16),
        grad_key.reshape(key_rows.shape).astype(jnp.bfloat16),
        grad_value.reshape(value_rows.shape).astype(jnp.bfloat16),
    )


def self_forward(query_rows, key_rows, value_rows, lengths_part):
    return attend(query_rows, key_rows, value_rows, causal_mask(lengths_part, query_rows.shape[1]))


def cross_forward(query_rows, key_rows, value_rows):
    return attend(query_rows, key_rows, value_rows, None)


def self_backward(query_rows, key_rows, value_rows, lengths_part, logsum, grad_rows):
    return attend_back(
        query_rows,
        key_rows,
        value_rows,
        causal_mask(lengths_part, query_rows.shape[1]),
        logsum,
        grad_rows,
    )


def cross_backward(query_rows, key_rows, value_rows, logsum, grad_rows):
    return attend_back(query_rows, key_rows, value_rows, None, logsum, grad_rows)


def dot(left, right, contract):
    return lax.dot_general(left, right, (contract, ((), ())), preferred_element_type=jnp.float32)


def ffn_body(rows_ref, grad_ref, expand_ref, reduce_ref, order_ref, out_ref, back_ref, rgrad_ref, egrad_ref, *, ratio):
    rows, grad = rows_ref[...], grad_ref[...]
    width = rows.shape[1]
    stacked = jnp.concatenate([reduce_ref[:, k * width : (k + 1) * width] for k in range(ratio)], axis=0)
    reduce = dot(order_ref[...], stacked, ((1,), (0,))).astype(jnp.bfloat16)
    expand = expand_ref[...]
    gate = dot(rows, expand, ((1,), (0,)))
    grad_hidden = dot(grad, reduce, ((1,), (1,)))
    share = 0.5 * (1.0 + lax.erf(gate * math.sqrt(0.5)))
    slope = share + gate * (jnp.exp(-0.5 * gate * gate) * (1.0 / math.sqrt(2.0 * math.pi)))
    hidden = (gate * share).astype(jnp.bfloat16)
    grad_gate = (grad_hidden * slope).astype(jnp.bfloat16)
    rgrad_ref[...] = dot(hidden, grad, ((0,), (0,))).astype(jnp.bfloat16)
    egrad_ref[...] = dot(rows, grad_gate, ((0,), (0,))).astype(jnp.bfloat16)
    first = pl.program_id(0) == 0
    @pl.when(first)
    def _():
        out_ref[...] = jnp.zeros_like(out_ref)
        back_ref[...] = jnp.zeros_like(back_ref)
    out_ref[...] += dot(hidden, reduce, ((1,), (0,)))
    back_ref[...] += dot(grad_gate, expand, ((1,), (1,)))


def ffn(rows, grad, others, per_device, hidden_width):
    count, width = rows.shape
    ratio = hidden_width // width
    part = TILE // ratio
    place = jnp.arange(TILE)
    chunk = per_device * ratio
    source = part * (place % chunk // per_device) + per_device * (place // chunk) + place % per_device
    order = (source[:, None] == place[None, :]).astype(jnp.bfloat16)
    whole = lambda shape: pl.BlockSpec(shape, lambda j: (0, 0))
    return pl.pallas_call(
        functools.partial(ffn_body, ratio=ratio),
        grid=(hidden_width // TILE,),
        in_specs=[
            whole((count, width)), whole((count, width)),
            pl.BlockSpec((width, TILE), lambda j: (0, hidden_width // TILE + j)),
            pl.BlockSpec((part, hidden_width), lambda j: (j, 0)),
            whole((TILE, TILE)),
        ],
        out_specs=[
            whole((count, width)), whole((count, width)),
            pl.BlockSpec((TILE, width), lambda j: (j, 0)),
            pl.BlockSpec((width, TILE), lambda j: (0, j)),
        ],
        out_shape=[
            jax.ShapeDtypeStruct((count, width), jnp.float32),
            jax.ShapeDtypeStruct((count, width), jnp.float32),
            jax.ShapeDtypeStruct((hidden_width, width), jnp.bfloat16),
            jax.ShapeDtypeStruct((width, hidden_width), jnp.bfloat16),
        ],
        compiler_params=pltpu.CompilerParams(dimension_semantics=("arbitrary",), vmem_limit_bytes=48 << 20),
        name="ffn",
    )(rows, grad, others, others, order)


def index_bits():
    found = []
    for axis in ("dp", "seq"):
        count = lax.axis_size(axis)
        found += [(axis, bit) for bit in reversed(range(count.bit_length() - 1))]
    return found


def swap_pairs(axis, bit):
    return [(i, i ^ (1 << bit)) for i in range(lax.axis_size(axis))]


def own_bit(axis, bit):
    return (lax.axis_index(axis) >> bit) & 1


def gather_order(flip):
    far = [("dp", bit) for bit in range(1, lax.axis_size("dp").bit_length() - 1)]
    near = [[("dp", 0)], [("seq", bit) for bit in range(1, lax.axis_size("seq").bit_length() - 1)]]
    if flip:
        near = near[::-1]
    return far + near[0] + near[1] + [("seq", 0)]


def gather_rows(part, flip):
    bits = index_bits()
    own = [own_bit(*place) for place in bits]
    rest = [0] * part.ndim
    known = [1] * len(bits)
    piece = part.reshape((1,) * len(bits) + part.shape)
    whole = jnp.zeros((2,) * len(bits) + part.shape, part.dtype)
    whole = lax.dynamic_update_slice(whole, piece, own + rest)
    for place in gather_order(flip):
        dim = bits.index(place)
        starts = [0 if size == 2 else bit for size, bit in zip(known, own)]
        if max(known) == 2:
            piece = lax.dynamic_slice(whole, starts + rest, known + list(part.shape))
        other = lax.ppermute(piece, place[0], swap_pairs(*place))
        starts[dim] = 1 - own[dim]
        whole = lax.dynamic_update_slice(whole, other, starts + rest)
        known[dim] = 2
    return whole.reshape((-1,) + part.shape[1:])


class Scatter:
    def __init__(self, whole, flip):
        bits = index_bits()
        self.rows = whole.shape[0] >> len(bits)
        self.tail = whole.shape[1:]
        self.state = whole.reshape((2,) * len(bits) + (self.rows,) + self.tail)
        order = gather_order(flip)
        self.left = [order[-1]] + order[:-1][::-1]

    def step(self):
        place = self.left.pop(0)
        dim = index_bits().index(place)
        mine = own_bit(*place)
        given = lax.dynamic_slice_in_dim(self.state, 1 - mine, 1, dim)
        kept = lax.dynamic_slice_in_dim(self.state, mine, 1, dim)
        self.state = kept + lax.ppermute(given, place[0], swap_pairs(*place))

    def finish(self):
        while self.left:
            self.step()
        return self.state.reshape((self.rows,) + self.tail).astype(jnp.float32)


def tie(scatters, *values):
    held = lax.optimization_barrier(tuple(one.state for one in scatters) + values)
    for one, state in zip(scatters, held):
        one.state = state
    return held[len(scatters):] if len(values) > 1 else held[-1]


def route(table_rows, pick, place):
    peers = lax.axis_size("seq")
    position = lax.axis_index("seq")
    arrived = []
    for k in range(peers):
        rows = jnp.take(table_rows, pick[position ^ k], axis=0)
        if k:
            rows = lax.ppermute(rows, "seq", [(i, i ^ k) for i in range(peers)])
        arrived.append(rows)
    return jnp.take(jnp.concatenate(arrived, axis=0), place, axis=0)


def shards(
    caption_tokens,
    image_tokens,
    caption_lengths,
    caption_image,
    norm_gain,
    norm_bias,
    self_packed,
    self_output,
    cross_query,
    cross_pair,
    cross_output,
    expand_weight,
    reduce_weight,
    cotangent,
):
    captions, seq_len, model_width = caption_tokens.shape
    peer_count = lax.axis_size("seq")
    position = lax.axis_index("seq")
    per_peer = captions // peer_count

    owner = (caption_image // captions % peer_count).reshape(peer_count, captions)
    slot = (caption_image % captions).reshape(peer_count, captions)
    by_owner = jnp.argsort(owner, axis=1, stable=True).reshape(peer_count, peer_count, per_peer)
    slot_by_owner = jnp.take_along_axis(
        slot, by_owner.reshape(peer_count, captions), axis=1
    ).reshape(peer_count, peer_count, per_peer)
    asked = slot_by_owner[:, position]
    held = by_owner[position]
    turns = position ^ jnp.arange(peer_count)
    image_place = jnp.argsort(held[turns].reshape(-1))
    home_place = jnp.argsort(asked[turns].reshape(-1))
    paired = route(image_tokens, asked, image_place)

    norm_columns = jnp.pad(jnp.concatenate([norm_gain, norm_bias], axis=1), ((0, 0), (0, 122)))
    first_group = gather_rows(jnp.concatenate([self_packed, norm_columns], axis=1), False)
    rows = self_packed.shape[0]
    ratio = reduce_weight.shape[0] // rows
    reduce_blocks = [reduce_weight[k * rows : (k + 1) * rows] for k in range(ratio)]
    others = lax.all_gather(
        jnp.concatenate(
            reduce_blocks + [expand_weight, cross_pair, self_output, cross_query, cross_output],
            axis=1,
        ),
        ("dp", "seq"),
        axis=0,
        tiled=True,
    )
    packed_weight = first_group[:, : 3 * model_width]
    norm_values = first_group[:, 3 * model_width : 3 * model_width + 6].astype(jnp.float32)
    norm_gains, norm_shifts = norm_values[:, :3], norm_values[:, 3:]
    hidden_width = expand_weight.shape[1]
    narrower = others[:, 2 * hidden_width :]
    pair_weight = narrower[:, : 2 * model_width]
    output_weight = narrower[:, 2 * model_width : 3 * model_width]
    query_weight = narrower[:, 3 * model_width : 4 * model_width]
    cross_weight = narrower[:, 4 * model_width :]

    live_rows = jnp.arange(seq_len)[None, :] < caption_lengths[:, None]
    inputs = caption_tokens.astype(jnp.float32)
    normed_full, scaled_one, inverse_one = layer_norm(inputs, norm_gains[:, 0], norm_shifts[:, 0])
    normed_one = normed_full.astype(jnp.bfloat16)
    packed = project(normed_one, packed_weight).astype(jnp.bfloat16)
    query_part = packed[..., :model_width]
    key_part = packed[..., model_width : 2 * model_width]
    value_part = packed[..., 2 * model_width :]
    attended, logsum_one = self_forward(query_part, key_part, value_part, caption_lengths)
    after_self = inputs + project(attended, output_weight)
    normed_full_two, scaled_two, inverse_two = layer_norm(
        after_self, norm_gains[:, 1], norm_shifts[:, 1]
    )
    normed_two = normed_full_two.astype(jnp.bfloat16)
    image_pair = project(paired, pair_weight).astype(jnp.bfloat16)
    image_key = image_pair[..., :model_width]
    image_value = image_pair[..., model_width:]
    query_rows = project(normed_two, query_weight).astype(jnp.bfloat16)
    mixed_rows, logsum_two = cross_forward(query_rows, image_key, image_value)
    branch = project(mixed_rows, cross_weight).astype(jnp.bfloat16)
    after_cross = after_self + branch.astype(jnp.float32)
    normed_full_three, scaled_three, inverse_three = layer_norm(
        after_cross, norm_gains[:, 2], norm_shifts[:, 2]
    )
    normed_three = normed_full_three.astype(jnp.bfloat16)
    grad_out = jnp.where(live_rows[..., None], cotangent, jnp.zeros_like(cotangent))
    flat = lambda member: member.reshape(-1, model_width)
    forward, backward, reduce_part, expand_part = ffn(
        flat(normed_three), flat(grad_out), others, rows, hidden_width
    )
    caption_out = jnp.where(
        live_rows[..., None], after_cross + forward.reshape(after_cross.shape), 0.0
    ).astype(jnp.bfloat16)

    narrow = lambda member: member.astype(jnp.bfloat16)
    reduce_sums = Scatter(reduce_part, True)
    expand_sums = Scatter(expand_part, False)
    reduce_sums.step()
    expand_sums.step()
    grad_norm_three, gain_three, shift_three = norm_back(
        backward.reshape(after_cross.shape), scaled_three, inverse_three, norm_gains[:, 2]
    )
    grad_second = grad_out.astype(jnp.float32) + grad_norm_three
    grad_branch = grad_second.astype(jnp.bfloat16)
    cross_output_grad = weight_grad(mixed_rows, grad_branch)
    grad_cross_mixed = project_back(grad_branch, cross_weight).astype(jnp.bfloat16)
    grad_cross_mixed = tie([reduce_sums, expand_sums], grad_cross_mixed)
    reduce_sums.step()
    expand_sums.step()
    grad_cross_rows, grad_image_key, grad_image_value = cross_backward(
        query_rows, image_key, image_value, logsum_two, grad_cross_mixed
    )
    grad_pair = jnp.concatenate([grad_image_key, grad_image_value], axis=-1)
    image_grad = route(
        project_back(grad_pair, pair_weight).astype(jnp.bfloat16), held, home_place
    )
    cross_pair_grad = weight_grad(paired, grad_pair)
    cross_sums = Scatter(
        narrow(jnp.concatenate([cross_pair_grad, cross_output_grad], axis=1)), True
    )
    grad_cross_rows = tie([cross_sums], grad_cross_rows)
    cross_sums.step()
    cross_query_grad = weight_grad(normed_two, grad_cross_rows)
    grad_norm_two, gain_two, shift_two = norm_back(
        project_back(grad_cross_rows, query_weight).astype(jnp.bfloat16).astype(jnp.float32),
        scaled_two,
        inverse_two,
        norm_gains[:, 1],
    )
    grad_first = grad_second + grad_norm_two
    grad_self = grad_first.astype(jnp.bfloat16)
    self_output_grad = weight_grad(attended, grad_self)
    query_sums = Scatter(
        narrow(jnp.concatenate([cross_query_grad, self_output_grad], axis=1)), False
    )
    grad_self = tie([reduce_sums, expand_sums, cross_sums, query_sums], grad_self)
    for one in (reduce_sums, expand_sums, query_sums, cross_sums):
        one.step()
    grad_attended = project_back(grad_self, output_weight).astype(jnp.bfloat16)
    grad_query, grad_key, grad_value = self_backward(
        query_part, key_part, value_part, caption_lengths, logsum_one, grad_attended
    )
    grad_packed = jnp.concatenate([grad_query, grad_key, grad_value], axis=-1)
    grad_packed = tie([reduce_sums, expand_sums, query_sums], grad_packed)
    for one in (reduce_sums, expand_sums, query_sums):
        one.step()
    self_packed_grad = weight_grad(normed_one, grad_packed)
    grad_norm_one, gain_one, shift_one = norm_back(
        project_back(grad_packed, packed_weight), scaled_one, inverse_one, norm_gains[:, 0]
    )
    caption_grad = (grad_first + grad_norm_one).astype(jnp.bfloat16)
    norm_sums = jnp.stack([gain_one, gain_two, gain_three, shift_one, shift_two, shift_three], axis=1)
    half = 3 * model_width // 2
    first_sums = Scatter(narrow(self_packed_grad[:, :half]), False)
    second_sums = Scatter(
        narrow(
            jnp.concatenate(
                [self_packed_grad[:, half:], jnp.pad(norm_sums, ((0, 0), (0, 122)))], axis=1
            )
        ),
        True,
    )
    reduce_grad, expand_grad = reduce_sums.finish(), expand_sums.finish()
    first_sums, second_sums = first_sums.finish(), second_sums.finish()
    cross_sums, query_sums = cross_sums.finish(), query_sums.finish()
    return (
        caption_out,
        caption_grad,
        image_grad,
        second_sums[:, half : half + 3],
        second_sums[:, half + 3 : half + 6],
        jnp.concatenate([first_sums, second_sums[:, :half]], axis=1),
        query_sums[:, model_width:],
        query_sums[:, :model_width],
        cross_sums[:, : 2 * model_width],
        cross_sums[:, 2 * model_width :],
        expand_grad,
        reduce_grad,
    )


def solution(mesh):
    placed = (
        P(("dp", "seq"), None, None),
        P(("dp", "seq"), None, None),
        P(("dp", "seq")),
        P("dp"),
        P(("dp", "seq"), None),
        P(("dp", "seq"), None),
        P(("dp", "seq"), None),
        P(("dp", "seq"), None),
        P(("dp", "seq"), None),
        P(("dp", "seq"), None),
        P(("dp", "seq"), None),
        P(("dp", "seq"), None),
        P(("dp", "seq"), None),
        P(("dp", "seq"), None, None),
    )
    return jax.shard_map(
        shards,
        mesh=mesh,
        in_specs=placed,
        out_specs=(
            P(("dp", "seq"), None, None),
            P(("dp", "seq"), None, None),
            P(("dp", "seq"), None, None),
            P(("dp", "seq"), None),
            P(("dp", "seq"), None),
            P(("dp", "seq"), None),
            P(("dp", "seq"), None),
            P(("dp", "seq"), None),
            P(("dp", "seq"), None),
            P(("dp", "seq"), None),
            P(("dp", "seq"), None),
            P(("dp", "seq"), None),
        ),
        check_vma=False,
    )
```

```python
import functools
import math

import jax
import jax.numpy as jnp
from jax import lax
from jax.experimental import pallas as pl
from jax.experimental.pallas import tpu as pltpu
from jax.sharding import PartitionSpec as P

HEADS = 12
HEAD_DIM = 64


epsilon = 1e-05


TILE = 384
LANES = 128


def project(values, weight):
    flat_rows = values.reshape(-1, values.shape[-1])
    return jnp.dot(flat_rows, weight, preferred_element_type=jnp.float32).reshape(
        values.shape[:-1] + (weight.shape[1],)
    )


def project_back(values, weight):
    flat_rows = values.reshape(-1, values.shape[-1])
    result = lax.dot_general(
        flat_rows, weight, (((1,), (1,)), ((), ())), preferred_element_type=jnp.float32
    )
    return result.reshape(values.shape[:-1] + (weight.shape[0],))


def weight_grad(left_rows, right_rows):
    return lax.dot_general(
        left_rows.reshape(-1, left_rows.shape[-1]),
        right_rows.reshape(-1, right_rows.shape[-1]),
        (((0,), (0,)), ((), ())),
        preferred_element_type=jnp.float32,
    )


def layer_norm(values, gain, shift):
    centred = values - jnp.mean(values, axis=-1, keepdims=True)
    spread = jnp.mean(centred * centred, axis=-1, keepdims=True)
    inverse = lax.rsqrt(spread + epsilon)
    scaled = centred * inverse
    return (scaled * gain + shift, scaled, inverse)


def norm_back(grad_rows, scaled, inverse, gain):
    weighted = grad_rows * gain
    result = inverse * (
        weighted
        - jnp.mean(weighted, axis=-1, keepdims=True)
        - scaled * jnp.mean(weighted * scaled, axis=-1, keepdims=True)
    )
    flat_grad = grad_rows.reshape(-1, grad_rows.shape[-1])
    flat_scaled = scaled.reshape(-1, scaled.shape[-1])
    return (result, jnp.sum(flat_grad * flat_scaled, axis=0), jnp.sum(flat_grad, axis=0))


def dot(left, right, contract):
    return lax.dot_general(left, right, (contract, ((), ())), preferred_element_type=jnp.float32)


def ffn_body(rows_ref, grad_ref, expand_ref, reduce_ref, order_ref, out_ref, back_ref, rgrad_ref, egrad_ref, *, ratio):
    rows, grad = rows_ref[...], grad_ref[...]
    width = rows.shape[1]
    stacked = jnp.concatenate([reduce_ref[:, k * width : (k + 1) * width] for k in range(ratio)], axis=0)
    reduce = dot(order_ref[...], stacked, ((1,), (0,))).astype(jnp.bfloat16)
    expand = expand_ref[...]
    gate = dot(rows, expand, ((1,), (0,)))
    grad_hidden = dot(grad, reduce, ((1,), (1,)))
    share = 0.5 * (1.0 + lax.erf(gate * math.sqrt(0.5)))
    slope = share + gate * (jnp.exp(-0.5 * gate * gate) * (1.0 / math.sqrt(2.0 * math.pi)))
    hidden = (gate * share).astype(jnp.bfloat16)
    grad_gate = (grad_hidden * slope).astype(jnp.bfloat16)
    rgrad_ref[...] = dot(hidden, grad, ((0,), (0,))).astype(jnp.bfloat16)
    egrad_ref[...] = dot(rows, grad_gate, ((0,), (0,))).astype(jnp.bfloat16)
    first = pl.program_id(0) == 0
    @pl.when(first)
    def _():
        out_ref[...] = jnp.zeros_like(out_ref)
        back_ref[...] = jnp.zeros_like(back_ref)
    out_ref[...] += dot(hidden, reduce, ((1,), (0,)))
    back_ref[...] += dot(grad_gate, expand, ((1,), (1,)))


def ffn(rows, grad, others, per_device, hidden_width):
    count, width = rows.shape
    ratio = hidden_width // width
    part = TILE // ratio
    place = jnp.arange(TILE)
    chunk = per_device * ratio
    source = part * (place % chunk // per_device) + per_device * (place // chunk) + place % per_device
    order = (source[:, None] == place[None, :]).astype(jnp.bfloat16)
    whole = lambda shape: pl.BlockSpec(shape, lambda j: (0, 0))
    return pl.pallas_call(
        functools.partial(ffn_body, ratio=ratio),
        grid=(hidden_width // TILE,),
        in_specs=[
            whole((count, width)), whole((count, width)),
            pl.BlockSpec((width, TILE), lambda j: (0, hidden_width // TILE + j)),
            pl.BlockSpec((part, hidden_width), lambda j: (j, 0)),
            whole((TILE, TILE)),
        ],
        out_specs=[
            whole((count, width)), whole((count, width)),
            pl.BlockSpec((TILE, width), lambda j: (j, 0)),
            pl.BlockSpec((width, TILE), lambda j: (0, j)),
        ],
        out_shape=[
            jax.ShapeDtypeStruct((count, width), jnp.float32),
            jax.ShapeDtypeStruct((count, width), jnp.float32),
            jax.ShapeDtypeStruct((hidden_width, width), jnp.bfloat16),
            jax.ShapeDtypeStruct((width, hidden_width), jnp.bfloat16),
        ],
        compiler_params=pltpu.CompilerParams(dimension_semantics=("arbitrary",), vmem_limit_bytes=48 << 20),
        name="ffn",
    )(rows, grad, others, others, order)


def stack_heads(block):
    left = lax.broadcasted_iota(jnp.int32, block.shape, 1) < HEAD_DIM
    none = jnp.zeros_like(block)
    return jnp.concatenate([jnp.where(left, block, none), jnp.where(left, none, block)], axis=0)


def join_heads(stacked):
    count = stacked.shape[0] // 2
    left = lax.broadcasted_iota(jnp.int32, (count, LANES), 1) < HEAD_DIM
    return jnp.where(left, stacked[:count], stacked[count:])


def pair_probs(query, key, length):
    scores = dot(key, query, ((1,), (1,)))
    if length is not None:
        row = lax.broadcasted_iota(jnp.int32, scores.shape, 0)
        column = lax.broadcasted_iota(jnp.int32, scores.shape, 1) % (scores.shape[1] // 2)
        scores = jnp.where((row <= column) & (row < length), scores, -1e30)
    spread = jnp.exp(scores - jnp.max(scores, axis=0, keepdims=True))
    return spread * (1.0 / jnp.sum(spread, axis=0, keepdims=True))


def scaled(block):
    return block * jnp.asarray(1.0 / math.sqrt(HEAD_DIM), block.dtype)


def attend_body(lengths_ref, query_ref, key_ref, value_ref, out_ref, *, causal):
    length = lengths_ref[pl.program_id(0)] if causal else None
    for start in range(0, HEADS * HEAD_DIM, LANES):
        lanes = slice(start, start + LANES)
        query = stack_heads(scaled(query_ref[0, :, lanes]))
        probs = pair_probs(query, key_ref[0, :, lanes], length).astype(jnp.bfloat16)
        out_ref[0, :, lanes] = join_heads(dot(probs, value_ref[0, :, lanes], ((0,), (0,)))).astype(jnp.bfloat16)


def attend_back_body(lengths_ref, query_ref, key_ref, value_ref, grad_ref, query_grad_ref, pair_grad_ref, *, causal):
    length = lengths_ref[pl.program_id(0)] if causal else None
    width = HEADS * HEAD_DIM
    for start in range(0, width, LANES):
        lanes = slice(start, start + LANES)
        query = stack_heads(scaled(query_ref[0, :, lanes]))
        grad = stack_heads(grad_ref[0, :, lanes])
        key, value = key_ref[0, :, lanes], value_ref[0, :, lanes]
        probs = pair_probs(query, key, length)
        grad_probs = dot(value, grad, ((1,), (1,)))
        grad_scores = probs * (grad_probs - jnp.sum(grad_probs * probs, axis=0, keepdims=True))
        grad_scores = grad_scores.astype(jnp.bfloat16)
        back = lambda left, right: dot(left, right, ((1,), (0,))).astype(jnp.bfloat16)
        grad_query = scaled(join_heads(dot(grad_scores, key, ((0,), (0,))))).astype(jnp.bfloat16)
        grad_key, grad_value = back(grad_scores, query), back(probs.astype(jnp.bfloat16), grad)
        query_grad_ref[0, :, lanes] = grad_query
        if causal:
            query_grad_ref[0, :, slice(width + start, width + start + LANES)] = grad_key
            query_grad_ref[0, :, slice(2 * width + start, 2 * width + start + LANES)] = grad_value
        else:
            pair_grad_ref[0, :, lanes] = grad_key
            pair_grad_ref[0, :, slice(width + start, width + start + LANES)] = grad_value


def attention(body, lengths, arrays, outs, name, heavy):
    width = HEADS * HEAD_DIM
    captions = arrays[0][0].shape[0]
    spec = lambda rows, cols, at: pl.BlockSpec((1, rows, cols), lambda c, _: (c, 0, at))
    work = heavy * 2 * captions * arrays[0][0].shape[1] * arrays[1][0].shape[1] * width
    return pl.pallas_call(
        body,
        grid_spec=pltpu.PrefetchScalarGridSpec(
            num_scalar_prefetch=1,
            grid=(captions,),
            in_specs=[spec(array.shape[1], width, at) for array, at in arrays],
            out_specs=[spec(rows, cols, 0) for rows, cols in outs],
        ),
        out_shape=[jax.ShapeDtypeStruct((captions, rows, cols), jnp.bfloat16) for rows, cols in outs],
        compiler_params=pltpu.CompilerParams(dimension_semantics=("arbitrary",), vmem_limit_bytes=48 << 20),
        cost_estimate=pl.CostEstimate(flops=work, transcendentals=0, bytes_accessed=0),
        name=name,
    )(lengths, *(array for array, _ in arrays))


def self_forward(packed, lengths):
    rows, width = packed.shape[1], HEADS * HEAD_DIM
    return attention(functools.partial(attend_body, causal=True), lengths,
        [(packed, 0), (packed, 1), (packed, 2)], [(rows, width)], "self_attention", 2)[0]


def cross_forward(query_rows, pair, lengths):
    return attention(functools.partial(attend_body, causal=False), lengths,
        [(query_rows, 0), (pair, 0), (pair, 1)], [query_rows.shape[1:]], "cross_attention", 2)[0]


def self_body(*refs):
    attend_back_body(*refs, None, causal=True)


def self_backward(packed, grad_rows, lengths):
    return attention(self_body, lengths,
        [(packed, 0), (packed, 1), (packed, 2), (grad_rows, 0)], [packed.shape[1:]], "self_backward", 5)[0]


def cross_backward(query_rows, pair, grad_rows, lengths):
    return attention(functools.partial(attend_back_body, causal=False), lengths,
        [(query_rows, 0), (pair, 0), (pair, 1), (grad_rows, 0)],
        [query_rows.shape[1:], pair.shape[1:]], "cross_backward", 5)


def index_bits():
    found = []
    for axis in ("dp", "seq"):
        count = lax.axis_size(axis)
        found += [(axis, bit) for bit in reversed(range(count.bit_length() - 1))]
    return found


def swap_pairs(axis, bit):
    return [(i, i ^ (1 << bit)) for i in range(lax.axis_size(axis))]


def own_bit(axis, bit):
    return (lax.axis_index(axis) >> bit) & 1


def gather_order(flip):
    far = [("dp", bit) for bit in range(1, lax.axis_size("dp").bit_length() - 1)]
    near = [[("dp", 0)], [("seq", bit) for bit in range(1, lax.axis_size("seq").bit_length() - 1)]]
    if flip:
        near = near[::-1]
    return far + near[0] + near[1] + [("seq", 0)]


def gather_rows(part, flip):
    bits = index_bits()
    own = [own_bit(*place) for place in bits]
    rest = [0] * part.ndim
    known = [1] * len(bits)
    piece = part.reshape((1,) * len(bits) + part.shape)
    whole = jnp.zeros((2,) * len(bits) + part.shape, part.dtype)
    whole = lax.dynamic_update_slice(whole, piece, own + rest)
    for place in gather_order(flip):
        dim = bits.index(place)
        starts = [0 if size == 2 else bit for size, bit in zip(known, own)]
        if max(known) == 2:
            piece = lax.dynamic_slice(whole, starts + rest, known + list(part.shape))
        other = lax.ppermute(piece, place[0], swap_pairs(*place))
        starts[dim] = 1 - own[dim]
        whole = lax.dynamic_update_slice(whole, other, starts + rest)
        known[dim] = 2
    return whole.reshape((-1,) + part.shape[1:])


class Scatter:
    def __init__(self, whole, flip):
        bits = index_bits()
        self.rows = whole.shape[0] >> len(bits)
        self.tail = whole.shape[1:]
        self.state = whole.reshape((2,) * len(bits) + (self.rows,) + self.tail)
        order = gather_order(flip)
        self.left = [order[-1]] + order[:-1][::-1]

    def step(self):
        place = self.left.pop(0)
        dim = index_bits().index(place)
        mine = own_bit(*place)
        given = lax.dynamic_slice_in_dim(self.state, 1 - mine, 1, dim)
        kept = lax.dynamic_slice_in_dim(self.state, mine, 1, dim)
        self.state = kept + lax.ppermute(given, place[0], swap_pairs(*place))

    def finish(self):
        while self.left:
            self.step()
        return self.state.reshape((self.rows,) + self.tail).astype(jnp.float32)


def advance(scatters, *values):
    held = lax.optimization_barrier(tuple(one.state for one in scatters) + values)
    for one, state in zip(scatters, held):
        one.state = state
        if one.left:
            one.step()
    return held[len(scatters) :] if len(values) > 1 else held[-1]


def route(table_rows, pick, place):
    peers = lax.axis_size("seq")
    position = lax.axis_index("seq")
    arrived = []
    for k in range(peers):
        rows = jnp.take(table_rows, pick[position ^ k], axis=0)
        if k:
            rows = lax.ppermute(rows, "seq", [(i, i ^ k) for i in range(peers)])
        arrived.append(rows)
    return jnp.take(jnp.concatenate(arrived, axis=0), place, axis=0)


def shards(
    caption_tokens,
    image_tokens,
    caption_lengths,
    caption_image,
    norm_gain,
    norm_bias,
    self_packed,
    self_output,
    cross_query,
    cross_pair,
    cross_output,
    expand_weight,
    reduce_weight,
    cotangent,
):
    captions, seq_len, model_width = caption_tokens.shape
    peer_count = lax.axis_size("seq")
    position = lax.axis_index("seq")
    per_peer = captions // peer_count

    owner = (caption_image // captions % peer_count).reshape(peer_count, captions)
    slot = (caption_image % captions).reshape(peer_count, captions)
    by_owner = jnp.argsort(owner, axis=1, stable=True).reshape(peer_count, peer_count, per_peer)
    slot_by_owner = jnp.take_along_axis(
        slot, by_owner.reshape(peer_count, captions), axis=1
    ).reshape(peer_count, peer_count, per_peer)
    asked = slot_by_owner[:, position]
    held = by_owner[position]
    turns = position ^ jnp.arange(peer_count)
    image_place = jnp.argsort(held[turns].reshape(-1))
    home_place = jnp.argsort(asked[turns].reshape(-1))
    paired = route(image_tokens, asked, image_place)

    norm_columns = jnp.pad(jnp.concatenate([norm_gain, norm_bias], axis=1), ((0, 0), (0, 122)))
    first_group = gather_rows(jnp.concatenate([self_packed, norm_columns], axis=1), False)
    rows = self_packed.shape[0]
    ratio = reduce_weight.shape[0] // rows
    reduce_blocks = [reduce_weight[k * rows : (k + 1) * rows] for k in range(ratio)]
    others = lax.all_gather(
        jnp.concatenate(
            reduce_blocks + [expand_weight, cross_pair, self_output, cross_query, cross_output],
            axis=1,
        ),
        ("dp", "seq"),
        axis=0,
        tiled=True,
    )
    packed_weight = first_group[:, : 3 * model_width]
    norm_values = first_group[:, 3 * model_width : 3 * model_width + 6].astype(jnp.float32)
    norm_gains, norm_shifts = norm_values[:, :3], norm_values[:, 3:]
    hidden_width = expand_weight.shape[1]
    narrower = others[:, 2 * hidden_width :]
    pair_weight = narrower[:, : 2 * model_width]
    output_weight = narrower[:, 2 * model_width : 3 * model_width]
    query_weight = narrower[:, 3 * model_width : 4 * model_width]
    cross_weight = narrower[:, 4 * model_width :]

    live_rows = jnp.arange(seq_len)[None, :] < caption_lengths[:, None]
    inputs = caption_tokens.astype(jnp.float32)
    normed_full, scaled_one, inverse_one = layer_norm(inputs, norm_gains[:, 0], norm_shifts[:, 0])
    normed_one = normed_full.astype(jnp.bfloat16)
    packed = project(normed_one, packed_weight).astype(jnp.bfloat16)
    attended = self_forward(packed, caption_lengths)
    after_self = inputs + project(attended, output_weight)
    normed_full_two, scaled_two, inverse_two = layer_norm(
        after_self, norm_gains[:, 1], norm_shifts[:, 1]
    )
    normed_two = normed_full_two.astype(jnp.bfloat16)
    image_pair = project(paired, pair_weight).astype(jnp.bfloat16)
    query_rows = project(normed_two, query_weight).astype(jnp.bfloat16)
    mixed_rows = cross_forward(query_rows, image_pair, caption_lengths)
    branch = project(mixed_rows, cross_weight).astype(jnp.bfloat16)
    after_cross = after_self + branch.astype(jnp.float32)
    normed_full_three, scaled_three, inverse_three = layer_norm(
        after_cross, norm_gains[:, 2], norm_shifts[:, 2]
    )
    normed_three = normed_full_three.astype(jnp.bfloat16)
    grad_out = jnp.where(live_rows[..., None], cotangent, jnp.zeros_like(cotangent))
    flat = lambda member: member.reshape(-1, model_width)
    forward, backward, reduce_part, expand_part = ffn(
        flat(normed_three), flat(grad_out), others, rows, hidden_width
    )
    caption_out = jnp.where(
        live_rows[..., None], after_cross + forward.reshape(after_cross.shape), 0.0
    ).astype(jnp.bfloat16)

    narrow = lambda member: member.astype(jnp.bfloat16)
    reduce_sums = Scatter(reduce_part, True)
    expand_sums = Scatter(expand_part, False)
    reduce_sums.step()
    expand_sums.step()
    grad_norm_three, gain_three, shift_three = norm_back(
        backward.reshape(after_cross.shape), scaled_three, inverse_three, norm_gains[:, 2]
    )
    grad_second = grad_out.astype(jnp.float32) + grad_norm_three
    grad_branch = grad_second.astype(jnp.bfloat16)
    grad_cross_mixed = project_back(grad_branch, cross_weight).astype(jnp.bfloat16)
    grad_cross_mixed, grad_branch = advance(
        [reduce_sums, expand_sums], grad_cross_mixed, grad_branch
    )
    cross_output_grad = weight_grad(mixed_rows, grad_branch)
    grad_cross_rows, grad_pair = cross_backward(
        query_rows, image_pair, grad_cross_mixed, caption_lengths
    )
    cross_pair_grad = weight_grad(paired, grad_pair)
    cross_sums = Scatter(
        narrow(jnp.concatenate([cross_pair_grad, cross_output_grad], axis=1)), True
    )
    grad_pair, grad_cross_rows = advance(
        [reduce_sums, expand_sums, cross_sums], grad_pair, grad_cross_rows
    )
    image_rows = project_back(grad_pair, pair_weight).astype(jnp.bfloat16)
    cross_query_grad = weight_grad(normed_two, grad_cross_rows)
    grad_norm_two, gain_two, shift_two = norm_back(
        project_back(grad_cross_rows, query_weight).astype(jnp.bfloat16).astype(jnp.float32),
        scaled_two,
        inverse_two,
        norm_gains[:, 1],
    )
    grad_first = grad_second + grad_norm_two
    grad_self = grad_first.astype(jnp.bfloat16)
    self_output_grad = weight_grad(attended, grad_self)
    query_sums = Scatter(
        narrow(jnp.concatenate([cross_query_grad, self_output_grad], axis=1)), True
    )
    grad_self, image_rows = advance(
        [reduce_sums, expand_sums, cross_sums, query_sums], grad_self, image_rows
    )
    image_grad = route(image_rows, held, home_place)
    grad_attended = project_back(grad_self, output_weight).astype(jnp.bfloat16)
    grad_packed = self_backward(packed, grad_attended, caption_lengths)
    grad_packed = advance([reduce_sums, expand_sums, cross_sums, query_sums], grad_packed)
    self_packed_grad = weight_grad(normed_one, grad_packed)
    grad_norm_one, gain_one, shift_one = norm_back(
        project_back(grad_packed, packed_weight), scaled_one, inverse_one, norm_gains[:, 0]
    )
    caption_grad = (grad_first + grad_norm_one).astype(jnp.bfloat16)
    norm_sums = jnp.stack([gain_one, gain_two, gain_three, shift_one, shift_two, shift_three], axis=1)
    half = 3 * model_width // 2
    first_sums = Scatter(narrow(self_packed_grad[:, :half]), False)
    second_sums = Scatter(
        narrow(
            jnp.concatenate(
                [self_packed_grad[:, half:], jnp.pad(norm_sums, ((0, 0), (0, 122)))], axis=1
            )
        ),
        True,
    )
    last = [first_sums, second_sums]
    for one in last:
        one.step()
    groups = [query_sums, cross_sums, reduce_sums, expand_sums] + last
    while any(one.left for one in groups):
        advance(groups)
    reduce_grad, expand_grad = reduce_sums.finish(), expand_sums.finish()
    first_sums, second_sums = first_sums.finish(), second_sums.finish()
    cross_sums, query_sums = cross_sums.finish(), query_sums.finish()
    return (
        caption_out,
        caption_grad,
        image_grad,
        second_sums[:, half : half + 3],
        second_sums[:, half + 3 : half + 6],
        jnp.concatenate([first_sums, second_sums[:, :half]], axis=1),
        query_sums[:, model_width:],
        query_sums[:, :model_width],
        cross_sums[:, : 2 * model_width],
        cross_sums[:, 2 * model_width :],
        expand_grad,
        reduce_grad,
    )


def solution(mesh):
    placed = (
        P(("dp", "seq"), None, None),
        P(("dp", "seq"), None, None),
        P(("dp", "seq")),
        P("dp"),
        P(("dp", "seq"), None),
        P(("dp", "seq"), None),
        P(("dp", "seq"), None),
        P(("dp", "seq"), None),
        P(("dp", "seq"), None),
        P(("dp", "seq"), None),
        P(("dp", "seq"), None),
        P(("dp", "seq"), None),
        P(("dp", "seq"), None),
        P(("dp", "seq"), None, None),
    )
    return jax.shard_map(
        shards,
        mesh=mesh,
        in_specs=placed,
        out_specs=(
            P(("dp", "seq"), None, None),
            P(("dp", "seq"), None, None),
            P(("dp", "seq"), None, None),
            P(("dp", "seq"), None),
            P(("dp", "seq"), None),
            P(("dp", "seq"), None),
            P(("dp", "seq"), None),
            P(("dp", "seq"), None),
            P(("dp", "seq"), None),
            P(("dp", "seq"), None),
            P(("dp", "seq"), None),
            P(("dp", "seq"), None),
        ),
        check_vma=False,
    )
```

```python
import functools
import math

import jax
import jax.numpy as jnp
from jax import lax
from jax.experimental import pallas as pl
from jax.experimental.pallas import tpu as pltpu
from jax.sharding import PartitionSpec as P

HEADS = 12
HEAD_DIM = 64


epsilon = 1e-05


TILE = 384
LANES = 128


def project(values, weight):
    flat_rows = values.reshape(-1, values.shape[-1])
    return jnp.dot(flat_rows, weight, preferred_element_type=jnp.float32).reshape(
        values.shape[:-1] + (weight.shape[1],)
    )


def project_back(values, weight):
    flat_rows = values.reshape(-1, values.shape[-1])
    result = lax.dot_general(
        flat_rows, weight, (((1,), (1,)), ((), ())), preferred_element_type=jnp.float32
    )
    return result.reshape(values.shape[:-1] + (weight.shape[0],))


def weight_grad(left_rows, right_rows):
    return lax.dot_general(
        left_rows.reshape(-1, left_rows.shape[-1]),
        right_rows.reshape(-1, right_rows.shape[-1]),
        (((0,), (0,)), ((), ())),
        preferred_element_type=jnp.float32,
    )


def layer_norm(values, gain, shift):
    centred = values - jnp.mean(values, axis=-1, keepdims=True)
    spread = jnp.mean(centred * centred, axis=-1, keepdims=True)
    inverse = lax.rsqrt(spread + epsilon)
    scaled = centred * inverse
    return (scaled * gain + shift, scaled, inverse)


def norm_back(grad_rows, scaled, inverse, gain):
    weighted = grad_rows * gain
    result = inverse * (
        weighted
        - jnp.mean(weighted, axis=-1, keepdims=True)
        - scaled * jnp.mean(weighted * scaled, axis=-1, keepdims=True)
    )
    flat_grad = grad_rows.reshape(-1, grad_rows.shape[-1])
    flat_scaled = scaled.reshape(-1, scaled.shape[-1])
    return (result, jnp.sum(flat_grad * flat_scaled, axis=0), jnp.sum(flat_grad, axis=0))


def dot(left, right, contract):
    return lax.dot_general(left, right, (contract, ((), ())), preferred_element_type=jnp.float32)


def ffn_body(rows_ref, grad_ref, expand_ref, reduce_ref, order_ref, out_ref, back_ref, rgrad_ref, egrad_ref, *, ratio):
    rows, grad = rows_ref[...], grad_ref[...]
    width = rows.shape[1]
    stacked = jnp.concatenate([reduce_ref[:, k * width : (k + 1) * width] for k in range(ratio)], axis=0)
    reduce = dot(order_ref[...], stacked, ((1,), (0,))).astype(jnp.bfloat16)
    expand = expand_ref[...]
    gate = dot(rows, expand, ((1,), (0,)))
    grad_hidden = dot(grad, reduce, ((1,), (1,)))
    share = 0.5 * (1.0 + lax.erf(gate * math.sqrt(0.5)))
    slope = share + gate * (jnp.exp(-0.5 * gate * gate) * (1.0 / math.sqrt(2.0 * math.pi)))
    hidden = (gate * share).astype(jnp.bfloat16)
    grad_gate = (grad_hidden * slope).astype(jnp.bfloat16)
    rgrad_ref[...] = dot(hidden, grad, ((0,), (0,))).astype(jnp.bfloat16)
    egrad_ref[...] = dot(rows, grad_gate, ((0,), (0,))).astype(jnp.bfloat16)
    first = pl.program_id(0) == 0
    @pl.when(first)
    def _():
        out_ref[...] = jnp.zeros_like(out_ref)
        back_ref[...] = jnp.zeros_like(back_ref)
    out_ref[...] += dot(hidden, reduce, ((1,), (0,)))
    back_ref[...] += dot(grad_gate, expand, ((1,), (1,)))


def ffn(rows, grad, others, per_device, hidden_width):
    count, width = rows.shape
    ratio = hidden_width // width
    part = TILE // ratio
    place = jnp.arange(TILE)
    chunk = per_device * ratio
    source = part * (place % chunk // per_device) + per_device * (place // chunk) + place % per_device
    order = (source[:, None] == place[None, :]).astype(jnp.bfloat16)
    whole = lambda shape: pl.BlockSpec(shape, lambda j: (0, 0))
    return pl.pallas_call(
        functools.partial(ffn_body, ratio=ratio),
        grid=(hidden_width // TILE,),
        in_specs=[
            whole((count, width)), whole((count, width)),
            pl.BlockSpec((width, TILE), lambda j: (0, hidden_width // TILE + j)),
            pl.BlockSpec((part, hidden_width), lambda j: (j, 0)),
            whole((TILE, TILE)),
        ],
        out_specs=[
            whole((count, width)), whole((count, width)),
            pl.BlockSpec((TILE, width), lambda j: (j, 0)),
            pl.BlockSpec((width, TILE), lambda j: (0, j)),
        ],
        out_shape=[
            jax.ShapeDtypeStruct((count, width), jnp.float32),
            jax.ShapeDtypeStruct((count, width), jnp.float32),
            jax.ShapeDtypeStruct((hidden_width, width), jnp.bfloat16),
            jax.ShapeDtypeStruct((width, hidden_width), jnp.bfloat16),
        ],
        compiler_params=pltpu.CompilerParams(dimension_semantics=("arbitrary",), vmem_limit_bytes=48 << 20),
        name="ffn",
    )(rows, grad, others, others, order)


def stack_heads(block):
    left = lax.broadcasted_iota(jnp.int32, block.shape, 1) < HEAD_DIM
    none = jnp.zeros_like(block)
    return jnp.concatenate([jnp.where(left, block, none), jnp.where(left, none, block)], axis=0)


def join_heads(stacked):
    count = stacked.shape[0] // 2
    left = lax.broadcasted_iota(jnp.int32, (count, LANES), 1) < HEAD_DIM
    return jnp.where(left, stacked[:count], stacked[count:])


def pair_probs(query, key, length):
    scores = dot(key, query, ((1,), (1,)))
    if length is not None:
        row = lax.broadcasted_iota(jnp.int32, scores.shape, 0)
        column = lax.broadcasted_iota(jnp.int32, scores.shape, 1) % (scores.shape[1] // 2)
        scores = jnp.where((row <= column) & (row < length), scores, -1e30)
    spread = jnp.exp(scores - jnp.max(scores, axis=0, keepdims=True))
    return spread * (1.0 / jnp.sum(spread, axis=0, keepdims=True))


def scaled(block):
    return block * jnp.asarray(1.0 / math.sqrt(HEAD_DIM), block.dtype)


def attend_body(table_ref, query_ref, key_ref, value_ref, out_ref, *, causal):
    length = table_ref[pl.program_id(0)] if causal else None
    for start in range(0, HEADS * HEAD_DIM, LANES):
        lanes = slice(start, start + LANES)
        query = stack_heads(scaled(query_ref[0, :, lanes]))
        probs = pair_probs(query, key_ref[0, :, lanes], length).astype(jnp.bfloat16)
        out_ref[0, :, lanes] = join_heads(dot(probs, value_ref[0, :, lanes], ((0,), (0,)))).astype(jnp.bfloat16)


def attend_back_body(table_ref, query_ref, key_ref, value_ref, grad_ref, query_grad_ref, pair_grad_ref, *, causal):
    length = table_ref[pl.program_id(0)] if causal else None
    width = HEADS * HEAD_DIM
    for start in range(0, width, LANES):
        lanes = slice(start, start + LANES)
        query = stack_heads(scaled(query_ref[0, :, lanes]))
        grad = stack_heads(grad_ref[0, :, lanes])
        key, value = key_ref[0, :, lanes], value_ref[0, :, lanes]
        probs = pair_probs(query, key, length)
        grad_probs = dot(value, grad, ((1,), (1,)))
        grad_scores = probs * (grad_probs - jnp.sum(grad_probs * probs, axis=0, keepdims=True))
        grad_scores = grad_scores.astype(jnp.bfloat16)
        back = lambda left, right: dot(left, right, ((1,), (0,))).astype(jnp.bfloat16)
        grad_query = scaled(join_heads(dot(grad_scores, key, ((0,), (0,))))).astype(jnp.bfloat16)
        grad_key, grad_value = back(grad_scores, query), back(probs.astype(jnp.bfloat16), grad)
        query_grad_ref[0, :, lanes] = grad_query
        if causal:
            query_grad_ref[0, :, slice(width + start, width + start + LANES)] = grad_key
            query_grad_ref[0, :, slice(2 * width + start, 2 * width + start + LANES)] = grad_value
        else:
            pair_grad_ref[0, :, lanes] = grad_key
            pair_grad_ref[0, :, slice(width + start, width + start + LANES)] = grad_value


def attention(body, table, arrays, outs, name, heavy, routed=False):
    width = HEADS * HEAD_DIM
    captions = arrays[0][0].shape[0]
    own = arrays[0][0].shape[1]

    def spec(rows, cols, at):
        if routed and rows != own:
            return pl.BlockSpec((1, rows, cols), lambda c, place: (place[c], 0, at))
        return pl.BlockSpec((1, rows, cols), lambda c, place: (c, 0, at))

    work = heavy * 2 * captions * arrays[0][0].shape[1] * arrays[1][0].shape[1] * width
    return pl.pallas_call(
        body,
        grid_spec=pltpu.PrefetchScalarGridSpec(
            num_scalar_prefetch=1,
            grid=(captions,),
            in_specs=[spec(array.shape[1], width, at) for array, at in arrays],
            out_specs=[spec(rows, cols, 0) for rows, cols in outs],
        ),
        out_shape=[jax.ShapeDtypeStruct((captions, rows, cols), jnp.bfloat16) for rows, cols in outs],
        compiler_params=pltpu.CompilerParams(dimension_semantics=("arbitrary",), vmem_limit_bytes=48 << 20),
        cost_estimate=pl.CostEstimate(flops=work, transcendentals=0, bytes_accessed=0),
        name=name,
    )(table, *(array for array, _ in arrays))


def self_forward(packed, lengths):
    rows, width = packed.shape[1], HEADS * HEAD_DIM
    return attention(functools.partial(attend_body, causal=True), lengths,
        [(packed, 0), (packed, 1), (packed, 2)], [(rows, width)], "self_attention", 2)[0]


def cross_forward(query_rows, pair, place):
    return attention(functools.partial(attend_body, causal=False), place,
        [(query_rows, 0), (pair, 0), (pair, 1)], [query_rows.shape[1:]], "cross_attention", 2, True)[0]


def self_body(*refs):
    attend_back_body(*refs, None, causal=True)


def self_backward(packed, grad_rows, lengths):
    return attention(self_body, lengths,
        [(packed, 0), (packed, 1), (packed, 2), (grad_rows, 0)], [packed.shape[1:]], "self_backward", 5)[0]


def cross_backward(query_rows, pair, grad_rows, place):
    return attention(functools.partial(attend_back_body, causal=False), place,
        [(query_rows, 0), (pair, 0), (pair, 1), (grad_rows, 0)],
        [query_rows.shape[1:], pair.shape[1:]], "cross_backward", 5, True)


def index_bits():
    found = []
    for axis in ("dp", "seq"):
        count = lax.axis_size(axis)
        found += [(axis, bit) for bit in reversed(range(count.bit_length() - 1))]
    return found


def swap_pairs(axis, bit):
    return [(i, i ^ (1 << bit)) for i in range(lax.axis_size(axis))]


def own_bit(axis, bit):
    return (lax.axis_index(axis) >> bit) & 1


def gather_order(flip):
    far = [("dp", bit) for bit in range(1, lax.axis_size("dp").bit_length() - 1)]
    near = [[("dp", 0)], [("seq", bit) for bit in range(1, lax.axis_size("seq").bit_length() - 1)]]
    if flip:
        near = near[::-1]
    return far + near[0] + near[1] + [("seq", 0)]


def gather_rows(part, flip):
    bits = index_bits()
    own = [own_bit(*place) for place in bits]
    rest = [0] * part.ndim
    known = [1] * len(bits)
    piece = part.reshape((1,) * len(bits) + part.shape)
    whole = jnp.zeros((2,) * len(bits) + part.shape, part.dtype)
    whole = lax.dynamic_update_slice(whole, piece, own + rest)
    for place in gather_order(flip):
        dim = bits.index(place)
        starts = [0 if size == 2 else bit for size, bit in zip(known, own)]
        if max(known) == 2:
            piece = lax.dynamic_slice(whole, starts + rest, known + list(part.shape))
        other = lax.ppermute(piece, place[0], swap_pairs(*place))
        starts[dim] = 1 - own[dim]
        whole = lax.dynamic_update_slice(whole, other, starts + rest)
        known[dim] = 2
    return whole.reshape((-1,) + part.shape[1:])


class Scatter:
    def __init__(self, whole, flip):
        bits = index_bits()
        self.rows = whole.shape[0] >> len(bits)
        self.tail = whole.shape[1:]
        self.kept = whole.reshape((2,) * len(bits) + (self.rows,) + self.tail)
        self.given = None
        order = gather_order(flip)
        self.left = [order[-1]] + order[:-1][::-1]

    def half(self, dim, which):
        part = lax.dynamic_slice_in_dim(self.kept, which, 1, dim)
        if self.given is None:
            return part
        return part + lax.dynamic_slice_in_dim(self.given, which, 1, dim)

    def step(self):
        place = self.left.pop(0)
        dim = index_bits().index(place)
        mine = own_bit(*place)
        other = lax.ppermute(self.half(dim, 1 - mine), place[0], swap_pairs(*place))
        self.kept, self.given = self.half(dim, mine), other

    def finish(self):
        while self.left:
            self.step()
        whole = self.kept + self.given
        return whole.reshape((self.rows,) + self.tail).astype(jnp.float32)


def advance(scatters, *values):
    last = [one.kept if one.given is None else one.given for one in scatters]
    held = lax.optimization_barrier(tuple(last) + values)
    for one, state in zip(scatters, held):
        if one.given is None:
            one.kept = state
        else:
            one.given = state
        if one.left:
            one.step()
    return held[len(scatters) :] if len(values) > 1 else held[-1]


def swap(rows, k):
    if not k:
        return rows
    return lax.ppermute(rows, "seq", [(i, i ^ k) for i in range(lax.axis_size("seq"))])


def shards(
    caption_tokens,
    image_tokens,
    caption_lengths,
    caption_image,
    norm_gain,
    norm_bias,
    self_packed,
    self_output,
    cross_query,
    cross_pair,
    cross_output,
    expand_weight,
    reduce_weight,
    cotangent,
):
    captions, seq_len, model_width = caption_tokens.shape
    peer_count = lax.axis_size("seq")
    position = lax.axis_index("seq")

    owner = (caption_image // captions % peer_count).reshape(peer_count, captions)
    slot = (caption_image % captions).reshape(peer_count, captions)
    peers = jnp.arange(peer_count)
    mine = (peers == position).astype(jnp.int32)
    place = jnp.sum(owner * mine[:, None], axis=0) ^ position
    asked = jnp.sum(jnp.where(owner == position, slot, 0), axis=1)
    turned = (peers[:, None] ^ position) == peers[None, :]
    asked = jnp.sum(jnp.where(turned, asked[None, :], 0), axis=1)
    paired = jnp.concatenate(
        [
            swap(lax.dynamic_slice_in_dim(image_tokens, asked[k], 1), k)
            for k in range(peer_count)
        ]
    )

    norm_columns = jnp.pad(jnp.concatenate([norm_gain, norm_bias], axis=1), ((0, 0), (0, 122)))
    first_group = gather_rows(jnp.concatenate([self_packed, norm_columns], axis=1), False)
    rows = self_packed.shape[0]
    ratio = reduce_weight.shape[0] // rows
    reduce_blocks = [reduce_weight[k * rows : (k + 1) * rows] for k in range(ratio)]
    others = lax.all_gather(
        jnp.concatenate(
            reduce_blocks + [expand_weight, cross_pair, self_output, cross_query, cross_output],
            axis=1,
        ),
        ("dp", "seq"),
        axis=0,
        tiled=True,
    )
    packed_weight = first_group[:, : 3 * model_width]
    norm_values = first_group[:, 3 * model_width : 3 * model_width + 6].astype(jnp.float32)
    norm_gains, norm_shifts = norm_values[:, :3], norm_values[:, 3:]
    hidden_width = expand_weight.shape[1]
    narrower = others[:, 2 * hidden_width :]
    pair_weight = narrower[:, : 2 * model_width]
    output_weight = narrower[:, 2 * model_width : 3 * model_width]
    query_weight = narrower[:, 3 * model_width : 4 * model_width]
    cross_weight = narrower[:, 4 * model_width :]

    live_rows = jnp.arange(seq_len)[None, :] < caption_lengths[:, None]
    inputs = caption_tokens.astype(jnp.float32)
    normed_full, scaled_one, inverse_one = layer_norm(inputs, norm_gains[:, 0], norm_shifts[:, 0])
    normed_one = normed_full.astype(jnp.bfloat16)
    packed = project(normed_one, packed_weight).astype(jnp.bfloat16)
    attended = self_forward(packed, caption_lengths)
    after_self = inputs + project(attended, output_weight)
    normed_full_two, scaled_two, inverse_two = layer_norm(
        after_self, norm_gains[:, 1], norm_shifts[:, 1]
    )
    normed_two = normed_full_two.astype(jnp.bfloat16)
    image_pair = project(paired, pair_weight).astype(jnp.bfloat16)
    query_rows = project(normed_two, query_weight).astype(jnp.bfloat16)
    mixed_rows = cross_forward(query_rows, image_pair, place)
    branch = project(mixed_rows, cross_weight).astype(jnp.bfloat16)
    after_cross = after_self + branch.astype(jnp.float32)
    normed_full_three, scaled_three, inverse_three = layer_norm(
        after_cross, norm_gains[:, 2], norm_shifts[:, 2]
    )
    normed_three = normed_full_three.astype(jnp.bfloat16)
    grad_out = jnp.where(live_rows[..., None], cotangent, jnp.zeros_like(cotangent))
    flat = lambda member: member.reshape(-1, model_width)
    forward, backward, reduce_part, expand_part = ffn(
        flat(normed_three), flat(grad_out), others, rows, hidden_width
    )
    caption_out = jnp.where(
        live_rows[..., None], after_cross + forward.reshape(after_cross.shape), 0.0
    ).astype(jnp.bfloat16)

    narrow = lambda member: member.astype(jnp.bfloat16)
    reduce_sums = Scatter(reduce_part, True)
    expand_sums = Scatter(expand_part, False)
    reduce_sums.step()
    expand_sums.step()
    grad_norm_three, gain_three, shift_three = norm_back(
        backward.reshape(after_cross.shape), scaled_three, inverse_three, norm_gains[:, 2]
    )
    grad_second = grad_out.astype(jnp.float32) + grad_norm_three
    grad_branch = grad_second.astype(jnp.bfloat16)
    grad_cross_mixed = project_back(grad_branch, cross_weight).astype(jnp.bfloat16)
    grad_cross_mixed, grad_branch = advance(
        [reduce_sums, expand_sums], grad_cross_mixed, grad_branch
    )
    cross_output_grad = weight_grad(mixed_rows, grad_branch)
    grad_cross_rows, grad_pair = cross_backward(
        query_rows, image_pair, grad_cross_mixed, place
    )
    cross_pair_grad = weight_grad(paired, grad_pair)
    cross_sums = Scatter(
        narrow(jnp.concatenate([cross_pair_grad, cross_output_grad], axis=1)), True
    )
    grad_pair, grad_cross_rows = advance(
        [reduce_sums, expand_sums, cross_sums], grad_pair, grad_cross_rows
    )
    image_rows = project_back(grad_pair, pair_weight).astype(jnp.bfloat16)
    cross_query_grad = weight_grad(normed_two, grad_cross_rows)
    grad_norm_two, gain_two, shift_two = norm_back(
        project_back(grad_cross_rows, query_weight).astype(jnp.bfloat16).astype(jnp.float32),
        scaled_two,
        inverse_two,
        norm_gains[:, 1],
    )
    grad_first = grad_second + grad_norm_two
    grad_self = grad_first.astype(jnp.bfloat16)
    self_output_grad = weight_grad(attended, grad_self)
    query_sums = Scatter(
        narrow(jnp.concatenate([cross_query_grad, self_output_grad], axis=1)), True
    )
    grad_self, image_rows = advance(
        [reduce_sums, expand_sums, cross_sums, query_sums], grad_self, image_rows
    )
    image_grad = jnp.zeros_like(image_rows)
    for k in range(peer_count):
        home = swap(image_rows[k : k + 1], k)
        image_grad = lax.dynamic_update_slice_in_dim(image_grad, home, asked[k], 0)
    grad_attended = project_back(grad_self, output_weight).astype(jnp.bfloat16)
    grad_packed = self_backward(packed, grad_attended, caption_lengths)
    grad_packed = advance([reduce_sums, expand_sums, cross_sums, query_sums], grad_packed)
    self_packed_grad = weight_grad(normed_one, grad_packed)
    grad_norm_one, gain_one, shift_one = norm_back(
        project_back(grad_packed, packed_weight), scaled_one, inverse_one, norm_gains[:, 0]
    )
    caption_grad = (grad_first + grad_norm_one).astype(jnp.bfloat16)
    norm_sums = jnp.stack([gain_one, gain_two, gain_three, shift_one, shift_two, shift_three], axis=1)
    half = 3 * model_width // 2
    first_sums = Scatter(narrow(self_packed_grad[:, :half]), False)
    second_sums = Scatter(
        narrow(
            jnp.concatenate(
                [self_packed_grad[:, half:], jnp.pad(norm_sums, ((0, 0), (0, 122)))], axis=1
            )
        ),
        True,
    )
    last = [first_sums, second_sums]
    for one in last:
        one.step()
    groups = [query_sums, cross_sums, reduce_sums, expand_sums] + last
    while any(one.left for one in groups):
        advance(groups)
    reduce_grad, expand_grad = reduce_sums.finish(), expand_sums.finish()
    first_sums, second_sums = first_sums.finish(), second_sums.finish()
    cross_sums, query_sums = cross_sums.finish(), query_sums.finish()
    return (
        caption_out,
        caption_grad,
        image_grad,
        second_sums[:, half : half + 3],
        second_sums[:, half + 3 : half + 6],
        jnp.concatenate([first_sums, second_sums[:, :half]], axis=1),
        query_sums[:, model_width:],
        query_sums[:, :model_width],
        cross_sums[:, : 2 * model_width],
        cross_sums[:, 2 * model_width :],
        expand_grad,
        reduce_grad,
    )


def solution(mesh):
    placed = (
        P(("dp", "seq"), None, None),
        P(("dp", "seq"), None, None),
        P(("dp", "seq")),
        P("dp"),
        P(("dp", "seq"), None),
        P(("dp", "seq"), None),
        P(("dp", "seq"), None),
        P(("dp", "seq"), None),
        P(("dp", "seq"), None),
        P(("dp", "seq"), None),
        P(("dp", "seq"), None),
        P(("dp", "seq"), None),
        P(("dp", "seq"), None),
        P(("dp", "seq"), None, None),
    )
    return jax.shard_map(
        shards,
        mesh=mesh,
        in_specs=placed,
        out_specs=(
            P(("dp", "seq"), None, None),
            P(("dp", "seq"), None, None),
            P(("dp", "seq"), None, None),
            P(("dp", "seq"), None),
            P(("dp", "seq"), None),
            P(("dp", "seq"), None),
            P(("dp", "seq"), None),
            P(("dp", "seq"), None),
            P(("dp", "seq"), None),
            P(("dp", "seq"), None),
            P(("dp", "seq"), None),
            P(("dp", "seq"), None),
        ),
        check_vma=False,
    )
```

```python
import functools
import math

import jax
import jax.numpy as jnp
from jax import lax
from jax.experimental import pallas as pl
from jax.experimental.pallas import tpu as pltpu
from jax.sharding import PartitionSpec as P

HEADS = 12
HEAD_DIM = 64


epsilon = 1e-05


TILE = 384
LANES = 128


def project(values, weight):
    flat_rows = values.reshape(-1, values.shape[-1])
    return jnp.dot(flat_rows, weight, preferred_element_type=jnp.float32).reshape(
        values.shape[:-1] + (weight.shape[1],)
    )


def project_back(values, weight):
    flat_rows = values.reshape(-1, values.shape[-1])
    result = lax.dot_general(
        flat_rows, weight, (((1,), (1,)), ((), ())), preferred_element_type=jnp.float32
    )
    return result.reshape(values.shape[:-1] + (weight.shape[0],))


def weight_grad(left_rows, right_rows):
    return lax.dot_general(
        left_rows.reshape(-1, left_rows.shape[-1]),
        right_rows.reshape(-1, right_rows.shape[-1]),
        (((0,), (0,)), ((), ())),
        preferred_element_type=jnp.float32,
    )


def layer_norm(values, gain, shift):
    centred = values - jnp.mean(values, axis=-1, keepdims=True)
    spread = jnp.mean(centred * centred, axis=-1, keepdims=True)
    inverse = lax.rsqrt(spread + epsilon)
    scaled = centred * inverse
    return (scaled * gain + shift, scaled, inverse)


def norm_back(grad_rows, scaled, inverse, gain):
    weighted = grad_rows * gain
    result = inverse * (
        weighted
        - jnp.mean(weighted, axis=-1, keepdims=True)
        - scaled * jnp.mean(weighted * scaled, axis=-1, keepdims=True)
    )
    flat_grad = grad_rows.reshape(-1, grad_rows.shape[-1])
    flat_scaled = scaled.reshape(-1, scaled.shape[-1])
    return (result, jnp.sum(flat_grad * flat_scaled, axis=0), jnp.sum(flat_grad, axis=0))


def dot(left, right, contract):
    return lax.dot_general(left, right, (contract, ((), ())), preferred_element_type=jnp.float32)


def ffn_body(rows_ref, grad_ref, expand_ref, reduce_ref, order_ref, out_ref, back_ref, rgrad_ref, egrad_ref, *, ratio):
    rows, grad = rows_ref[...], grad_ref[...]
    width = rows.shape[1]
    stacked = jnp.concatenate([reduce_ref[:, k * width : (k + 1) * width] for k in range(ratio)], axis=0)
    reduce = dot(order_ref[...], stacked, ((1,), (0,))).astype(jnp.bfloat16)
    expand = expand_ref[...]
    gate = dot(rows, expand, ((1,), (0,)))
    grad_hidden = dot(grad, reduce, ((1,), (1,)))
    share = 0.5 * (1.0 + lax.erf(gate * math.sqrt(0.5)))
    slope = share + gate * (jnp.exp(-0.5 * gate * gate) * (1.0 / math.sqrt(2.0 * math.pi)))
    hidden = (gate * share).astype(jnp.bfloat16)
    grad_gate = (grad_hidden * slope).astype(jnp.bfloat16)
    rgrad_ref[...] = dot(hidden, grad, ((0,), (0,))).astype(jnp.bfloat16)
    egrad_ref[...] = dot(rows, grad_gate, ((0,), (0,))).astype(jnp.bfloat16)
    first = pl.program_id(0) == 0
    @pl.when(first)
    def _():
        out_ref[...] = jnp.zeros_like(out_ref)
        back_ref[...] = jnp.zeros_like(back_ref)
    out_ref[...] += dot(hidden, reduce, ((1,), (0,)))
    back_ref[...] += dot(grad_gate, expand, ((1,), (1,)))


def ffn(rows, grad, others, per_device, hidden_width):
    count, width = rows.shape
    ratio = hidden_width // width
    part = TILE // ratio
    place = jnp.arange(TILE)
    chunk = per_device * ratio
    source = part * (place % chunk // per_device) + per_device * (place // chunk) + place % per_device
    order = (source[:, None] == place[None, :]).astype(jnp.bfloat16)
    whole = lambda shape: pl.BlockSpec(shape, lambda j: (0, 0))
    return pl.pallas_call(
        functools.partial(ffn_body, ratio=ratio),
        grid=(hidden_width // TILE,),
        in_specs=[
            whole((count, width)), whole((count, width)),
            pl.BlockSpec((width, TILE), lambda j: (0, hidden_width // TILE + j)),
            pl.BlockSpec((part, hidden_width), lambda j: (j, 0)),
            whole((TILE, TILE)),
        ],
        out_specs=[
            whole((count, width)), whole((count, width)),
            pl.BlockSpec((TILE, width), lambda j: (j, 0)),
            pl.BlockSpec((width, TILE), lambda j: (0, j)),
        ],
        out_shape=[
            jax.ShapeDtypeStruct((count, width), jnp.float32),
            jax.ShapeDtypeStruct((count, width), jnp.float32),
            jax.ShapeDtypeStruct((hidden_width, width), jnp.bfloat16),
            jax.ShapeDtypeStruct((width, hidden_width), jnp.bfloat16),
        ],
        compiler_params=pltpu.CompilerParams(dimension_semantics=("arbitrary",), vmem_limit_bytes=48 << 20),
        name="ffn",
    )(rows, grad, others, others, order)


def stack_heads(block):
    left = lax.broadcasted_iota(jnp.int32, block.shape, 1) < HEAD_DIM
    none = jnp.zeros_like(block)
    return jnp.concatenate([jnp.where(left, block, none), jnp.where(left, none, block)], axis=0)


def join_heads(stacked):
    count = stacked.shape[0] // 2
    left = lax.broadcasted_iota(jnp.int32, (count, LANES), 1) < HEAD_DIM
    return jnp.where(left, stacked[:count], stacked[count:])


def pair_probs(query, key, length):
    scores = dot(key, query, ((1,), (1,)))
    if length is not None:
        row = lax.broadcasted_iota(jnp.int32, scores.shape, 0)
        column = lax.broadcasted_iota(jnp.int32, scores.shape, 1) % (scores.shape[1] // 2)
        scores = jnp.where((row <= column) & (row < length), scores, -1e30)
    spread = jnp.exp(scores - jnp.max(scores, axis=0, keepdims=True))
    return spread * (1.0 / jnp.sum(spread, axis=0, keepdims=True))


def scaled(block):
    return block * jnp.asarray(1.0 / math.sqrt(HEAD_DIM), block.dtype)


def attend_body(table_ref, query_ref, key_ref, value_ref, out_ref, *, causal):
    length = table_ref[pl.program_id(0)] if causal else None
    for start in range(0, HEADS * HEAD_DIM, LANES):
        lanes = slice(start, start + LANES)
        query = stack_heads(scaled(query_ref[0, :, lanes]))
        probs = pair_probs(query, key_ref[0, :, lanes], length).astype(jnp.bfloat16)
        out_ref[0, :, lanes] = join_heads(dot(probs, value_ref[0, :, lanes], ((0,), (0,)))).astype(jnp.bfloat16)


def attend_back_body(table_ref, query_ref, key_ref, value_ref, grad_ref, query_grad_ref, pair_grad_ref, *, causal):
    length = table_ref[pl.program_id(0)] if causal else None
    width = HEADS * HEAD_DIM
    for start in range(0, width, LANES):
        lanes = slice(start, start + LANES)
        query = stack_heads(scaled(query_ref[0, :, lanes]))
        grad = stack_heads(grad_ref[0, :, lanes])
        key, value = key_ref[0, :, lanes], value_ref[0, :, lanes]
        probs = pair_probs(query, key, length)
        grad_probs = dot(value, grad, ((1,), (1,)))
        grad_scores = probs * (grad_probs - jnp.sum(grad_probs * probs, axis=0, keepdims=True))
        grad_scores = grad_scores.astype(jnp.bfloat16)
        back = lambda left, right: dot(left, right, ((1,), (0,))).astype(jnp.bfloat16)
        grad_query = scaled(join_heads(dot(grad_scores, key, ((0,), (0,))))).astype(jnp.bfloat16)
        grad_key, grad_value = back(grad_scores, query), back(probs.astype(jnp.bfloat16), grad)
        query_grad_ref[0, :, lanes] = grad_query
        if causal:
            query_grad_ref[0, :, slice(width + start, width + start + LANES)] = grad_key
            query_grad_ref[0, :, slice(2 * width + start, 2 * width + start + LANES)] = grad_value
        else:
            pair_grad_ref[0, :, lanes] = grad_key
            pair_grad_ref[0, :, slice(width + start, width + start + LANES)] = grad_value


def attention(body, table, arrays, outs, name, heavy, routed=False):
    width = HEADS * HEAD_DIM
    captions = arrays[0][0].shape[0]
    own = arrays[0][0].shape[1]

    def spec(rows, cols, at):
        if routed and rows != own:
            return pl.BlockSpec((1, rows, cols), lambda c, place: (place[c], 0, at))
        return pl.BlockSpec((1, rows, cols), lambda c, place: (c, 0, at))

    work = heavy * 2 * captions * arrays[0][0].shape[1] * arrays[1][0].shape[1] * width
    return pl.pallas_call(
        body,
        grid_spec=pltpu.PrefetchScalarGridSpec(
            num_scalar_prefetch=1,
            grid=(captions,),
            in_specs=[spec(array.shape[1], width, at) for array, at in arrays],
            out_specs=[spec(rows, cols, 0) for rows, cols in outs],
        ),
        out_shape=[jax.ShapeDtypeStruct((captions, rows, cols), jnp.bfloat16) for rows, cols in outs],
        compiler_params=pltpu.CompilerParams(dimension_semantics=("arbitrary",), vmem_limit_bytes=48 << 20),
        cost_estimate=pl.CostEstimate(flops=work, transcendentals=0, bytes_accessed=0),
        name=name,
    )(table, *(array for array, _ in arrays))


def self_forward(packed, lengths):
    rows, width = packed.shape[1], HEADS * HEAD_DIM
    return attention(functools.partial(attend_body, causal=True), lengths,
        [(packed, 0), (packed, 1), (packed, 2)], [(rows, width)], "self_attention", 2)[0]


def cross_forward(query_rows, pair, place):
    return attention(functools.partial(attend_body, causal=False), place,
        [(query_rows, 0), (pair, 0), (pair, 1)], [query_rows.shape[1:]], "cross_attention", 2, True)[0]


def self_body(*refs):
    attend_back_body(*refs, None, causal=True)


def self_backward(packed, grad_rows, lengths):
    return attention(self_body, lengths,
        [(packed, 0), (packed, 1), (packed, 2), (grad_rows, 0)], [packed.shape[1:]], "self_backward", 5)[0]


def cross_backward(query_rows, pair, grad_rows, place):
    return attention(functools.partial(attend_back_body, causal=False), place,
        [(query_rows, 0), (pair, 0), (pair, 1), (grad_rows, 0)],
        [query_rows.shape[1:], pair.shape[1:]], "cross_backward", 5, True)


def index_bits():
    found = []
    for axis in ("dp", "seq"):
        count = lax.axis_size(axis)
        found += [(axis, bit) for bit in reversed(range(count.bit_length() - 1))]
    return found


def swap_pairs(axis, bit):
    return [(i, i ^ (1 << bit)) for i in range(lax.axis_size(axis))]


def own_bit(axis, bit):
    return (lax.axis_index(axis) >> bit) & 1


def gather_order(flip):
    far = [("dp", bit) for bit in range(1, lax.axis_size("dp").bit_length() - 1)]
    near = [[("dp", 0)], [("seq", bit) for bit in range(1, lax.axis_size("seq").bit_length() - 1)]]
    if flip:
        near = near[::-1]
    return far + near[0] + near[1] + [("seq", 0)]


class Gather:
    def __init__(self, part, flip):
        bits = index_bits()
        self.own = [own_bit(*place) for place in bits]
        self.known = [1] * len(bits)
        self.shape = part.shape
        self.piece = part.reshape((1,) * len(bits) + part.shape)
        self.whole = jnp.zeros((2,) * len(bits) + part.shape, part.dtype)
        self.whole = self.put(self.piece, self.own)
        self.left = gather_order(flip)

    def put(self, piece, starts):
        return lax.dynamic_update_slice(self.whole, piece, starts + [0] * len(self.shape))

    def starts(self):
        return [0 if size == 2 else bit for size, bit in zip(self.known, self.own)]

    def step(self, after=None):
        place = self.left.pop(0)
        dim = index_bits().index(place)
        starts = self.starts()
        if self.piece is None:
            self.piece = lax.dynamic_slice(
                self.whole, starts + [0] * len(self.shape), self.known + list(self.shape)
            )
        if after is not None:
            self.piece, after = lax.optimization_barrier((self.piece, after))
        other = lax.ppermute(self.piece, place[0], swap_pairs(*place))
        starts[dim] = 1 - self.own[dim]
        self.whole = self.put(other, starts)
        self.known[dim] = 2
        self.piece = None
        return other

    def rows(self):
        return self.whole.reshape((-1,) + self.shape[1:])


class Scatter:
    def __init__(self, whole, flip):
        bits = index_bits()
        self.rows = whole.shape[0] >> len(bits)
        self.tail = whole.shape[1:]
        self.state = whole.reshape((2,) * len(bits) + (self.rows,) + self.tail)
        order = gather_order(flip)
        self.left = [order[-1]] + order[:-1][::-1]

    def step(self):
        place = self.left.pop(0)
        dim = index_bits().index(place)
        mine = own_bit(*place)
        given = lax.dynamic_slice_in_dim(self.state, 1 - mine, 1, dim)
        kept = lax.dynamic_slice_in_dim(self.state, mine, 1, dim)
        self.state = kept + lax.ppermute(given, place[0], swap_pairs(*place))

    def finish(self):
        while self.left:
            self.step()
        return self.state.reshape((self.rows,) + self.tail).astype(jnp.float32)


def advance(scatters, *values):
    held = lax.optimization_barrier(tuple(one.state for one in scatters) + values)
    for one, state in zip(scatters, held):
        one.state = state
        if one.left:
            one.step()
    return held[len(scatters) :] if len(values) > 1 else held[-1]


def swap(rows, k):
    if not k:
        return rows
    return lax.ppermute(rows, "seq", [(i, i ^ k) for i in range(lax.axis_size("seq"))])


def put_body(table_ref, *refs):
    for k, ref in enumerate(refs[:-1]):

        @pl.when(pl.program_id(0) == k)
        def _():
            refs[-1][...] = ref[...]


def put_rows(pieces, table):
    shape = pieces[0].shape
    return pl.pallas_call(
        put_body,
        grid_spec=pltpu.PrefetchScalarGridSpec(
            num_scalar_prefetch=1,
            grid=(len(pieces),),
            in_specs=[pl.BlockSpec(shape, lambda k, at: (0, 0, 0)) for _ in pieces],
            out_specs=pl.BlockSpec(shape, lambda k, at: (at[k], 0, 0)),
        ),
        out_shape=jax.ShapeDtypeStruct((len(pieces),) + shape[1:], pieces[0].dtype),
        compiler_params=pltpu.CompilerParams(dimension_semantics=("arbitrary",)),
        name="put_rows",
    )(table, *pieces)


def shards(
    caption_tokens,
    image_tokens,
    caption_lengths,
    caption_image,
    norm_gain,
    norm_bias,
    self_packed,
    self_output,
    cross_query,
    cross_pair,
    cross_output,
    expand_weight,
    reduce_weight,
    cotangent,
):
    captions, seq_len, model_width = caption_tokens.shape
    peer_count = lax.axis_size("seq")
    position = lax.axis_index("seq")

    owner = (caption_image // captions % peer_count).reshape(peer_count, captions)
    slot = (caption_image % captions).reshape(peer_count, captions)
    peers = jnp.arange(peer_count)
    mine = (peers == position).astype(jnp.int32)
    place = jnp.sum(owner * mine[:, None], axis=0) ^ position
    asked = jnp.sum(jnp.where(owner == position, slot, 0), axis=1)
    turned = (peers[:, None] ^ position) == peers[None, :]
    asked = jnp.sum(jnp.where(turned, asked[None, :], 0), axis=1)
    paired = jnp.concatenate(
        [
            swap(lax.dynamic_slice_in_dim(image_tokens, asked[k], 1), k)
            for k in range(peer_count)
        ]
    )

    norm_columns = jnp.pad(jnp.concatenate([norm_gain, norm_bias], axis=1), ((0, 0), (0, 122)))
    rows = self_packed.shape[0]
    ratio = reduce_weight.shape[0] // rows
    reduce_blocks = [reduce_weight[k * rows : (k + 1) * rows] for k in range(ratio)]
    wide = lax.all_gather(
        jnp.concatenate(reduce_blocks + [expand_weight], axis=1),
        ("dp", "seq"),
        axis=0,
        tiled=True,
    )
    first_group = Gather(jnp.concatenate([self_packed, norm_columns], axis=1), True)
    second_group = Gather(
        jnp.concatenate([cross_pair, self_output, cross_query, cross_output], axis=1), True
    )
    while first_group.left:
        second_group.step(first_group.step())
    first_group, narrower = first_group.rows(), second_group.rows()
    packed_weight = first_group[:, : 3 * model_width]
    norm_values = first_group[:, 3 * model_width : 3 * model_width + 6].astype(jnp.float32)
    norm_gains, norm_shifts = norm_values[:, :3], norm_values[:, 3:]
    hidden_width = expand_weight.shape[1]
    pair_weight = narrower[:, : 2 * model_width]
    output_weight = narrower[:, 2 * model_width : 3 * model_width]
    query_weight = narrower[:, 3 * model_width : 4 * model_width]
    cross_weight = narrower[:, 4 * model_width :]

    live_rows = jnp.arange(seq_len)[None, :] < caption_lengths[:, None]
    inputs = caption_tokens.astype(jnp.float32)
    normed_full, scaled_one, inverse_one = layer_norm(inputs, norm_gains[:, 0], norm_shifts[:, 0])
    normed_one = normed_full.astype(jnp.bfloat16)
    packed = project(normed_one, packed_weight).astype(jnp.bfloat16)
    attended = self_forward(packed, caption_lengths)
    after_self = inputs + project(attended, output_weight)
    normed_full_two, scaled_two, inverse_two = layer_norm(
        after_self, norm_gains[:, 1], norm_shifts[:, 1]
    )
    normed_two = normed_full_two.astype(jnp.bfloat16)
    image_pair = project(paired, pair_weight).astype(jnp.bfloat16)
    query_rows = project(normed_two, query_weight).astype(jnp.bfloat16)
    mixed_rows = cross_forward(query_rows, image_pair, place)
    branch = project(mixed_rows, cross_weight).astype(jnp.bfloat16)
    after_cross = after_self + branch.astype(jnp.float32)
    normed_full_three, scaled_three, inverse_three = layer_norm(
        after_cross, norm_gains[:, 2], norm_shifts[:, 2]
    )
    normed_three = normed_full_three.astype(jnp.bfloat16)
    grad_out = jnp.where(live_rows[..., None], cotangent, jnp.zeros_like(cotangent))
    flat = lambda member: member.reshape(-1, model_width)
    forward, backward, reduce_part, expand_part = ffn(
        flat(normed_three), flat(grad_out), wide, rows, hidden_width
    )
    caption_out = jnp.where(
        live_rows[..., None], after_cross + forward.reshape(after_cross.shape), 0.0
    ).astype(jnp.bfloat16)

    narrow = lambda member: member.astype(jnp.bfloat16)
    reduce_sums = Scatter(reduce_part, True)
    expand_sums = Scatter(expand_part, False)
    reduce_sums.step()
    expand_sums.step()
    grad_norm_three, gain_three, shift_three = norm_back(
        backward.reshape(after_cross.shape), scaled_three, inverse_three, norm_gains[:, 2]
    )
    grad_second = grad_out.astype(jnp.float32) + grad_norm_three
    grad_branch = grad_second.astype(jnp.bfloat16)
    grad_cross_mixed = project_back(grad_branch, cross_weight).astype(jnp.bfloat16)
    grad_cross_mixed, grad_branch = advance(
        [reduce_sums, expand_sums], grad_cross_mixed, grad_branch
    )
    cross_output_grad = weight_grad(mixed_rows, grad_branch)
    grad_cross_rows, grad_pair = cross_backward(
        query_rows, image_pair, grad_cross_mixed, place
    )
    cross_pair_grad = weight_grad(paired, grad_pair)
    cross_sums = Scatter(
        narrow(jnp.concatenate([cross_pair_grad, cross_output_grad], axis=1)), True
    )
    grad_pair, grad_cross_rows = advance(
        [reduce_sums, expand_sums, cross_sums], grad_pair, grad_cross_rows
    )
    image_rows = project_back(grad_pair, pair_weight).astype(jnp.bfloat16)
    cross_query_grad = weight_grad(normed_two, grad_cross_rows)
    grad_norm_two, gain_two, shift_two = norm_back(
        project_back(grad_cross_rows, query_weight).astype(jnp.bfloat16).astype(jnp.float32),
        scaled_two,
        inverse_two,
        norm_gains[:, 1],
    )
    grad_first = grad_second + grad_norm_two
    grad_self = grad_first.astype(jnp.bfloat16)
    self_output_grad = weight_grad(attended, grad_self)
    query_sums = Scatter(
        narrow(jnp.concatenate([cross_query_grad, self_output_grad], axis=1)), True
    )
    grad_self, image_rows = advance(
        [reduce_sums, expand_sums, cross_sums, query_sums], grad_self, image_rows
    )
    image_grad = put_rows(
        [swap(image_rows[k : k + 1], k) for k in range(peer_count)], asked
    )
    grad_attended = project_back(grad_self, output_weight).astype(jnp.bfloat16)
    grad_packed = self_backward(packed, grad_attended, caption_lengths)
    grad_packed = advance([reduce_sums, expand_sums, cross_sums, query_sums], grad_packed)
    self_packed_grad = weight_grad(normed_one, grad_packed)
    grad_norm_one, gain_one, shift_one = norm_back(
        project_back(grad_packed, packed_weight), scaled_one, inverse_one, norm_gains[:, 0]
    )
    caption_grad = (grad_first + grad_norm_one).astype(jnp.bfloat16)
    norm_sums = jnp.stack([gain_one, gain_two, gain_three, shift_one, shift_two, shift_three], axis=1)
    half = 3 * model_width // 2
    first_sums = Scatter(narrow(self_packed_grad[:, :half]), False)
    second_sums = Scatter(
        narrow(
            jnp.concatenate(
                [self_packed_grad[:, half:], jnp.pad(norm_sums, ((0, 0), (0, 122)))], axis=1
            )
        ),
        True,
    )
    last = [first_sums, second_sums]
    for one in last:
        one.step()
    groups = [query_sums, cross_sums, reduce_sums, expand_sums] + last
    while any(one.left for one in groups):
        advance(groups)
    reduce_grad, expand_grad = reduce_sums.finish(), expand_sums.finish()
    first_sums, second_sums = first_sums.finish(), second_sums.finish()
    cross_sums, query_sums = cross_sums.finish(), query_sums.finish()
    return (
        caption_out,
        caption_grad,
        image_grad,
        second_sums[:, half : half + 3],
        second_sums[:, half + 3 : half + 6],
        jnp.concatenate([first_sums, second_sums[:, :half]], axis=1),
        query_sums[:, model_width:],
        query_sums[:, :model_width],
        cross_sums[:, : 2 * model_width],
        cross_sums[:, 2 * model_width :],
        expand_grad,
        reduce_grad,
    )


def solution(mesh):
    placed = (
        P(("dp", "seq"), None, None),
        P(("dp", "seq"), None, None),
        P(("dp", "seq")),
        P("dp"),
        P(("dp", "seq"), None),
        P(("dp", "seq"), None),
        P(("dp", "seq"), None),
        P(("dp", "seq"), None),
        P(("dp", "seq"), None),
        P(("dp", "seq"), None),
        P(("dp", "seq"), None),
        P(("dp", "seq"), None),
        P(("dp", "seq"), None),
        P(("dp", "seq"), None, None),
    )
    return jax.shard_map(
        shards,
        mesh=mesh,
        in_specs=placed,
        out_specs=(
            P(("dp", "seq"), None, None),
            P(("dp", "seq"), None, None),
            P(("dp", "seq"), None, None),
            P(("dp", "seq"), None),
            P(("dp", "seq"), None),
            P(("dp", "seq"), None),
            P(("dp", "seq"), None),
            P(("dp", "seq"), None),
            P(("dp", "seq"), None),
            P(("dp", "seq"), None),
            P(("dp", "seq"), None),
            P(("dp", "seq"), None),
        ),
        check_vma=False,
    )
```

```python
import functools
import itertools
import math

import jax
import jax.numpy as jnp
from jax import lax
from jax.experimental import pallas as pl
from jax.experimental.pallas import tpu as pltpu
from jax.sharding import PartitionSpec as P

HEADS = 12
HEAD_DIM = 64


epsilon = 1e-05


TILE = 384
LANES = 128


def project(values, weight):
    flat_rows = values.reshape(-1, values.shape[-1])
    return jnp.dot(flat_rows, weight, preferred_element_type=jnp.float32).reshape(
        values.shape[:-1] + (weight.shape[1],)
    )


def project_back(values, weight):
    flat_rows = values.reshape(-1, values.shape[-1])
    result = lax.dot_general(
        flat_rows, weight, (((1,), (1,)), ((), ())), preferred_element_type=jnp.float32
    )
    return result.reshape(values.shape[:-1] + (weight.shape[0],))


def weight_grad(left_rows, right_rows):
    return lax.dot_general(
        left_rows.reshape(-1, left_rows.shape[-1]),
        right_rows.reshape(-1, right_rows.shape[-1]),
        (((0,), (0,)), ((), ())),
        preferred_element_type=jnp.float32,
    )


def layer_norm(values, gain, shift):
    centred = values - jnp.mean(values, axis=-1, keepdims=True)
    spread = jnp.mean(centred * centred, axis=-1, keepdims=True)
    inverse = lax.rsqrt(spread + epsilon)
    scaled = centred * inverse
    return (scaled * gain + shift, scaled, inverse)


def norm_back(grad_rows, scaled, inverse, gain):
    weighted = grad_rows * gain
    result = inverse * (
        weighted
        - jnp.mean(weighted, axis=-1, keepdims=True)
        - scaled * jnp.mean(weighted * scaled, axis=-1, keepdims=True)
    )
    flat_grad = grad_rows.reshape(-1, grad_rows.shape[-1])
    flat_scaled = scaled.reshape(-1, scaled.shape[-1])
    return (result, jnp.sum(flat_grad * flat_scaled, axis=0), jnp.sum(flat_grad, axis=0))


def dot(left, right, contract):
    return lax.dot_general(left, right, (contract, ((), ())), preferred_element_type=jnp.float32)


def ffn_body(rows_ref, grad_ref, expand_ref, reduce_ref, order_ref, out_ref, back_ref, rgrad_ref, egrad_ref, *, ratio):
    rows, grad = rows_ref[...], grad_ref[...]
    width = rows.shape[1]
    stacked = jnp.concatenate([reduce_ref[:, k * width : (k + 1) * width] for k in range(ratio)], axis=0)
    reduce = dot(order_ref[...], stacked, ((1,), (0,))).astype(jnp.bfloat16)
    expand = expand_ref[...]
    gate = dot(rows, expand, ((1,), (0,)))
    grad_hidden = dot(grad, reduce, ((1,), (1,)))
    share = 0.5 * (1.0 + lax.erf(gate * math.sqrt(0.5)))
    slope = share + gate * (jnp.exp(-0.5 * gate * gate) * (1.0 / math.sqrt(2.0 * math.pi)))
    hidden = (gate * share).astype(jnp.bfloat16)
    grad_gate = (grad_hidden * slope).astype(jnp.bfloat16)
    rgrad_ref[...] = dot(hidden, grad, ((0,), (0,))).astype(jnp.bfloat16)
    egrad_ref[...] = dot(rows, grad_gate, ((0,), (0,))).astype(jnp.bfloat16)
    first = pl.program_id(0) == 0
    @pl.when(first)
    def _():
        out_ref[...] = jnp.zeros_like(out_ref)
        back_ref[...] = jnp.zeros_like(back_ref)
    out_ref[...] += dot(hidden, reduce, ((1,), (0,)))
    back_ref[...] += dot(grad_gate, expand, ((1,), (1,)))


def ffn(rows, grad, others, per_device, hidden_width):
    count, width = rows.shape
    ratio = hidden_width // width
    part = TILE // ratio
    place = jnp.arange(TILE)
    chunk = per_device * ratio
    source = part * (place % chunk // per_device) + per_device * (place // chunk) + place % per_device
    order = (source[:, None] == place[None, :]).astype(jnp.bfloat16)
    whole = lambda shape: pl.BlockSpec(shape, lambda j: (0, 0))
    return pl.pallas_call(
        functools.partial(ffn_body, ratio=ratio),
        grid=(hidden_width // TILE,),
        in_specs=[
            whole((count, width)), whole((count, width)),
            pl.BlockSpec((width, TILE), lambda j: (0, hidden_width // TILE + j)),
            pl.BlockSpec((part, hidden_width), lambda j: (j, 0)),
            whole((TILE, TILE)),
        ],
        out_specs=[
            whole((count, width)), whole((count, width)),
            pl.BlockSpec((TILE, width), lambda j: (j, 0)),
            pl.BlockSpec((width, TILE), lambda j: (0, j)),
        ],
        out_shape=[
            jax.ShapeDtypeStruct((count, width), jnp.float32),
            jax.ShapeDtypeStruct((count, width), jnp.float32),
            jax.ShapeDtypeStruct((hidden_width, width), jnp.bfloat16),
            jax.ShapeDtypeStruct((width, hidden_width), jnp.bfloat16),
        ],
        compiler_params=pltpu.CompilerParams(dimension_semantics=("arbitrary",), vmem_limit_bytes=48 << 20),
        name="ffn",
    )(rows, grad, others, others, order)


def stack_heads(block):
    left = lax.broadcasted_iota(jnp.int32, block.shape, 1) < HEAD_DIM
    none = jnp.zeros_like(block)
    return jnp.concatenate([jnp.where(left, block, none), jnp.where(left, none, block)], axis=0)


def join_heads(stacked):
    count = stacked.shape[0] // 2
    left = lax.broadcasted_iota(jnp.int32, (count, LANES), 1) < HEAD_DIM
    return jnp.where(left, stacked[:count], stacked[count:])


def pair_probs(query, key, length):
    scores = dot(key, query, ((1,), (1,)))
    if length is not None:
        row = lax.broadcasted_iota(jnp.int32, scores.shape, 0)
        column = lax.broadcasted_iota(jnp.int32, scores.shape, 1) % (scores.shape[1] // 2)
        scores = jnp.where((row <= column) & (row < length), scores, -1e30)
    spread = jnp.exp(scores - jnp.max(scores, axis=0, keepdims=True))
    return spread * (1.0 / jnp.sum(spread, axis=0, keepdims=True))


def scaled(block):
    return block * jnp.asarray(1.0 / math.sqrt(HEAD_DIM), block.dtype)


def attend_body(table_ref, query_ref, key_ref, value_ref, out_ref, *, causal):
    length = table_ref[pl.program_id(0)] if causal else None
    for start in range(0, HEADS * HEAD_DIM, LANES):
        lanes = slice(start, start + LANES)
        query = stack_heads(scaled(query_ref[0, :, lanes]))
        probs = pair_probs(query, key_ref[0, :, lanes], length).astype(jnp.bfloat16)
        out_ref[0, :, lanes] = join_heads(dot(probs, value_ref[0, :, lanes], ((0,), (0,)))).astype(jnp.bfloat16)


def attend_back_body(table_ref, query_ref, key_ref, value_ref, grad_ref, query_grad_ref, pair_grad_ref, *, causal):
    length = table_ref[pl.program_id(0)] if causal else None
    width = HEADS * HEAD_DIM
    for start in range(0, width, LANES):
        lanes = slice(start, start + LANES)
        query = stack_heads(scaled(query_ref[0, :, lanes]))
        grad = stack_heads(grad_ref[0, :, lanes])
        key, value = key_ref[0, :, lanes], value_ref[0, :, lanes]
        probs = pair_probs(query, key, length)
        grad_probs = dot(value, grad, ((1,), (1,)))
        grad_scores = probs * (grad_probs - jnp.sum(grad_probs * probs, axis=0, keepdims=True))
        grad_scores = grad_scores.astype(jnp.bfloat16)
        back = lambda left, right: dot(left, right, ((1,), (0,))).astype(jnp.bfloat16)
        grad_query = scaled(join_heads(dot(grad_scores, key, ((0,), (0,))))).astype(jnp.bfloat16)
        grad_key, grad_value = back(grad_scores, query), back(probs.astype(jnp.bfloat16), grad)
        query_grad_ref[0, :, lanes] = grad_query
        if causal:
            query_grad_ref[0, :, slice(width + start, width + start + LANES)] = grad_key
            query_grad_ref[0, :, slice(2 * width + start, 2 * width + start + LANES)] = grad_value
        else:
            pair_grad_ref[0, :, lanes] = grad_key
            pair_grad_ref[0, :, slice(width + start, width + start + LANES)] = grad_value


def attention(body, table, arrays, outs, name, heavy, routed=False):
    width = HEADS * HEAD_DIM
    captions = arrays[0][0].shape[0]
    own = arrays[0][0].shape[1]

    def spec(rows, cols, at):
        if routed and rows != own:
            return pl.BlockSpec((1, rows, cols), lambda c, place: (place[c], 0, at))
        return pl.BlockSpec((1, rows, cols), lambda c, place: (c, 0, at))

    work = heavy * 2 * captions * arrays[0][0].shape[1] * arrays[1][0].shape[1] * width
    return pl.pallas_call(
        body,
        grid_spec=pltpu.PrefetchScalarGridSpec(
            num_scalar_prefetch=1,
            grid=(captions,),
            in_specs=[spec(array.shape[1], width, at) for array, at in arrays],
            out_specs=[spec(rows, cols, 0) for rows, cols in outs],
        ),
        out_shape=[jax.ShapeDtypeStruct((captions, rows, cols), jnp.bfloat16) for rows, cols in outs],
        compiler_params=pltpu.CompilerParams(dimension_semantics=("arbitrary",), vmem_limit_bytes=48 << 20),
        cost_estimate=pl.CostEstimate(flops=work, transcendentals=0, bytes_accessed=0),
        name=name,
    )(table, *(array for array, _ in arrays))


def self_forward(packed, lengths):
    rows, width = packed.shape[1], HEADS * HEAD_DIM
    return attention(functools.partial(attend_body, causal=True), lengths,
        [(packed, 0), (packed, 1), (packed, 2)], [(rows, width)], "self_attention", 2)[0]


def cross_forward(query_rows, pair, place):
    return attention(functools.partial(attend_body, causal=False), place,
        [(query_rows, 0), (pair, 0), (pair, 1)], [query_rows.shape[1:]], "cross_attention", 2, True)[0]


def self_body(*refs):
    attend_back_body(*refs, None, causal=True)


def self_backward(packed, grad_rows, lengths):
    return attention(self_body, lengths,
        [(packed, 0), (packed, 1), (packed, 2), (grad_rows, 0)], [packed.shape[1:]], "self_backward", 5)[0]


def cross_backward(query_rows, pair, grad_rows, place):
    return attention(functools.partial(attend_back_body, causal=False), place,
        [(query_rows, 0), (pair, 0), (pair, 1), (grad_rows, 0)],
        [query_rows.shape[1:], pair.shape[1:]], "cross_backward", 5, True)


def index_bits():
    found = []
    for axis in ("dp", "seq"):
        count = lax.axis_size(axis)
        found += [(axis, bit) for bit in reversed(range(count.bit_length() - 1))]
    return found


def swap_pairs(axis, bit):
    return [(i, i ^ (1 << bit)) for i in range(lax.axis_size(axis))]


def own_bit(axis, bit):
    return (lax.axis_index(axis) >> bit) & 1


def gather_order(flip):
    far = [("dp", bit) for bit in range(1, lax.axis_size("dp").bit_length() - 1)]
    near = [[("dp", 0)], [("seq", bit) for bit in range(1, lax.axis_size("seq").bit_length() - 1)]]
    if flip:
        near = near[::-1]
    return far + near[0] + near[1] + [("seq", 0)]


class Gather:
    def __init__(self, part, flip):
        bits = index_bits()
        self.own = [own_bit(*place) for place in bits]
        self.known = [1] * len(bits)
        self.shape = part.shape
        self.piece = part.reshape((1,) * len(bits) + part.shape)
        self.whole = jnp.zeros((2,) * len(bits) + part.shape, part.dtype)
        self.whole = self.put(self.piece, self.own)
        self.left = gather_order(flip)

    def put(self, piece, starts):
        return lax.dynamic_update_slice(self.whole, piece, starts + [0] * len(self.shape))

    def starts(self):
        return [0 if size == 2 else bit for size, bit in zip(self.known, self.own)]

    def step(self):
        place = self.left.pop(0)
        dim = index_bits().index(place)
        starts = self.starts()
        if self.piece is None:
            self.piece = lax.dynamic_slice(
                self.whole, starts + [0] * len(self.shape), self.known + list(self.shape)
            )
        other = lax.ppermute(self.piece, place[0], swap_pairs(*place))
        starts[dim] = 1 - self.own[dim]
        self.whole = self.put(other, starts)
        self.known[dim] = 2
        self.piece = None

    def rows(self):
        return self.whole.reshape((-1,) + self.shape[1:])


class Scatter:
    def __init__(self, whole, flip, span):
        bits = index_bits()
        self.rows = whole.shape[0] >> len(bits)
        self.tail = whole.shape[1:]
        self.state = whole.reshape((2,) * len(bits) + (self.rows,) + self.tail)
        order = gather_order(flip)
        far = [place for place in order[:-3]][::-1]
        pairs = [far[i : i + span] for i in range(0, len(far), span)]
        self.left = [[order[-1]], [order[-2]], [order[-3]]] + pairs

    def part(self, places, turn):
        part = self.state
        for place, flipped in zip(places, turn):
            dim = index_bits().index(place)
            part = lax.dynamic_slice_in_dim(part, own_bit(*place) ^ flipped, 1, dim)
        return part

    def step(self):
        places = self.left.pop(0)
        axis = places[0][0]
        total = self.part(places, [0] * len(places))
        for turn in list(itertools.product((0, 1), repeat=len(places)))[1:]:
            mask = sum(flipped << place[1] for place, flipped in zip(places, turn))
            pairs = [(i, i ^ mask) for i in range(lax.axis_size(axis))]
            total = total + lax.ppermute(self.part(places, turn), axis, pairs)
        self.state = total

    def join(self, other):
        self.state = jnp.concatenate([self.state, other.state], axis=-1)
        self.tail = self.state.shape[-1:]

    def finish(self):
        while self.left:
            self.step()
        return self.state.reshape((self.rows,) + self.tail).astype(jnp.float32)


def advance(scatters, *values):
    held = lax.optimization_barrier(tuple(one.state for one in scatters) + values)
    for one, state in zip(scatters, held):
        one.state = state
        if one.left:
            one.step()
    values = held[len(scatters) :]
    return values[0] if len(values) == 1 else values


def swap(rows, k):
    if not k:
        return rows
    return lax.ppermute(rows, "seq", [(i, i ^ k) for i in range(lax.axis_size("seq"))])


def put_body(table_ref, *refs):
    for k, ref in enumerate(refs[:-1]):

        @pl.when(pl.program_id(0) == k)
        def _():
            refs[-1][...] = ref[...]


def put_rows(pieces, table):
    shape = pieces[0].shape
    return pl.pallas_call(
        put_body,
        grid_spec=pltpu.PrefetchScalarGridSpec(
            num_scalar_prefetch=1,
            grid=(len(pieces),),
            in_specs=[pl.BlockSpec(shape, lambda k, at: (0, 0, 0)) for _ in pieces],
            out_specs=pl.BlockSpec(shape, lambda k, at: (at[k], 0, 0)),
        ),
        out_shape=jax.ShapeDtypeStruct((len(pieces),) + shape[1:], pieces[0].dtype),
        compiler_params=pltpu.CompilerParams(dimension_semantics=("arbitrary",)),
        cost_estimate=pl.CostEstimate(
            flops=0, transcendentals=0, bytes_accessed=4 * len(pieces) * shape[1] * shape[2]
        ),
        name="put_rows",
    )(table, *pieces)


def shards(
    caption_tokens,
    image_tokens,
    caption_lengths,
    caption_image,
    norm_gain,
    norm_bias,
    self_packed,
    self_output,
    cross_query,
    cross_pair,
    cross_output,
    expand_weight,
    reduce_weight,
    cotangent,
):
    captions, seq_len, model_width = caption_tokens.shape
    peer_count = lax.axis_size("seq")
    position = lax.axis_index("seq")

    owner = (caption_image // captions % peer_count).reshape(peer_count, captions)
    slot = (caption_image % captions).reshape(peer_count, captions)
    peers = jnp.arange(peer_count)
    mine = (peers == position).astype(jnp.int32)
    place = jnp.sum(owner * mine[:, None], axis=0) ^ position
    asked = jnp.sum(jnp.where(owner == position, slot, 0), axis=1)
    turned = (peers[:, None] ^ position) == peers[None, :]
    asked = jnp.sum(jnp.where(turned, asked[None, :], 0), axis=1)
    paired = jnp.concatenate(
        [
            swap(lax.dynamic_slice_in_dim(image_tokens, asked[k], 1), k)
            for k in range(peer_count)
        ]
    )

    norm_columns = jnp.pad(jnp.concatenate([norm_gain, norm_bias], axis=1), ((0, 0), (0, 122)))
    rows = self_packed.shape[0]
    ratio = reduce_weight.shape[0] // rows
    reduce_blocks = [reduce_weight[k * rows : (k + 1) * rows] for k in range(ratio)]
    wide = lax.all_gather(
        jnp.concatenate(
            reduce_blocks + [expand_weight, cross_pair, self_output, cross_query, cross_output],
            axis=1,
        ),
        ("dp", "seq"),
        axis=0,
        tiled=True,
    )
    first_group = Gather(jnp.concatenate([self_packed, norm_columns], axis=1), False)
    while first_group.left:
        first_group.step()
    first_group = first_group.rows()
    packed_weight = first_group[:, : 3 * model_width]
    norm_values = first_group[:, 3 * model_width : 3 * model_width + 6].astype(jnp.float32)
    norm_gains, norm_shifts = norm_values[:, :3], norm_values[:, 3:]
    hidden_width = expand_weight.shape[1]
    narrower = wide[:, 2 * hidden_width :]
    pair_weight = narrower[:, : 2 * model_width]
    output_weight = narrower[:, 2 * model_width : 3 * model_width]
    query_weight = narrower[:, 3 * model_width : 4 * model_width]
    cross_weight = narrower[:, 4 * model_width :]

    live_rows = jnp.arange(seq_len)[None, :] < caption_lengths[:, None]
    inputs = caption_tokens.astype(jnp.float32)
    normed_full, scaled_one, inverse_one = layer_norm(inputs, norm_gains[:, 0], norm_shifts[:, 0])
    normed_one = normed_full.astype(jnp.bfloat16)
    packed = project(normed_one, packed_weight).astype(jnp.bfloat16)
    attended = self_forward(packed, caption_lengths)
    after_self = inputs + project(attended, output_weight)
    normed_full_two, scaled_two, inverse_two = layer_norm(
        after_self, norm_gains[:, 1], norm_shifts[:, 1]
    )
    normed_two = normed_full_two.astype(jnp.bfloat16)
    image_pair = project(paired, pair_weight).astype(jnp.bfloat16)
    query_rows = project(normed_two, query_weight).astype(jnp.bfloat16)
    mixed_rows = cross_forward(query_rows, image_pair, place)
    branch = project(mixed_rows, cross_weight).astype(jnp.bfloat16)
    after_cross = after_self + branch.astype(jnp.float32)
    normed_full_three, scaled_three, inverse_three = layer_norm(
        after_cross, norm_gains[:, 2], norm_shifts[:, 2]
    )
    normed_three = normed_full_three.astype(jnp.bfloat16)
    grad_out = jnp.where(live_rows[..., None], cotangent, jnp.zeros_like(cotangent))
    flat = lambda member: member.reshape(-1, model_width)
    forward, backward, reduce_part, expand_part = ffn(
        flat(normed_three), flat(grad_out), wide, rows, hidden_width
    )
    caption_out = jnp.where(
        live_rows[..., None], after_cross + forward.reshape(after_cross.shape), 0.0
    ).astype(jnp.bfloat16)

    narrow = lambda member: member.astype(jnp.bfloat16)
    reduce_sums = Scatter(reduce_part, True, 1)
    expand_sums = Scatter(expand_part, False, 1)
    reduce_sums.step()
    expand_sums.step()
    grad_norm_three, gain_three, shift_three = norm_back(
        backward.reshape(after_cross.shape), scaled_three, inverse_three, norm_gains[:, 2]
    )
    grad_second = grad_out.astype(jnp.float32) + grad_norm_three
    grad_branch = grad_second.astype(jnp.bfloat16)
    grad_cross_mixed = project_back(grad_branch, cross_weight).astype(jnp.bfloat16)
    grad_cross_mixed, grad_branch = advance(
        [reduce_sums, expand_sums], grad_cross_mixed, grad_branch
    )
    cross_output_grad = weight_grad(mixed_rows, grad_branch)
    grad_cross_rows, grad_pair = cross_backward(
        query_rows, image_pair, grad_cross_mixed, place
    )
    cross_pair_grad = weight_grad(paired, grad_pair)
    cross_sums = Scatter(
        narrow(jnp.concatenate([cross_pair_grad, cross_output_grad], axis=1)), True, 2
    )
    grad_pair, grad_cross_rows = advance(
        [reduce_sums, expand_sums, cross_sums], grad_pair, grad_cross_rows
    )
    image_rows = project_back(grad_pair, pair_weight).astype(jnp.bfloat16)
    cross_query_grad = weight_grad(normed_two, grad_cross_rows)
    grad_norm_two, gain_two, shift_two = norm_back(
        project_back(grad_cross_rows, query_weight).astype(jnp.bfloat16).astype(jnp.float32),
        scaled_two,
        inverse_two,
        norm_gains[:, 1],
    )
    grad_first = grad_second + grad_norm_two
    grad_self = grad_first.astype(jnp.bfloat16)
    self_output_grad = weight_grad(attended, grad_self)
    query_sums = Scatter(
        narrow(jnp.concatenate([cross_query_grad, self_output_grad], axis=1)), True, 2
    )
    grad_self, image_rows = advance(
        [reduce_sums, expand_sums, cross_sums, query_sums], grad_self, image_rows
    )
    home = [swap(image_rows[k : k + 1], k) for k in range(peer_count)]
    grad_attended = project_back(grad_self, output_weight).astype(jnp.bfloat16)
    grad_packed = self_backward(packed, grad_attended, caption_lengths)
    grad_packed, *home = advance(
        [reduce_sums, expand_sums, cross_sums, query_sums], grad_packed, *home
    )
    self_packed_grad = weight_grad(normed_one, grad_packed)
    grad_norm_one, gain_one, shift_one = norm_back(
        project_back(grad_packed, packed_weight), scaled_one, inverse_one, norm_gains[:, 0]
    )
    caption_grad = (grad_first + grad_norm_one).astype(jnp.bfloat16)
    norm_sums = jnp.stack([gain_one, gain_two, gain_three, shift_one, shift_two, shift_three], axis=1)
    half = 3 * model_width // 2
    first_sums = Scatter(narrow(self_packed_grad[:, :half]), False, 2)
    second_sums = Scatter(
        narrow(
            jnp.concatenate(
                [self_packed_grad[:, half:], jnp.pad(norm_sums, ((0, 0), (0, 122)))], axis=1
            )
        ),
        True,
        2,
    )
    last = [first_sums, second_sums]
    for one in last:
        one.step()
    groups = [query_sums, cross_sums, reduce_sums, expand_sums] + last
    while len(first_sums.left) > 1:
        advance(groups)
    first_sums.join(second_sums)
    home = advance([first_sums], *home)
    image_grad = put_rows(list(home), asked)
    self_sums = first_sums.finish()
    reduce_grad, expand_grad = reduce_sums.finish(), expand_sums.finish()
    cross_sums, query_sums = cross_sums.finish(), query_sums.finish()
    return (
        caption_out,
        caption_grad,
        image_grad,
        self_sums[:, 2 * half : 2 * half + 3],
        self_sums[:, 2 * half + 3 : 2 * half + 6],
        self_sums[:, : 2 * half],
        query_sums[:, model_width:],
        query_sums[:, :model_width],
        cross_sums[:, : 2 * model_width],
        cross_sums[:, 2 * model_width :],
        expand_grad,
        reduce_grad,
    )


def solution(mesh):
    placed = (
        P(("dp", "seq"), None, None),
        P(("dp", "seq"), None, None),
        P(("dp", "seq")),
        P("dp"),
        P(("dp", "seq"), None),
        P(("dp", "seq"), None),
        P(("dp", "seq"), None),
        P(("dp", "seq"), None),
        P(("dp", "seq"), None),
        P(("dp", "seq"), None),
        P(("dp", "seq"), None),
        P(("dp", "seq"), None),
        P(("dp", "seq"), None),
        P(("dp", "seq"), None, None),
    )
    return jax.shard_map(
        shards,
        mesh=mesh,
        in_specs=placed,
        out_specs=(
            P(("dp", "seq"), None, None),
            P(("dp", "seq"), None, None),
            P(("dp", "seq"), None, None),
            P(("dp", "seq"), None),
            P(("dp", "seq"), None),
            P(("dp", "seq"), None),
            P(("dp", "seq"), None),
            P(("dp", "seq"), None),
            P(("dp", "seq"), None),
            P(("dp", "seq"), None),
            P(("dp", "seq"), None),
            P(("dp", "seq"), None),
        ),
        check_vma=False,
    )
```

```python
import functools
import itertools
import math

import jax
import jax.numpy as jnp
from jax import lax
from jax.experimental import pallas as pl
from jax.experimental.pallas import tpu as pltpu
from jax.sharding import PartitionSpec as P

HEADS = 12
HEAD_DIM = 64


epsilon = 1e-05


TILE = 384
LANES = 128


def project(values, weight):
    flat_rows = values.reshape(-1, values.shape[-1])
    return jnp.dot(flat_rows, weight, preferred_element_type=jnp.float32).reshape(
        values.shape[:-1] + (weight.shape[1],)
    )


def project_back(values, weight):
    flat_rows = values.reshape(-1, values.shape[-1])
    result = lax.dot_general(
        flat_rows, weight, (((1,), (1,)), ((), ())), preferred_element_type=jnp.float32
    )
    return result.reshape(values.shape[:-1] + (weight.shape[0],))


def weight_grad(left_rows, right_rows):
    return lax.dot_general(
        left_rows.reshape(-1, left_rows.shape[-1]),
        right_rows.reshape(-1, right_rows.shape[-1]),
        (((0,), (0,)), ((), ())),
        preferred_element_type=jnp.float32,
    )


def layer_norm(values, gain, shift):
    centred = values - jnp.mean(values, axis=-1, keepdims=True)
    spread = jnp.mean(centred * centred, axis=-1, keepdims=True)
    inverse = lax.rsqrt(spread + epsilon)
    scaled = centred * inverse
    return (scaled * gain + shift, scaled, inverse)


def norm_back(grad_rows, scaled, inverse, gain):
    weighted = grad_rows * gain
    result = inverse * (
        weighted
        - jnp.mean(weighted, axis=-1, keepdims=True)
        - scaled * jnp.mean(weighted * scaled, axis=-1, keepdims=True)
    )
    flat_grad = grad_rows.reshape(-1, grad_rows.shape[-1])
    flat_scaled = scaled.reshape(-1, scaled.shape[-1])
    return (result, jnp.sum(flat_grad * flat_scaled, axis=0), jnp.sum(flat_grad, axis=0))


def dot(left, right, contract):
    return lax.dot_general(left, right, (contract, ((), ())), preferred_element_type=jnp.float32)


def ffn_body(rows_ref, grad_ref, expand_ref, reduce_ref, order_ref, out_ref, back_ref, rgrad_ref, egrad_ref, *, ratio):
    rows, grad = rows_ref[...], grad_ref[...]
    width = rows.shape[1]
    stacked = jnp.concatenate([reduce_ref[:, k * width : (k + 1) * width] for k in range(ratio)], axis=0)
    reduce = dot(order_ref[...], stacked, ((1,), (0,))).astype(jnp.bfloat16)
    expand = expand_ref[...]
    gate = dot(rows, expand, ((1,), (0,)))
    grad_hidden = dot(grad, reduce, ((1,), (1,)))
    share = 0.5 * (1.0 + lax.erf(gate * math.sqrt(0.5)))
    slope = share + gate * (jnp.exp(-0.5 * gate * gate) * (1.0 / math.sqrt(2.0 * math.pi)))
    hidden = (gate * share).astype(jnp.bfloat16)
    grad_gate = (grad_hidden * slope).astype(jnp.bfloat16)
    rgrad_ref[...] = dot(hidden, grad, ((0,), (0,))).astype(jnp.bfloat16)
    egrad_ref[...] = dot(rows, grad_gate, ((0,), (0,))).astype(jnp.bfloat16)
    first = pl.program_id(0) == 0
    @pl.when(first)
    def _():
        out_ref[...] = jnp.zeros_like(out_ref)
        back_ref[...] = jnp.zeros_like(back_ref)
    out_ref[...] += dot(hidden, reduce, ((1,), (0,)))
    back_ref[...] += dot(grad_gate, expand, ((1,), (1,)))


def ffn(rows, grad, others, per_device, hidden_width):
    count, width = rows.shape
    ratio = hidden_width // width
    part = TILE // ratio
    place = jnp.arange(TILE)
    chunk = per_device * ratio
    source = part * (place % chunk // per_device) + per_device * (place // chunk) + place % per_device
    order = (source[:, None] == place[None, :]).astype(jnp.bfloat16)
    whole = lambda shape: pl.BlockSpec(shape, lambda j: (0, 0))
    return pl.pallas_call(
        functools.partial(ffn_body, ratio=ratio),
        grid=(hidden_width // TILE,),
        in_specs=[
            whole((count, width)), whole((count, width)),
            pl.BlockSpec((width, TILE), lambda j: (0, hidden_width // TILE + j)),
            pl.BlockSpec((part, hidden_width), lambda j: (j, 0)),
            whole((TILE, TILE)),
        ],
        out_specs=[
            whole((count, width)), whole((count, width)),
            pl.BlockSpec((TILE, width), lambda j: (j, 0)),
            pl.BlockSpec((width, TILE), lambda j: (0, j)),
        ],
        out_shape=[
            jax.ShapeDtypeStruct((count, width), jnp.float32),
            jax.ShapeDtypeStruct((count, width), jnp.float32),
            jax.ShapeDtypeStruct((hidden_width, width), jnp.bfloat16),
            jax.ShapeDtypeStruct((width, hidden_width), jnp.bfloat16),
        ],
        compiler_params=pltpu.CompilerParams(dimension_semantics=("arbitrary",), vmem_limit_bytes=48 << 20),
        name="ffn",
    )(rows, grad, others, others, order)


def stack_heads(block):
    left = lax.broadcasted_iota(jnp.int32, block.shape, 1) < HEAD_DIM
    none = jnp.zeros_like(block)
    return jnp.concatenate([jnp.where(left, block, none), jnp.where(left, none, block)], axis=0)


def join_heads(stacked):
    count = stacked.shape[0] // 2
    left = lax.broadcasted_iota(jnp.int32, (count, LANES), 1) < HEAD_DIM
    return jnp.where(left, stacked[:count], stacked[count:])


def pair_probs(query, key, length):
    scores = dot(key, query, ((1,), (1,)))
    if length is not None:
        row = lax.broadcasted_iota(jnp.int32, scores.shape, 0)
        column = lax.broadcasted_iota(jnp.int32, scores.shape, 1) % (scores.shape[1] // 2)
        scores = jnp.where((row <= column) & (row < length), scores, -1e30)
    spread = jnp.exp(scores - jnp.max(scores, axis=0, keepdims=True))
    return spread * (1.0 / jnp.sum(spread, axis=0, keepdims=True))


def scaled(block):
    return block * jnp.asarray(1.0 / math.sqrt(HEAD_DIM), block.dtype)


def attend_body(table_ref, query_ref, key_ref, value_ref, out_ref, *, causal):
    length = table_ref[pl.program_id(0)] if causal else None
    for start in range(0, HEADS * HEAD_DIM, LANES):
        lanes = slice(start, start + LANES)
        query = stack_heads(scaled(query_ref[0, :, lanes]))
        probs = pair_probs(query, key_ref[0, :, lanes], length).astype(jnp.bfloat16)
        out_ref[0, :, lanes] = join_heads(dot(probs, value_ref[0, :, lanes], ((0,), (0,)))).astype(jnp.bfloat16)


def attend_back_body(table_ref, query_ref, key_ref, value_ref, grad_ref, query_grad_ref, pair_grad_ref, *, causal):
    length = table_ref[pl.program_id(0)] if causal else None
    width = HEADS * HEAD_DIM
    for start in range(0, width, LANES):
        lanes = slice(start, start + LANES)
        query = stack_heads(scaled(query_ref[0, :, lanes]))
        grad = stack_heads(grad_ref[0, :, lanes])
        key, value = key_ref[0, :, lanes], value_ref[0, :, lanes]
        probs = pair_probs(query, key, length)
        grad_probs = dot(value, grad, ((1,), (1,)))
        grad_scores = probs * (grad_probs - jnp.sum(grad_probs * probs, axis=0, keepdims=True))
        grad_scores = grad_scores.astype(jnp.bfloat16)
        back = lambda left, right: dot(left, right, ((1,), (0,))).astype(jnp.bfloat16)
        grad_query = scaled(join_heads(dot(grad_scores, key, ((0,), (0,))))).astype(jnp.bfloat16)
        grad_key, grad_value = back(grad_scores, query), back(probs.astype(jnp.bfloat16), grad)
        query_grad_ref[0, :, lanes] = grad_query
        if causal:
            query_grad_ref[0, :, slice(width + start, width + start + LANES)] = grad_key
            query_grad_ref[0, :, slice(2 * width + start, 2 * width + start + LANES)] = grad_value
        else:
            pair_grad_ref[0, :, lanes] = grad_key
            pair_grad_ref[0, :, slice(width + start, width + start + LANES)] = grad_value


def attention(body, table, arrays, outs, name, heavy, routed=False):
    width = HEADS * HEAD_DIM
    captions = arrays[0][0].shape[0]
    own = arrays[0][0].shape[1]

    def spec(rows, cols, at):
        if routed and rows != own:
            return pl.BlockSpec((1, rows, cols), lambda c, place: (place[c], 0, at))
        return pl.BlockSpec((1, rows, cols), lambda c, place: (c, 0, at))

    work = heavy * 2 * captions * arrays[0][0].shape[1] * arrays[1][0].shape[1] * width
    return pl.pallas_call(
        body,
        grid_spec=pltpu.PrefetchScalarGridSpec(
            num_scalar_prefetch=1,
            grid=(captions,),
            in_specs=[spec(array.shape[1], width, at) for array, at in arrays],
            out_specs=[spec(rows, cols, 0) for rows, cols in outs],
        ),
        out_shape=[jax.ShapeDtypeStruct((captions, rows, cols), jnp.bfloat16) for rows, cols in outs],
        compiler_params=pltpu.CompilerParams(dimension_semantics=("arbitrary",), vmem_limit_bytes=48 << 20),
        cost_estimate=pl.CostEstimate(flops=work, transcendentals=0, bytes_accessed=0),
        name=name,
    )(table, *(array for array, _ in arrays))


def self_forward(packed, lengths):
    rows, width = packed.shape[1], HEADS * HEAD_DIM
    return attention(functools.partial(attend_body, causal=True), lengths,
        [(packed, 0), (packed, 1), (packed, 2)], [(rows, width)], "self_attention", 2)[0]


def cross_forward(query_rows, pair, place):
    return attention(functools.partial(attend_body, causal=False), place,
        [(query_rows, 0), (pair, 0), (pair, 1)], [query_rows.shape[1:]], "cross_attention", 2, True)[0]


def self_body(*refs):
    attend_back_body(*refs, None, causal=True)


def self_backward(packed, grad_rows, lengths):
    return attention(self_body, lengths,
        [(packed, 0), (packed, 1), (packed, 2), (grad_rows, 0)], [packed.shape[1:]], "self_backward", 5)[0]


def cross_backward(query_rows, pair, grad_rows, place):
    return attention(functools.partial(attend_back_body, causal=False), place,
        [(query_rows, 0), (pair, 0), (pair, 1), (grad_rows, 0)],
        [query_rows.shape[1:], pair.shape[1:]], "cross_backward", 5, True)


def index_bits():
    found = []
    for axis in ("dp", "seq"):
        count = lax.axis_size(axis)
        found += [(axis, bit) for bit in reversed(range(count.bit_length() - 1))]
    return found


def swap_pairs(axis, bit):
    return [(i, i ^ (1 << bit)) for i in range(lax.axis_size(axis))]


def own_bit(axis, bit):
    return (lax.axis_index(axis) >> bit) & 1


def gather_order(flip):
    far = [("dp", bit) for bit in range(1, lax.axis_size("dp").bit_length() - 1)][::-1]
    near = [[("dp", 0)], [("seq", bit) for bit in range(1, lax.axis_size("seq").bit_length() - 1)]]
    if flip:
        near = near[::-1]
    return far + near[0] + near[1] + [("seq", 0)]


class Gather:
    def __init__(self, part, flip):
        bits = index_bits()
        self.own = [own_bit(*place) for place in bits]
        self.known = [1] * len(bits)
        self.shape = part.shape
        self.piece = part.reshape((1,) * len(bits) + part.shape)
        self.whole = jnp.zeros((2,) * len(bits) + part.shape, part.dtype)
        self.whole = self.put(self.piece, self.own)
        self.left = gather_order(flip)

    def put(self, piece, starts):
        return lax.dynamic_update_slice(self.whole, piece, starts + [0] * len(self.shape))

    def starts(self):
        return [0 if size == 2 else bit for size, bit in zip(self.known, self.own)]

    def step(self):
        place = self.left.pop(0)
        dim = index_bits().index(place)
        starts = self.starts()
        if self.piece is None:
            self.piece = lax.dynamic_slice(
                self.whole, starts + [0] * len(self.shape), self.known + list(self.shape)
            )
        other = lax.ppermute(self.piece, place[0], swap_pairs(*place))
        starts[dim] = 1 - self.own[dim]
        self.whole = self.put(other, starts)
        self.known[dim] = 2
        self.piece = None

    def rows(self):
        return self.whole.reshape((-1,) + self.shape[1:])


class Scatter:
    def __init__(self, whole, flip, span):
        bits = index_bits()
        self.rows = whole.shape[0] >> len(bits)
        self.tail = whole.shape[1:]
        self.state = whole.reshape((2,) * len(bits) + (self.rows,) + self.tail)
        order = gather_order(flip)
        far = [place for place in order[:-3]][::-1]
        pairs = [far[i : i + span] for i in range(0, len(far), span)]
        self.left = [[order[-1]], [order[-2]], [order[-3]]] + pairs

    def part(self, places, turn):
        part = self.state
        for place, flipped in zip(places, turn):
            dim = index_bits().index(place)
            part = lax.dynamic_slice_in_dim(part, own_bit(*place) ^ flipped, 1, dim)
        return part

    def step(self):
        places = self.left.pop(0)
        axis = places[0][0]
        total = self.part(places, [0] * len(places))
        for turn in list(itertools.product((0, 1), repeat=len(places)))[1:]:
            mask = sum(flipped << place[1] for place, flipped in zip(places, turn))
            pairs = [(i, i ^ mask) for i in range(lax.axis_size(axis))]
            total = total + lax.ppermute(self.part(places, turn), axis, pairs)
        self.state = total

    def join(self, other):
        self.state = jnp.concatenate([self.state, other.state], axis=-1)
        self.tail = self.state.shape[-1:]

    def finish(self):
        while self.left:
            self.step()
        return self.state.reshape((self.rows,) + self.tail).astype(jnp.float32)


def advance(scatters, *values):
    held = lax.optimization_barrier(tuple(one.state for one in scatters) + values)
    for one, state in zip(scatters, held):
        one.state = state
        if one.left:
            one.step()
    values = held[len(scatters) :]
    return values[0] if len(values) == 1 else values


def swap(rows, k):
    if not k:
        return rows
    return lax.ppermute(rows, "seq", [(i, i ^ k) for i in range(lax.axis_size("seq"))])


def lay_body(*refs):
    start = 0
    for ref in refs[:-1]:
        refs[-1][:, start : start + ref.shape[1]] = ref[...]
        start += ref.shape[1]


def lay_side_by_side(pieces):
    width = sum(piece.shape[1] for piece in pieces)
    return pl.pallas_call(
        lay_body,
        out_shape=jax.ShapeDtypeStruct((pieces[0].shape[0], width), pieces[0].dtype),
        name="lay_side_by_side",
    )(*pieces)


def put_body(table_ref, *refs):
    for k, ref in enumerate(refs[:-1]):

        @pl.when(pl.program_id(0) == k)
        def _():
            refs[-1][...] = ref[...]


def put_rows(pieces, table):
    shape = pieces[0].shape
    return pl.pallas_call(
        put_body,
        grid_spec=pltpu.PrefetchScalarGridSpec(
            num_scalar_prefetch=1,
            grid=(len(pieces),),
            in_specs=[pl.BlockSpec(shape, lambda k, at: (0, 0, 0)) for _ in pieces],
            out_specs=pl.BlockSpec(shape, lambda k, at: (at[k], 0, 0)),
        ),
        out_shape=jax.ShapeDtypeStruct((len(pieces),) + shape[1:], pieces[0].dtype),
        compiler_params=pltpu.CompilerParams(dimension_semantics=("arbitrary",)),
        cost_estimate=pl.CostEstimate(
            flops=0, transcendentals=0, bytes_accessed=4 * len(pieces) * shape[1] * shape[2]
        ),
        name="put_rows",
    )(table, *pieces)


def shards(
    caption_tokens,
    image_tokens,
    caption_lengths,
    caption_image,
    norm_gain,
    norm_bias,
    self_packed,
    self_output,
    cross_query,
    cross_pair,
    cross_output,
    expand_weight,
    reduce_weight,
    cotangent,
):
    captions, seq_len, model_width = caption_tokens.shape
    peer_count = lax.axis_size("seq")
    position = lax.axis_index("seq")

    owner = (caption_image // captions % peer_count).reshape(peer_count, captions)
    slot = (caption_image % captions).reshape(peer_count, captions)
    peers = jnp.arange(peer_count)
    mine = (peers == position).astype(jnp.int32)
    place = jnp.sum(owner * mine[:, None], axis=0) ^ position
    asked = jnp.sum(jnp.where(owner == position, slot, 0), axis=1)
    turned = (peers[:, None] ^ position) == peers[None, :]
    asked = jnp.sum(jnp.where(turned, asked[None, :], 0), axis=1)
    paired = jnp.concatenate(
        [
            swap(lax.dynamic_slice_in_dim(image_tokens, asked[k], 1), k)
            for k in range(peer_count)
        ]
    )

    norm_columns = jnp.pad(jnp.concatenate([norm_gain, norm_bias], axis=1), ((0, 0), (0, 122)))
    rows = self_packed.shape[0]
    ratio = reduce_weight.shape[0] // rows
    reduce_blocks = [reduce_weight[k * rows : (k + 1) * rows] for k in range(ratio)]
    wide = lax.all_gather(
        lay_side_by_side(
            reduce_blocks + [expand_weight, cross_pair, self_output, cross_query, cross_output]
        ),
        ("dp", "seq"),
        axis=0,
        tiled=True,
    )
    first_group = Gather(jnp.concatenate([self_packed, norm_columns], axis=1), False)
    while first_group.left:
        first_group.step()
    first_group = first_group.rows()
    packed_weight = first_group[:, : 3 * model_width]
    norm_values = first_group[:, 3 * model_width : 3 * model_width + 6].astype(jnp.float32)
    norm_gains, norm_shifts = norm_values[:, :3], norm_values[:, 3:]
    hidden_width = expand_weight.shape[1]
    narrower = wide[:, 2 * hidden_width :]
    pair_weight = narrower[:, : 2 * model_width]
    output_weight = narrower[:, 2 * model_width : 3 * model_width]
    query_weight = narrower[:, 3 * model_width : 4 * model_width]
    cross_weight = narrower[:, 4 * model_width :]

    live_rows = jnp.arange(seq_len)[None, :] < caption_lengths[:, None]
    inputs = caption_tokens.astype(jnp.float32)
    normed_full, scaled_one, inverse_one = layer_norm(inputs, norm_gains[:, 0], norm_shifts[:, 0])
    normed_one = normed_full.astype(jnp.bfloat16)
    packed = project(normed_one, packed_weight).astype(jnp.bfloat16)
    attended = self_forward(packed, caption_lengths)
    after_self = inputs + project(attended, output_weight)
    normed_full_two, scaled_two, inverse_two = layer_norm(
        after_self, norm_gains[:, 1], norm_shifts[:, 1]
    )
    normed_two = normed_full_two.astype(jnp.bfloat16)
    image_pair = project(paired, pair_weight).astype(jnp.bfloat16)
    query_rows = project(normed_two, query_weight).astype(jnp.bfloat16)
    mixed_rows = cross_forward(query_rows, image_pair, place)
    branch = project(mixed_rows, cross_weight).astype(jnp.bfloat16)
    after_cross = after_self + branch.astype(jnp.float32)
    normed_full_three, scaled_three, inverse_three = layer_norm(
        after_cross, norm_gains[:, 2], norm_shifts[:, 2]
    )
    normed_three = normed_full_three.astype(jnp.bfloat16)
    grad_out = jnp.where(live_rows[..., None], cotangent, jnp.zeros_like(cotangent))
    flat = lambda member: member.reshape(-1, model_width)
    forward, backward, reduce_part, expand_part = ffn(
        flat(normed_three), flat(grad_out), wide, rows, hidden_width
    )
    caption_out = jnp.where(
        live_rows[..., None], after_cross + forward.reshape(after_cross.shape), 0.0
    ).astype(jnp.bfloat16)

    narrow = lambda member: member.astype(jnp.bfloat16)
    reduce_sums = Scatter(reduce_part, True, 1)
    expand_sums = Scatter(expand_part, False, 1)
    reduce_sums.step()
    expand_sums.step()
    grad_norm_three, gain_three, shift_three = norm_back(
        backward.reshape(after_cross.shape), scaled_three, inverse_three, norm_gains[:, 2]
    )
    grad_second = grad_out.astype(jnp.float32) + grad_norm_three
    grad_branch = grad_second.astype(jnp.bfloat16)
    grad_cross_mixed = project_back(grad_branch, cross_weight).astype(jnp.bfloat16)
    grad_cross_mixed, grad_branch = advance(
        [reduce_sums, expand_sums], grad_cross_mixed, grad_branch
    )
    cross_output_grad = weight_grad(mixed_rows, grad_branch)
    grad_cross_rows, grad_pair = cross_backward(
        query_rows, image_pair, grad_cross_mixed, place
    )
    cross_pair_grad = weight_grad(paired, grad_pair)
    cross_sums = Scatter(
        narrow(jnp.concatenate([cross_pair_grad, cross_output_grad], axis=1)), True, 2
    )
    grad_pair, grad_cross_rows = advance(
        [reduce_sums, expand_sums, cross_sums], grad_pair, grad_cross_rows
    )
    image_rows = project_back(grad_pair, pair_weight).astype(jnp.bfloat16)
    cross_query_grad = weight_grad(normed_two, grad_cross_rows)
    grad_norm_two, gain_two, shift_two = norm_back(
        project_back(grad_cross_rows, query_weight).astype(jnp.bfloat16).astype(jnp.float32),
        scaled_two,
        inverse_two,
        norm_gains[:, 1],
    )
    grad_first = grad_second + grad_norm_two
    grad_self = grad_first.astype(jnp.bfloat16)
    self_output_grad = weight_grad(attended, grad_self)
    grad_self, image_rows = advance([reduce_sums, expand_sums, cross_sums], grad_self, image_rows)
    home = [swap(image_rows[k : k + 1], k) for k in range(peer_count)]
    grad_attended = project_back(grad_self, output_weight).astype(jnp.bfloat16)
    grad_packed = self_backward(packed, grad_attended, caption_lengths)
    grad_packed, *home = advance([reduce_sums, expand_sums, cross_sums], grad_packed, *home)
    self_packed_grad = weight_grad(normed_one, grad_packed)
    grad_norm_one, gain_one, shift_one = norm_back(
        project_back(grad_packed, packed_weight), scaled_one, inverse_one, norm_gains[:, 0]
    )
    caption_grad = (grad_first + grad_norm_one).astype(jnp.bfloat16)
    norm_sums = jnp.stack([gain_one, gain_two, gain_three, shift_one, shift_two, shift_three], axis=1)
    half = model_width // 2
    left = jnp.concatenate([cross_query_grad, self_output_grad, self_packed_grad[:, :half]], axis=1)
    right = jnp.concatenate(
        [self_packed_grad[:, half:], jnp.pad(norm_sums, ((0, 0), (0, 122)))], axis=1
    )
    left_sums = Scatter(narrow(left), True, 2)
    right_sums = Scatter(narrow(right), False, 2)
    left_sums.step()
    right_sums.step()
    groups = [cross_sums, reduce_sums, expand_sums, left_sums, right_sums]
    while len(left_sums.left) > 1:
        advance(groups)
    left_sums.join(right_sums)
    home = advance([left_sums], *home)
    image_grad = put_rows(list(home), asked)
    self_sums = left_sums.finish()
    reduce_grad, expand_grad = reduce_sums.finish(), expand_sums.finish()
    cross_sums = cross_sums.finish()
    last = 5 * model_width
    return (
        caption_out,
        caption_grad,
        image_grad,
        self_sums[:, last : last + 3],
        self_sums[:, last + 3 : last + 6],
        self_sums[:, 2 * model_width : last],
        self_sums[:, model_width : 2 * model_width],
        self_sums[:, :model_width],
        cross_sums[:, : 2 * model_width],
        cross_sums[:, 2 * model_width :],
        expand_grad,
        reduce_grad,
    )


def solution(mesh):
    placed = (
        P(("dp", "seq"), None, None),
        P(("dp", "seq"), None, None),
        P(("dp", "seq")),
        P("dp"),
        P(("dp", "seq"), None),
        P(("dp", "seq"), None),
        P(("dp", "seq"), None),
        P(("dp", "seq"), None),
        P(("dp", "seq"), None),
        P(("dp", "seq"), None),
        P(("dp", "seq"), None),
        P(("dp", "seq"), None),
        P(("dp", "seq"), None),
        P(("dp", "seq"), None, None),
    )
    return jax.shard_map(
        shards,
        mesh=mesh,
        in_specs=placed,
        out_specs=(
            P(("dp", "seq"), None, None),
            P(("dp", "seq"), None, None),
            P(("dp", "seq"), None, None),
            P(("dp", "seq"), None),
            P(("dp", "seq"), None),
            P(("dp", "seq"), None),
            P(("dp", "seq"), None),
            P(("dp", "seq"), None),
            P(("dp", "seq"), None),
            P(("dp", "seq"), None),
            P(("dp", "seq"), None),
            P(("dp", "seq"), None),
        ),
        check_vma=False,
    )
```

```python
import functools
import itertools
import math

import jax
import jax.numpy as jnp
from jax import lax
from jax.experimental import pallas as pl
from jax.experimental.pallas import tpu as pltpu
from jax.sharding import PartitionSpec as P

HEADS = 12
HEAD_DIM = 64


epsilon = 1e-05


TILE = 384
LANES = 128


def project(values, weight):
    flat_rows = values.reshape(-1, values.shape[-1])
    return jnp.dot(flat_rows, weight, preferred_element_type=jnp.float32).reshape(
        values.shape[:-1] + (weight.shape[1],)
    )


def project_back(values, weight):
    flat_rows = values.reshape(-1, values.shape[-1])
    result = lax.dot_general(
        flat_rows, weight, (((1,), (1,)), ((), ())), preferred_element_type=jnp.float32
    )
    return result.reshape(values.shape[:-1] + (weight.shape[0],))


def weight_grad(left_rows, right_rows):
    return lax.dot_general(
        left_rows.reshape(-1, left_rows.shape[-1]),
        right_rows.reshape(-1, right_rows.shape[-1]),
        (((0,), (0,)), ((), ())),
        preferred_element_type=jnp.float32,
    )


def layer_norm(values, gain, shift):
    centred = values - jnp.mean(values, axis=-1, keepdims=True)
    spread = jnp.mean(centred * centred, axis=-1, keepdims=True)
    inverse = lax.rsqrt(spread + epsilon)
    scaled = centred * inverse
    return (scaled * gain + shift, scaled, inverse)


def norm_back(grad_rows, scaled, inverse, gain):
    weighted = grad_rows * gain
    result = inverse * (
        weighted
        - jnp.mean(weighted, axis=-1, keepdims=True)
        - scaled * jnp.mean(weighted * scaled, axis=-1, keepdims=True)
    )
    flat_grad = grad_rows.reshape(-1, grad_rows.shape[-1])
    flat_scaled = scaled.reshape(-1, scaled.shape[-1])
    return (result, jnp.sum(flat_grad * flat_scaled, axis=0), jnp.sum(flat_grad, axis=0))


def dot(left, right, contract):
    return lax.dot_general(left, right, (contract, ((), ())), preferred_element_type=jnp.float32)


def ffn_body(rows_ref, grad_ref, expand_ref, reduce_ref, order_ref, out_ref, back_ref, rgrad_ref, egrad_ref, *, ratio):
    rows, grad = rows_ref[...], grad_ref[...]
    width = rows.shape[1]
    stacked = jnp.concatenate([reduce_ref[:, k * width : (k + 1) * width] for k in range(ratio)], axis=0)
    reduce = dot(order_ref[...], stacked, ((1,), (0,))).astype(jnp.bfloat16)
    expand = expand_ref[...]
    gate = dot(rows, expand, ((1,), (0,)))
    grad_hidden = dot(grad, reduce, ((1,), (1,)))
    share = 0.5 * (1.0 + lax.erf(gate * math.sqrt(0.5)))
    slope = share + gate * (jnp.exp(-0.5 * gate * gate) * (1.0 / math.sqrt(2.0 * math.pi)))
    hidden = (gate * share).astype(jnp.bfloat16)
    grad_gate = (grad_hidden * slope).astype(jnp.bfloat16)
    rgrad_ref[...] = dot(hidden, grad, ((0,), (0,))).astype(jnp.bfloat16)
    egrad_ref[...] = dot(rows, grad_gate, ((0,), (0,))).astype(jnp.bfloat16)
    first = pl.program_id(0) == 0
    @pl.when(first)
    def _():
        out_ref[...] = jnp.zeros_like(out_ref)
        back_ref[...] = jnp.zeros_like(back_ref)
    out_ref[...] += dot(hidden, reduce, ((1,), (0,)))
    back_ref[...] += dot(grad_gate, expand, ((1,), (1,)))


def ffn(rows, grad, others, per_device, hidden_width):
    count, width = rows.shape
    ratio = hidden_width // width
    part = TILE // ratio
    place = jnp.arange(TILE)
    chunk = per_device * ratio
    source = part * (place % chunk // per_device) + per_device * (place // chunk) + place % per_device
    order = (source[:, None] == place[None, :]).astype(jnp.bfloat16)
    whole = lambda shape: pl.BlockSpec(shape, lambda j: (0, 0))
    return pl.pallas_call(
        functools.partial(ffn_body, ratio=ratio),
        grid=(hidden_width // TILE,),
        in_specs=[
            whole((count, width)), whole((count, width)),
            pl.BlockSpec((width, TILE), lambda j: (0, hidden_width // TILE + j)),
            pl.BlockSpec((part, hidden_width), lambda j: (j, 0)),
            whole((TILE, TILE)),
        ],
        out_specs=[
            whole((count, width)), whole((count, width)),
            pl.BlockSpec((TILE, width), lambda j: (j, 0)),
            pl.BlockSpec((width, TILE), lambda j: (0, j)),
        ],
        out_shape=[
            jax.ShapeDtypeStruct((count, width), jnp.float32),
            jax.ShapeDtypeStruct((count, width), jnp.float32),
            jax.ShapeDtypeStruct((hidden_width, width), jnp.bfloat16),
            jax.ShapeDtypeStruct((width, hidden_width), jnp.bfloat16),
        ],
        compiler_params=pltpu.CompilerParams(dimension_semantics=("arbitrary",), vmem_limit_bytes=48 << 20),
        name="ffn",
    )(rows, grad, others, others, order)


def stack_heads(block):
    left = lax.broadcasted_iota(jnp.int32, block.shape, 1) < HEAD_DIM
    none = jnp.zeros_like(block)
    return jnp.concatenate([jnp.where(left, block, none), jnp.where(left, none, block)], axis=0)


def join_heads(stacked):
    count = stacked.shape[0] // 2
    left = lax.broadcasted_iota(jnp.int32, (count, LANES), 1) < HEAD_DIM
    return jnp.where(left, stacked[:count], stacked[count:])


def pair_probs(query, key, length):
    scores = dot(key, query, ((1,), (1,)))
    if length is not None:
        row = lax.broadcasted_iota(jnp.int32, scores.shape, 0)
        column = lax.broadcasted_iota(jnp.int32, scores.shape, 1) % (scores.shape[1] // 2)
        scores = jnp.where((row <= column) & (row < length), scores, -1e30)
    spread = jnp.exp(scores - jnp.max(scores, axis=0, keepdims=True))
    return spread * (1.0 / jnp.sum(spread, axis=0, keepdims=True))


def scaled(block):
    return block * jnp.asarray(1.0 / math.sqrt(HEAD_DIM), block.dtype)


def attend_body(table_ref, query_ref, key_ref, value_ref, out_ref, *, causal):
    length = table_ref[pl.program_id(0)] if causal else None
    for start in range(0, HEADS * HEAD_DIM, LANES):
        lanes = slice(start, start + LANES)
        query = stack_heads(scaled(query_ref[0, :, lanes]))
        probs = pair_probs(query, key_ref[0, :, lanes], length).astype(jnp.bfloat16)
        out_ref[0, :, lanes] = join_heads(dot(probs, value_ref[0, :, lanes], ((0,), (0,)))).astype(jnp.bfloat16)


def attend_back_body(table_ref, query_ref, key_ref, value_ref, grad_ref, query_grad_ref, pair_grad_ref, *, causal):
    length = table_ref[pl.program_id(0)] if causal else None
    width = HEADS * HEAD_DIM
    for start in range(0, width, LANES):
        lanes = slice(start, start + LANES)
        query = stack_heads(scaled(query_ref[0, :, lanes]))
        grad = stack_heads(grad_ref[0, :, lanes])
        key, value = key_ref[0, :, lanes], value_ref[0, :, lanes]
        probs = pair_probs(query, key, length)
        grad_probs = dot(value, grad, ((1,), (1,)))
        grad_scores = probs * (grad_probs - jnp.sum(grad_probs * probs, axis=0, keepdims=True))
        grad_scores = grad_scores.astype(jnp.bfloat16)
        back = lambda left, right: dot(left, right, ((1,), (0,))).astype(jnp.bfloat16)
        grad_query = scaled(join_heads(dot(grad_scores, key, ((0,), (0,))))).astype(jnp.bfloat16)
        grad_key, grad_value = back(grad_scores, query), back(probs.astype(jnp.bfloat16), grad)
        query_grad_ref[0, :, lanes] = grad_query
        if causal:
            query_grad_ref[0, :, slice(width + start, width + start + LANES)] = grad_key
            query_grad_ref[0, :, slice(2 * width + start, 2 * width + start + LANES)] = grad_value
        else:
            pair_grad_ref[0, :, lanes] = grad_key
            pair_grad_ref[0, :, slice(width + start, width + start + LANES)] = grad_value


def attention(body, table, arrays, outs, name, heavy, routed=False):
    width = HEADS * HEAD_DIM
    captions = arrays[0][0].shape[0]
    own = arrays[0][0].shape[1]

    def spec(rows, cols, at):
        if routed and rows != own:
            return pl.BlockSpec((1, rows, cols), lambda c, place: (place[c], 0, at))
        return pl.BlockSpec((1, rows, cols), lambda c, place: (c, 0, at))

    work = heavy * 2 * captions * arrays[0][0].shape[1] * arrays[1][0].shape[1] * width
    return pl.pallas_call(
        body,
        grid_spec=pltpu.PrefetchScalarGridSpec(
            num_scalar_prefetch=1,
            grid=(captions,),
            in_specs=[spec(array.shape[1], width, at) for array, at in arrays],
            out_specs=[spec(rows, cols, 0) for rows, cols in outs],
        ),
        out_shape=[jax.ShapeDtypeStruct((captions, rows, cols), jnp.bfloat16) for rows, cols in outs],
        compiler_params=pltpu.CompilerParams(dimension_semantics=("arbitrary",), vmem_limit_bytes=48 << 20),
        cost_estimate=pl.CostEstimate(flops=work, transcendentals=0, bytes_accessed=0),
        name=name,
    )(table, *(array for array, _ in arrays))


def self_forward(packed, lengths):
    rows, width = packed.shape[1], HEADS * HEAD_DIM
    return attention(functools.partial(attend_body, causal=True), lengths,
        [(packed, 0), (packed, 1), (packed, 2)], [(rows, width)], "self_attention", 2)[0]


def cross_forward(query_rows, pair, place):
    return attention(functools.partial(attend_body, causal=False), place,
        [(query_rows, 0), (pair, 0), (pair, 1)], [query_rows.shape[1:]], "cross_attention", 2, True)[0]


def self_body(*refs):
    attend_back_body(*refs, None, causal=True)


def self_backward(packed, grad_rows, lengths):
    return attention(self_body, lengths,
        [(packed, 0), (packed, 1), (packed, 2), (grad_rows, 0)], [packed.shape[1:]], "self_backward", 5)[0]


def cross_backward(query_rows, pair, grad_rows, place):
    return attention(functools.partial(attend_back_body, causal=False), place,
        [(query_rows, 0), (pair, 0), (pair, 1), (grad_rows, 0)],
        [query_rows.shape[1:], pair.shape[1:]], "cross_backward", 5, True)


def index_bits():
    found = []
    for axis in ("dp", "seq"):
        count = lax.axis_size(axis)
        found += [(axis, bit) for bit in reversed(range(count.bit_length() - 1))]
    return found


def swap_pairs(axis, bit):
    return [(i, i ^ (1 << bit)) for i in range(lax.axis_size(axis))]


def own_bit(axis, bit):
    return (lax.axis_index(axis) >> bit) & 1


def gather_order(flip):
    far = [("dp", bit) for bit in range(1, lax.axis_size("dp").bit_length() - 1)][::-1]
    near = [[("dp", 0)], [("seq", bit) for bit in range(1, lax.axis_size("seq").bit_length() - 1)]]
    if flip:
        near = near[::-1]
    return far + near[0] + near[1] + [("seq", 0)]


class Gather:
    def __init__(self, part, flip):
        bits = index_bits()
        self.own = [own_bit(*place) for place in bits]
        self.known = [1] * len(bits)
        self.shape = part.shape
        self.piece = part.reshape((1,) * len(bits) + part.shape)
        self.whole = jnp.zeros((2,) * len(bits) + part.shape, part.dtype)
        self.whole = self.put(self.piece, self.own)
        self.left = gather_order(flip)

    def put(self, piece, starts):
        return lax.dynamic_update_slice(self.whole, piece, starts + [0] * len(self.shape))

    def starts(self):
        return [0 if size == 2 else bit for size, bit in zip(self.known, self.own)]

    def step(self):
        place = self.left.pop(0)
        dim = index_bits().index(place)
        starts = self.starts()
        if self.piece is None:
            self.piece = lax.dynamic_slice(
                self.whole, starts + [0] * len(self.shape), self.known + list(self.shape)
            )
        other = lax.ppermute(self.piece, place[0], swap_pairs(*place))
        starts[dim] = 1 - self.own[dim]
        self.whole = self.put(other, starts)
        self.known[dim] = 2
        self.piece = None

    def rows(self):
        return self.whole.reshape((-1,) + self.shape[1:])


class Scatter:
    def __init__(self, whole, flip, span):
        bits = index_bits()
        self.rows = whole.shape[0] >> len(bits)
        self.tail = whole.shape[1:]
        self.state = whole.reshape((2,) * len(bits) + (self.rows,) + self.tail)
        order = gather_order(flip)
        far = [place for place in order[:-3]][::-1]
        pairs = [far[i : i + span] for i in range(0, len(far), span)]
        self.left = [[order[-1]], [order[-2]], [order[-3]]] + pairs

    def part(self, places, turn):
        part = self.state
        for place, flipped in zip(places, turn):
            dim = index_bits().index(place)
            part = lax.dynamic_slice_in_dim(part, own_bit(*place) ^ flipped, 1, dim)
        return part

    def step(self):
        places = self.left.pop(0)
        axis = places[0][0]
        total = self.part(places, [0] * len(places))
        for turn in list(itertools.product((0, 1), repeat=len(places)))[1:]:
            mask = sum(flipped << place[1] for place, flipped in zip(places, turn))
            pairs = [(i, i ^ mask) for i in range(lax.axis_size(axis))]
            total = total + lax.ppermute(self.part(places, turn), axis, pairs)
        self.state = total

    def join(self, other):
        self.state = jnp.concatenate([self.state, other.state], axis=-1)
        self.tail = self.state.shape[-1:]

    def finish(self):
        while self.left:
            self.step()
        return self.state.reshape((self.rows,) + self.tail).astype(jnp.float32)


def advance(scatters, *values):
    held = lax.optimization_barrier(tuple(one.state for one in scatters) + values)
    for one, state in zip(scatters, held):
        one.state = state
        if one.left:
            one.step()
    values = held[len(scatters) :]
    return values[0] if len(values) == 1 else values


def swap(rows, k):
    if not k:
        return rows
    return lax.ppermute(rows, "seq", [(i, i ^ k) for i in range(lax.axis_size("seq"))])


def lay_body(*refs):
    start = 0
    for ref in refs[:-1]:
        refs[-1][:, start : start + ref.shape[1]] = ref[...]
        start += ref.shape[1]


def lay_side_by_side(pieces):
    width = sum(piece.shape[1] for piece in pieces)
    return pl.pallas_call(
        lay_body,
        out_shape=jax.ShapeDtypeStruct((pieces[0].shape[0], width), pieces[0].dtype),
        name="lay_side_by_side",
    )(*pieces)


def put_body(table_ref, *refs):
    for k, ref in enumerate(refs[:-1]):

        @pl.when(pl.program_id(0) == k)
        def _():
            refs[-1][...] = ref[...]


def put_rows(pieces, table):
    shape = pieces[0].shape
    return pl.pallas_call(
        put_body,
        grid_spec=pltpu.PrefetchScalarGridSpec(
            num_scalar_prefetch=1,
            grid=(len(pieces),),
            in_specs=[pl.BlockSpec(shape, lambda k, at: (0, 0, 0)) for _ in pieces],
            out_specs=pl.BlockSpec(shape, lambda k, at: (at[k], 0, 0)),
        ),
        out_shape=jax.ShapeDtypeStruct((len(pieces),) + shape[1:], pieces[0].dtype),
        compiler_params=pltpu.CompilerParams(dimension_semantics=("arbitrary",)),
        cost_estimate=pl.CostEstimate(
            flops=0, transcendentals=0, bytes_accessed=4 * len(pieces) * shape[1] * shape[2]
        ),
        name="put_rows",
    )(table, *pieces)


def shards(
    caption_tokens,
    image_tokens,
    caption_lengths,
    caption_image,
    norm_gain,
    norm_bias,
    self_packed,
    self_output,
    cross_query,
    cross_pair,
    cross_output,
    expand_weight,
    reduce_weight,
    cotangent,
):
    captions, seq_len, model_width = caption_tokens.shape
    peer_count = lax.axis_size("seq")
    position = lax.axis_index("seq")

    owner = (caption_image // captions % peer_count).reshape(peer_count, captions)
    slot = (caption_image % captions).reshape(peer_count, captions)
    peers = jnp.arange(peer_count)
    mine = (peers == position).astype(jnp.int32)
    place = jnp.sum(owner * mine[:, None], axis=0) ^ position
    asked = jnp.sum(jnp.where(owner == position, slot, 0), axis=1)
    turned = (peers[:, None] ^ position) == peers[None, :]
    asked = jnp.sum(jnp.where(turned, asked[None, :], 0), axis=1)
    paired = jnp.concatenate(
        [
            swap(lax.dynamic_slice_in_dim(image_tokens, asked[k], 1), k)
            for k in range(peer_count)
        ]
    )

    norm_columns = jnp.pad(jnp.concatenate([norm_gain, norm_bias], axis=1), ((0, 0), (0, 122)))
    rows = self_packed.shape[0]
    ratio = reduce_weight.shape[0] // rows
    reduce_blocks = [reduce_weight[k * rows : (k + 1) * rows] for k in range(ratio)]
    wide = lax.all_gather(
        lay_side_by_side(
            reduce_blocks + [expand_weight, cross_pair, cross_query, cross_output]
        ),
        ("dp", "seq"),
        axis=0,
        tiled=True,
    )
    first_group = Gather(
        jnp.concatenate([self_packed, self_output, norm_columns], axis=1), False
    )
    while first_group.left:
        first_group.step()
    first_group = first_group.rows()
    packed_weight = first_group[:, : 3 * model_width]
    output_weight = first_group[:, 3 * model_width : 4 * model_width]
    norm_values = first_group[:, 4 * model_width : 4 * model_width + 6].astype(jnp.float32)
    norm_gains, norm_shifts = norm_values[:, :3], norm_values[:, 3:]
    hidden_width = expand_weight.shape[1]
    narrower = wide[:, 2 * hidden_width :]
    pair_weight = narrower[:, : 2 * model_width]
    query_weight = narrower[:, 2 * model_width : 3 * model_width]
    cross_weight = narrower[:, 3 * model_width :]

    live_rows = jnp.arange(seq_len)[None, :] < caption_lengths[:, None]
    inputs = caption_tokens.astype(jnp.float32)
    normed_full, scaled_one, inverse_one = layer_norm(inputs, norm_gains[:, 0], norm_shifts[:, 0])
    normed_one = normed_full.astype(jnp.bfloat16)
    packed = project(normed_one, packed_weight).astype(jnp.bfloat16)
    attended = self_forward(packed, caption_lengths)
    after_self = inputs + project(attended, output_weight)
    normed_full_two, scaled_two, inverse_two = layer_norm(
        after_self, norm_gains[:, 1], norm_shifts[:, 1]
    )
    normed_two = normed_full_two.astype(jnp.bfloat16)
    image_pair = project(paired, pair_weight).astype(jnp.bfloat16)
    query_rows = project(normed_two, query_weight).astype(jnp.bfloat16)
    mixed_rows = cross_forward(query_rows, image_pair, place)
    branch = project(mixed_rows, cross_weight).astype(jnp.bfloat16)
    after_cross = after_self + branch.astype(jnp.float32)
    normed_full_three, scaled_three, inverse_three = layer_norm(
        after_cross, norm_gains[:, 2], norm_shifts[:, 2]
    )
    normed_three = normed_full_three.astype(jnp.bfloat16)
    grad_out = jnp.where(live_rows[..., None], cotangent, jnp.zeros_like(cotangent))
    flat = lambda member: member.reshape(-1, model_width)
    forward, backward, reduce_part, expand_part = ffn(
        flat(normed_three), flat(grad_out), wide, rows, hidden_width
    )
    caption_out = jnp.where(
        live_rows[..., None], after_cross + forward.reshape(after_cross.shape), 0.0
    ).astype(jnp.bfloat16)

    narrow = lambda member: member.astype(jnp.bfloat16)
    reduce_sums = Scatter(reduce_part, True, 1)
    expand_sums = Scatter(expand_part, False, 1)
    reduce_sums.step()
    expand_sums.step()
    grad_norm_three, gain_three, shift_three = norm_back(
        backward.reshape(after_cross.shape), scaled_three, inverse_three, norm_gains[:, 2]
    )
    grad_second = grad_out.astype(jnp.float32) + grad_norm_three
    grad_branch = grad_second.astype(jnp.bfloat16)
    grad_cross_mixed = project_back(grad_branch, cross_weight).astype(jnp.bfloat16)
    grad_cross_mixed, grad_branch = advance(
        [reduce_sums, expand_sums], grad_cross_mixed, grad_branch
    )
    cross_output_grad = weight_grad(mixed_rows, grad_branch)
    grad_cross_rows, grad_pair = cross_backward(
        query_rows, image_pair, grad_cross_mixed, place
    )
    cross_pair_grad = weight_grad(paired, grad_pair)
    cross_sums = Scatter(
        narrow(jnp.concatenate([cross_pair_grad, cross_output_grad], axis=1)), True, 2
    )
    image_rows = project_back(grad_pair, pair_weight).astype(jnp.bfloat16)
    image_rows, grad_cross_rows = advance(
        [reduce_sums, expand_sums, cross_sums], image_rows, grad_cross_rows
    )
    cross_query_grad = weight_grad(normed_two, grad_cross_rows)
    grad_norm_two, gain_two, shift_two = norm_back(
        project_back(grad_cross_rows, query_weight).astype(jnp.bfloat16).astype(jnp.float32),
        scaled_two,
        inverse_two,
        norm_gains[:, 1],
    )
    grad_first = grad_second + grad_norm_two
    grad_self = grad_first.astype(jnp.bfloat16)
    self_output_grad = weight_grad(attended, grad_self)
    grad_self, image_rows = advance([reduce_sums, expand_sums, cross_sums], grad_self, image_rows)
    home = [swap(image_rows[k : k + 1], k) for k in range(peer_count)]
    grad_attended = project_back(grad_self, output_weight).astype(jnp.bfloat16)
    grad_packed = self_backward(packed, grad_attended, caption_lengths)
    grad_packed, *home = advance([reduce_sums, expand_sums, cross_sums], grad_packed, *home)
    self_packed_grad = weight_grad(normed_one, grad_packed)
    grad_norm_one, gain_one, shift_one = norm_back(
        project_back(grad_packed, packed_weight), scaled_one, inverse_one, norm_gains[:, 0]
    )
    caption_grad = (grad_first + grad_norm_one).astype(jnp.bfloat16)
    norm_sums = jnp.stack([gain_one, gain_two, gain_three, shift_one, shift_two, shift_three], axis=1)
    half = model_width // 2
    left = jnp.concatenate([cross_query_grad, self_output_grad, self_packed_grad[:, :half]], axis=1)
    right = jnp.concatenate(
        [self_packed_grad[:, half:], jnp.pad(norm_sums, ((0, 0), (0, 122)))], axis=1
    )
    left_sums = Scatter(narrow(left), True, 2)
    right_sums = Scatter(narrow(right), False, 2)
    left_sums.step()
    right_sums.step()
    groups = [cross_sums, reduce_sums, expand_sums, left_sums, right_sums]
    while len(left_sums.left) > 1:
        advance(groups)
    left_sums.join(right_sums)
    home = advance([left_sums], *home)
    image_grad = put_rows(list(home), asked)
    self_sums = left_sums.finish()
    reduce_grad, expand_grad = reduce_sums.finish(), expand_sums.finish()
    cross_sums = cross_sums.finish()
    last = 5 * model_width
    return (
        caption_out,
        caption_grad,
        image_grad,
        self_sums[:, last : last + 3],
        self_sums[:, last + 3 : last + 6],
        self_sums[:, 2 * model_width : last],
        self_sums[:, model_width : 2 * model_width],
        self_sums[:, :model_width],
        cross_sums[:, : 2 * model_width],
        cross_sums[:, 2 * model_width :],
        expand_grad,
        reduce_grad,
    )


def solution(mesh):
    placed = (
        P(("dp", "seq"), None, None),
        P(("dp", "seq"), None, None),
        P(("dp", "seq")),
        P("dp"),
        P(("dp", "seq"), None),
        P(("dp", "seq"), None),
        P(("dp", "seq"), None),
        P(("dp", "seq"), None),
        P(("dp", "seq"), None),
        P(("dp", "seq"), None),
        P(("dp", "seq"), None),
        P(("dp", "seq"), None),
        P(("dp", "seq"), None),
        P(("dp", "seq"), None, None),
    )
    return jax.shard_map(
        shards,
        mesh=mesh,
        in_specs=placed,
        out_specs=(
            P(("dp", "seq"), None, None),
            P(("dp", "seq"), None, None),
            P(("dp", "seq"), None, None),
            P(("dp", "seq"), None),
            P(("dp", "seq"), None),
            P(("dp", "seq"), None),
            P(("dp", "seq"), None),
            P(("dp", "seq"), None),
            P(("dp", "seq"), None),
            P(("dp", "seq"), None),
            P(("dp", "seq"), None),
            P(("dp", "seq"), None),
        ),
        check_vma=False,
    )
```

```python
import functools
import itertools
import math

import jax
import jax.numpy as jnp
from jax import lax
from jax.experimental import pallas as pl
from jax.experimental.pallas import tpu as pltpu
from jax.sharding import PartitionSpec as P

HEADS = 12
HEAD_DIM = 64


epsilon = 1e-05


TILE = 384
LANES = 128


def project(values, weight):
    flat_rows = values.reshape(-1, values.shape[-1])
    return jnp.dot(flat_rows, weight, preferred_element_type=jnp.float32).reshape(
        values.shape[:-1] + (weight.shape[1],)
    )


def project_back(values, weight):
    flat_rows = values.reshape(-1, values.shape[-1])
    result = lax.dot_general(
        flat_rows, weight, (((1,), (1,)), ((), ())), preferred_element_type=jnp.float32
    )
    return result.reshape(values.shape[:-1] + (weight.shape[0],))


def weight_grad(left_rows, right_rows):
    return lax.dot_general(
        left_rows.reshape(-1, left_rows.shape[-1]),
        right_rows.reshape(-1, right_rows.shape[-1]),
        (((0,), (0,)), ((), ())),
        preferred_element_type=jnp.float32,
    )


def layer_norm(values, gain, shift):
    centred = values - jnp.mean(values, axis=-1, keepdims=True)
    spread = jnp.mean(centred * centred, axis=-1, keepdims=True)
    inverse = lax.rsqrt(spread + epsilon)
    scaled = centred * inverse
    return (scaled * gain + shift, scaled, inverse)


def norm_back(grad_rows, scaled, inverse, gain):
    weighted = grad_rows * gain
    result = inverse * (
        weighted
        - jnp.mean(weighted, axis=-1, keepdims=True)
        - scaled * jnp.mean(weighted * scaled, axis=-1, keepdims=True)
    )
    flat_grad = grad_rows.reshape(-1, grad_rows.shape[-1])
    flat_scaled = scaled.reshape(-1, scaled.shape[-1])
    return (result, jnp.sum(flat_grad * flat_scaled, axis=0), jnp.sum(flat_grad, axis=0))


def dot(left, right, contract):
    return lax.dot_general(left, right, (contract, ((), ())), preferred_element_type=jnp.float32)


def ffn_body(rows_ref, grad_ref, expand_ref, reduce_ref, order_ref, out_ref, back_ref, rgrad_ref, egrad_ref, *, ratio):
    rows, grad = rows_ref[...], grad_ref[...]
    width = rows.shape[1]
    stacked = jnp.concatenate([reduce_ref[:, k * width : (k + 1) * width] for k in range(ratio)], axis=0)
    reduce = dot(order_ref[...], stacked, ((1,), (0,))).astype(jnp.bfloat16)
    expand = expand_ref[...]
    gate = dot(rows, expand, ((1,), (0,)))
    grad_hidden = dot(grad, reduce, ((1,), (1,)))
    share = 0.5 * (1.0 + lax.erf(gate * math.sqrt(0.5)))
    slope = share + gate * (jnp.exp(-0.5 * gate * gate) * (1.0 / math.sqrt(2.0 * math.pi)))
    hidden = (gate * share).astype(jnp.bfloat16)
    grad_gate = (grad_hidden * slope).astype(jnp.bfloat16)
    rgrad_ref[...] = dot(hidden, grad, ((0,), (0,))).astype(jnp.bfloat16)
    egrad_ref[...] = dot(rows, grad_gate, ((0,), (0,))).astype(jnp.bfloat16)
    first = pl.program_id(0) == 0
    @pl.when(first)
    def _():
        out_ref[...] = jnp.zeros_like(out_ref)
        back_ref[...] = jnp.zeros_like(back_ref)
    out_ref[...] += dot(hidden, reduce, ((1,), (0,)))
    back_ref[...] += dot(grad_gate, expand, ((1,), (1,)))


def ffn(rows, grad, others, per_device, hidden_width):
    count, width = rows.shape
    ratio = hidden_width // width
    part = TILE // ratio
    place = jnp.arange(TILE)
    chunk = per_device * ratio
    source = part * (place % chunk // per_device) + per_device * (place // chunk) + place % per_device
    order = (source[:, None] == place[None, :]).astype(jnp.bfloat16)
    whole = lambda shape: pl.BlockSpec(shape, lambda j: (0, 0))
    return pl.pallas_call(
        functools.partial(ffn_body, ratio=ratio),
        grid=(hidden_width // TILE,),
        in_specs=[
            whole((count, width)), whole((count, width)),
            pl.BlockSpec((width, TILE), lambda j: (0, hidden_width // TILE + j)),
            pl.BlockSpec((part, hidden_width), lambda j: (j, 0)),
            whole((TILE, TILE)),
        ],
        out_specs=[
            whole((count, width)), whole((count, width)),
            pl.BlockSpec((TILE, width), lambda j: (j, 0)),
            pl.BlockSpec((width, TILE), lambda j: (0, j)),
        ],
        out_shape=[
            jax.ShapeDtypeStruct((count, width), jnp.float32),
            jax.ShapeDtypeStruct((count, width), jnp.float32),
            jax.ShapeDtypeStruct((hidden_width, width), jnp.bfloat16),
            jax.ShapeDtypeStruct((width, hidden_width), jnp.bfloat16),
        ],
        compiler_params=pltpu.CompilerParams(dimension_semantics=("arbitrary",), vmem_limit_bytes=48 << 20),
        name="ffn",
    )(rows, grad, others, others, order)


def stack_heads(block):
    left = lax.broadcasted_iota(jnp.int32, block.shape, 1) < HEAD_DIM
    none = jnp.zeros_like(block)
    return jnp.concatenate([jnp.where(left, block, none), jnp.where(left, none, block)], axis=0)


def join_heads(stacked):
    count = stacked.shape[0] // 2
    left = lax.broadcasted_iota(jnp.int32, (count, LANES), 1) < HEAD_DIM
    return jnp.where(left, stacked[:count], stacked[count:])


def pair_probs(query, key, length):
    scores = dot(key, query, ((1,), (1,)))
    if length is not None:
        row = lax.broadcasted_iota(jnp.int32, scores.shape, 0)
        column = lax.broadcasted_iota(jnp.int32, scores.shape, 1) % (scores.shape[1] // 2)
        scores = jnp.where((row <= column) & (row < length), scores, -1e30)
    spread = jnp.exp(scores - jnp.max(scores, axis=0, keepdims=True))
    return spread * (1.0 / jnp.sum(spread, axis=0, keepdims=True))


def scaled(block):
    return block * jnp.asarray(1.0 / math.sqrt(HEAD_DIM), block.dtype)


def attend_body(table_ref, query_ref, key_ref, value_ref, out_ref, *, causal):
    length = table_ref[pl.program_id(0)] if causal else None
    for start in range(0, HEADS * HEAD_DIM, LANES):
        lanes = slice(start, start + LANES)
        query = stack_heads(scaled(query_ref[0, :, lanes]))
        probs = pair_probs(query, key_ref[0, :, lanes], length).astype(jnp.bfloat16)
        out_ref[0, :, lanes] = join_heads(dot(probs, value_ref[0, :, lanes], ((0,), (0,)))).astype(jnp.bfloat16)


def attend_back_body(table_ref, query_ref, key_ref, value_ref, grad_ref, query_grad_ref, pair_grad_ref, *, causal):
    length = table_ref[pl.program_id(0)] if causal else None
    width = HEADS * HEAD_DIM
    for start in range(0, width, LANES):
        lanes = slice(start, start + LANES)
        query = stack_heads(scaled(query_ref[0, :, lanes]))
        grad = stack_heads(grad_ref[0, :, lanes])
        key, value = key_ref[0, :, lanes], value_ref[0, :, lanes]
        probs = pair_probs(query, key, length)
        grad_probs = dot(value, grad, ((1,), (1,)))
        grad_scores = probs * (grad_probs - jnp.sum(grad_probs * probs, axis=0, keepdims=True))
        grad_scores = grad_scores.astype(jnp.bfloat16)
        back = lambda left, right: dot(left, right, ((1,), (0,))).astype(jnp.bfloat16)
        grad_query = scaled(join_heads(dot(grad_scores, key, ((0,), (0,))))).astype(jnp.bfloat16)
        grad_key, grad_value = back(grad_scores, query), back(probs.astype(jnp.bfloat16), grad)
        query_grad_ref[0, :, lanes] = grad_query
        if causal:
            query_grad_ref[0, :, slice(width + start, width + start + LANES)] = grad_key
            query_grad_ref[0, :, slice(2 * width + start, 2 * width + start + LANES)] = grad_value
        else:
            pair_grad_ref[0, :, lanes] = grad_key
            pair_grad_ref[0, :, slice(width + start, width + start + LANES)] = grad_value


def attention(body, table, arrays, outs, name, heavy, routed=False):
    width = HEADS * HEAD_DIM
    captions = arrays[0][0].shape[0]
    own = arrays[0][0].shape[1]

    def spec(rows, cols, at):
        if routed and rows != own:
            return pl.BlockSpec((1, rows, cols), lambda c, place: (place[c], 0, at))
        return pl.BlockSpec((1, rows, cols), lambda c, place: (c, 0, at))

    work = heavy * 2 * captions * arrays[0][0].shape[1] * arrays[1][0].shape[1] * width
    return pl.pallas_call(
        body,
        grid_spec=pltpu.PrefetchScalarGridSpec(
            num_scalar_prefetch=1,
            grid=(captions,),
            in_specs=[spec(array.shape[1], width, at) for array, at in arrays],
            out_specs=[spec(rows, cols, 0) for rows, cols in outs],
        ),
        out_shape=[jax.ShapeDtypeStruct((captions, rows, cols), jnp.bfloat16) for rows, cols in outs],
        compiler_params=pltpu.CompilerParams(dimension_semantics=("arbitrary",), vmem_limit_bytes=48 << 20),
        cost_estimate=pl.CostEstimate(flops=work, transcendentals=0, bytes_accessed=0),
        name=name,
    )(table, *(array for array, _ in arrays))


def self_forward(packed, lengths):
    rows, width = packed.shape[1], HEADS * HEAD_DIM
    return attention(functools.partial(attend_body, causal=True), lengths,
        [(packed, 0), (packed, 1), (packed, 2)], [(rows, width)], "self_attention", 2)[0]


def cross_forward(query_rows, pair, place):
    return attention(functools.partial(attend_body, causal=False), place,
        [(query_rows, 0), (pair, 0), (pair, 1)], [query_rows.shape[1:]], "cross_attention", 2, True)[0]


def self_body(*refs):
    attend_back_body(*refs, None, causal=True)


def self_backward(packed, grad_rows, lengths):
    return attention(self_body, lengths,
        [(packed, 0), (packed, 1), (packed, 2), (grad_rows, 0)], [packed.shape[1:]], "self_backward", 5)[0]


def cross_backward(query_rows, pair, grad_rows, place):
    return attention(functools.partial(attend_back_body, causal=False), place,
        [(query_rows, 0), (pair, 0), (pair, 1), (grad_rows, 0)],
        [query_rows.shape[1:], pair.shape[1:]], "cross_backward", 5, True)


def index_bits():
    found = []
    for axis in ("dp", "seq"):
        count = lax.axis_size(axis)
        found += [(axis, bit) for bit in reversed(range(count.bit_length() - 1))]
    return found


def swap_pairs(axis, bit):
    return [(i, i ^ (1 << bit)) for i in range(lax.axis_size(axis))]


def own_bit(axis, bit):
    return (lax.axis_index(axis) >> bit) & 1


def gather_order(flip):
    far = [("dp", bit) for bit in range(1, lax.axis_size("dp").bit_length() - 1)][::-1]
    near = [[("dp", 0)], [("seq", bit) for bit in range(1, lax.axis_size("seq").bit_length() - 1)]]
    if flip:
        near = near[::-1]
    return far + near[0] + near[1] + [("seq", 0)]


class Gather:
    def __init__(self, part, flip):
        bits = index_bits()
        self.own = [own_bit(*place) for place in bits]
        self.known = [1] * len(bits)
        self.shape = part.shape
        self.piece = part.reshape((1,) * len(bits) + part.shape)
        self.whole = jnp.zeros((2,) * len(bits) + part.shape, part.dtype)
        self.whole = self.put(self.piece, self.own)
        self.left = gather_order(flip)

    def put(self, piece, starts):
        return lax.dynamic_update_slice(self.whole, piece, starts + [0] * len(self.shape))

    def starts(self):
        return [0 if size == 2 else bit for size, bit in zip(self.known, self.own)]

    def step(self):
        place = self.left.pop(0)
        dim = index_bits().index(place)
        starts = self.starts()
        if self.piece is None:
            self.piece = lax.dynamic_slice(
                self.whole, starts + [0] * len(self.shape), self.known + list(self.shape)
            )
        other = lax.ppermute(self.piece, place[0], swap_pairs(*place))
        starts[dim] = 1 - self.own[dim]
        self.whole = self.put(other, starts)
        self.known[dim] = 2
        self.piece = None
        return other

    def rows(self):
        return self.whole.reshape((-1,) + self.shape[1:])


class Scatter:
    def __init__(self, whole, flip, span):
        bits = index_bits()
        self.rows = whole.shape[0] >> len(bits)
        self.tail = whole.shape[1:]
        self.state = whole.reshape((2,) * len(bits) + (self.rows,) + self.tail)
        order = gather_order(flip)
        far = [place for place in order[:-3]][::-1]
        pairs = [far[i : i + span] for i in range(0, len(far), span)]
        self.left = [[order[-1]], [order[-2]], [order[-3]]] + pairs

    def part(self, places, turn):
        part = self.state
        for place, flipped in zip(places, turn):
            dim = index_bits().index(place)
            part = lax.dynamic_slice_in_dim(part, own_bit(*place) ^ flipped, 1, dim)
        return part

    def step(self):
        places = self.left.pop(0)
        axis = places[0][0]
        total = self.part(places, [0] * len(places))
        for turn in list(itertools.product((0, 1), repeat=len(places)))[1:]:
            mask = sum(flipped << place[1] for place, flipped in zip(places, turn))
            pairs = [(i, i ^ mask) for i in range(lax.axis_size(axis))]
            total = total + lax.ppermute(self.part(places, turn), axis, pairs)
        self.state = total

    def join(self, other):
        self.state = jnp.concatenate([self.state, other.state], axis=-1)
        self.tail = self.state.shape[-1:]

    def finish(self):
        while self.left:
            self.step()
        return self.state.reshape((self.rows,) + self.tail).astype(jnp.float32)


def advance(scatters, *values):
    held = lax.optimization_barrier(tuple(one.state for one in scatters) + values)
    for one, state in zip(scatters, held):
        one.state = state
        if one.left:
            one.step()
    values = held[len(scatters) :]
    return values[0] if len(values) == 1 else values


def swap(rows, k):
    if not k:
        return rows
    return lax.ppermute(rows, "seq", [(i, i ^ k) for i in range(lax.axis_size("seq"))])


def lay_body(*refs):
    start = 0
    for ref in refs[:-1]:
        refs[-1][:, start : start + ref.shape[1]] = ref[...]
        start += ref.shape[1]


def lay_side_by_side(pieces):
    width = sum(piece.shape[1] for piece in pieces)
    return pl.pallas_call(
        lay_body,
        out_shape=jax.ShapeDtypeStruct((pieces[0].shape[0], width), pieces[0].dtype),
        name="lay_side_by_side",
    )(*pieces)


def put_body(table_ref, *refs):
    for k, ref in enumerate(refs[:-1]):

        @pl.when(pl.program_id(0) == k)
        def _():
            refs[-1][...] = ref[...]


def put_rows(pieces, table):
    shape = pieces[0].shape
    return pl.pallas_call(
        put_body,
        grid_spec=pltpu.PrefetchScalarGridSpec(
            num_scalar_prefetch=1,
            grid=(len(pieces),),
            in_specs=[pl.BlockSpec(shape, lambda k, at: (0, 0, 0)) for _ in pieces],
            out_specs=pl.BlockSpec(shape, lambda k, at: (at[k], 0, 0)),
        ),
        out_shape=jax.ShapeDtypeStruct((len(pieces),) + shape[1:], pieces[0].dtype),
        compiler_params=pltpu.CompilerParams(dimension_semantics=("arbitrary",)),
        cost_estimate=pl.CostEstimate(
            flops=0, transcendentals=0, bytes_accessed=4 * len(pieces) * shape[1] * shape[2]
        ),
        name="put_rows",
    )(table, *pieces)


def shards(
    caption_tokens,
    image_tokens,
    caption_lengths,
    caption_image,
    norm_gain,
    norm_bias,
    self_packed,
    self_output,
    cross_query,
    cross_pair,
    cross_output,
    expand_weight,
    reduce_weight,
    cotangent,
):
    captions, seq_len, model_width = caption_tokens.shape
    peer_count = lax.axis_size("seq")
    position = lax.axis_index("seq")

    owner = (caption_image // captions % peer_count).reshape(peer_count, captions)
    slot = (caption_image % captions).reshape(peer_count, captions)
    peers = jnp.arange(peer_count)
    mine = (peers == position).astype(jnp.int32)
    place = jnp.sum(owner * mine[:, None], axis=0) ^ position
    asked = jnp.sum(jnp.where(owner == position, slot, 0), axis=1)
    turned = (peers[:, None] ^ position) == peers[None, :]
    asked = jnp.sum(jnp.where(turned, asked[None, :], 0), axis=1)
    norm_columns = jnp.pad(jnp.concatenate([norm_gain, norm_bias], axis=1), ((0, 0), (0, 122)))
    rows = self_packed.shape[0]
    ratio = reduce_weight.shape[0] // rows
    reduce_blocks = [reduce_weight[k * rows : (k + 1) * rows] for k in range(ratio)]
    wide = lax.all_gather(
        lay_side_by_side(
            reduce_blocks + [expand_weight, cross_pair, cross_query, cross_output]
        ),
        ("dp", "seq"),
        axis=0,
        tiled=True,
    )
    first_group = Gather(
        jnp.concatenate([self_packed, self_output, norm_columns], axis=1), False
    )
    while len(first_group.left) > 1:
        came = first_group.step()
    wanted = [lax.dynamic_slice_in_dim(image_tokens, asked[k], 1) for k in range(peer_count)]
    wanted = lax.optimization_barrier((*wanted, came))[:-1]
    paired = [swap(row, k) for k, row in enumerate(wanted)]
    first_group.step()
    first_group = first_group.rows()
    packed_weight = first_group[:, : 3 * model_width]
    output_weight = first_group[:, 3 * model_width : 4 * model_width]
    norm_values = first_group[:, 4 * model_width : 4 * model_width + 6].astype(jnp.float32)
    norm_gains, norm_shifts = norm_values[:, :3], norm_values[:, 3:]
    hidden_width = expand_weight.shape[1]
    narrower = wide[:, 2 * hidden_width :]
    pair_weight = narrower[:, : 2 * model_width]
    query_weight = narrower[:, 2 * model_width : 3 * model_width]
    cross_weight = narrower[:, 3 * model_width :]

    live_rows = jnp.arange(seq_len)[None, :] < caption_lengths[:, None]
    inputs = caption_tokens.astype(jnp.float32)
    normed_full, scaled_one, inverse_one = layer_norm(inputs, norm_gains[:, 0], norm_shifts[:, 0])
    normed_one = normed_full.astype(jnp.bfloat16)
    packed = project(normed_one, packed_weight).astype(jnp.bfloat16)
    attended = self_forward(packed, caption_lengths)
    *paired, attended = lax.optimization_barrier((*paired, attended))
    paired = jnp.concatenate(paired)
    after_self = inputs + project(attended, output_weight)
    normed_full_two, scaled_two, inverse_two = layer_norm(
        after_self, norm_gains[:, 1], norm_shifts[:, 1]
    )
    normed_two = normed_full_two.astype(jnp.bfloat16)
    image_pair = project(paired, pair_weight).astype(jnp.bfloat16)
    query_rows = project(normed_two, query_weight).astype(jnp.bfloat16)
    mixed_rows = cross_forward(query_rows, image_pair, place)
    branch = project(mixed_rows, cross_weight).astype(jnp.bfloat16)
    after_cross = after_self + branch.astype(jnp.float32)
    normed_full_three, scaled_three, inverse_three = layer_norm(
        after_cross, norm_gains[:, 2], norm_shifts[:, 2]
    )
    normed_three = normed_full_three.astype(jnp.bfloat16)
    grad_out = jnp.where(live_rows[..., None], cotangent, jnp.zeros_like(cotangent))
    flat = lambda member: member.reshape(-1, model_width)
    forward, backward, reduce_part, expand_part = ffn(
        flat(normed_three), flat(grad_out), wide, rows, hidden_width
    )
    caption_out = jnp.where(
        live_rows[..., None], after_cross + forward.reshape(after_cross.shape), 0.0
    ).astype(jnp.bfloat16)

    narrow = lambda member: member.astype(jnp.bfloat16)
    reduce_sums = Scatter(reduce_part, True, 1)
    expand_sums = Scatter(expand_part, False, 1)
    reduce_sums.step()
    expand_sums.step()
    grad_norm_three, gain_three, shift_three = norm_back(
        backward.reshape(after_cross.shape), scaled_three, inverse_three, norm_gains[:, 2]
    )
    grad_second = grad_out.astype(jnp.float32) + grad_norm_three
    grad_branch = grad_second.astype(jnp.bfloat16)
    grad_cross_mixed = project_back(grad_branch, cross_weight).astype(jnp.bfloat16)
    grad_cross_mixed, grad_branch = advance(
        [reduce_sums, expand_sums], grad_cross_mixed, grad_branch
    )
    cross_output_grad = weight_grad(mixed_rows, grad_branch)
    grad_cross_rows, grad_pair = cross_backward(
        query_rows, image_pair, grad_cross_mixed, place
    )
    cross_pair_grad = weight_grad(paired, grad_pair)
    cross_sums = Scatter(
        narrow(jnp.concatenate([cross_pair_grad, cross_output_grad], axis=1)), True, 2
    )
    image_rows = project_back(grad_pair, pair_weight).astype(jnp.bfloat16)
    image_rows, grad_cross_rows = advance(
        [reduce_sums, expand_sums, cross_sums], image_rows, grad_cross_rows
    )
    cross_query_grad = weight_grad(normed_two, grad_cross_rows)
    grad_norm_two, gain_two, shift_two = norm_back(
        project_back(grad_cross_rows, query_weight).astype(jnp.bfloat16).astype(jnp.float32),
        scaled_two,
        inverse_two,
        norm_gains[:, 1],
    )
    grad_first = grad_second + grad_norm_two
    grad_self = grad_first.astype(jnp.bfloat16)
    self_output_grad = weight_grad(attended, grad_self)
    grad_self, image_rows = advance([reduce_sums, expand_sums, cross_sums], grad_self, image_rows)
    home = [swap(image_rows[k : k + 1], k) for k in range(peer_count)]
    grad_attended = project_back(grad_self, output_weight).astype(jnp.bfloat16)
    grad_packed = self_backward(packed, grad_attended, caption_lengths)
    grad_packed, *home = advance([reduce_sums, expand_sums, cross_sums], grad_packed, *home)
    self_packed_grad = weight_grad(normed_one, grad_packed)
    grad_norm_one, gain_one, shift_one = norm_back(
        project_back(grad_packed, packed_weight), scaled_one, inverse_one, norm_gains[:, 0]
    )
    caption_grad = (grad_first + grad_norm_one).astype(jnp.bfloat16)
    norm_sums = jnp.stack([gain_one, gain_two, gain_three, shift_one, shift_two, shift_three], axis=1)
    half = model_width // 2
    left = jnp.concatenate([cross_query_grad, self_output_grad, self_packed_grad[:, :half]], axis=1)
    right = jnp.concatenate(
        [self_packed_grad[:, half:], jnp.pad(norm_sums, ((0, 0), (0, 122)))], axis=1
    )
    left_sums = Scatter(narrow(left), True, 2)
    right_sums = Scatter(narrow(right), False, 2)
    left_sums.step()
    right_sums.step()
    groups = [cross_sums, reduce_sums, expand_sums, left_sums, right_sums]
    while len(left_sums.left) > 1:
        advance(groups)
    left_sums.join(right_sums)
    home = advance([left_sums], *home)
    image_grad = put_rows(list(home), asked)
    self_sums = left_sums.finish()
    reduce_grad, expand_grad = reduce_sums.finish(), expand_sums.finish()
    cross_sums = cross_sums.finish()
    last = 5 * model_width
    return (
        caption_out,
        caption_grad,
        image_grad,
        self_sums[:, last : last + 3],
        self_sums[:, last + 3 : last + 6],
        self_sums[:, 2 * model_width : last],
        self_sums[:, model_width : 2 * model_width],
        self_sums[:, :model_width],
        cross_sums[:, : 2 * model_width],
        cross_sums[:, 2 * model_width :],
        expand_grad,
        reduce_grad,
    )


def solution(mesh):
    placed = (
        P(("dp", "seq"), None, None),
        P(("dp", "seq"), None, None),
        P(("dp", "seq")),
        P("dp"),
        P(("dp", "seq"), None),
        P(("dp", "seq"), None),
        P(("dp", "seq"), None),
        P(("dp", "seq"), None),
        P(("dp", "seq"), None),
        P(("dp", "seq"), None),
        P(("dp", "seq"), None),
        P(("dp", "seq"), None),
        P(("dp", "seq"), None),
        P(("dp", "seq"), None, None),
    )
    return jax.shard_map(
        shards,
        mesh=mesh,
        in_specs=placed,
        out_specs=(
            P(("dp", "seq"), None, None),
            P(("dp", "seq"), None, None),
            P(("dp", "seq"), None, None),
            P(("dp", "seq"), None),
            P(("dp", "seq"), None),
            P(("dp", "seq"), None),
            P(("dp", "seq"), None),
            P(("dp", "seq"), None),
            P(("dp", "seq"), None),
            P(("dp", "seq"), None),
            P(("dp", "seq"), None),
            P(("dp", "seq"), None),
        ),
        check_vma=False,
    )
```

```python
import functools
import itertools
import math

import jax
import jax.numpy as jnp
from jax import lax
from jax.experimental import pallas as pl
from jax.experimental.pallas import tpu as pltpu
from jax.sharding import PartitionSpec as P

HEADS = 12
HEAD_DIM = 64


epsilon = 1e-05


TILE = 384
LANES = 128


def project(values, weight):
    flat_rows = values.reshape(-1, values.shape[-1])
    return jnp.dot(flat_rows, weight, preferred_element_type=jnp.float32).reshape(
        values.shape[:-1] + (weight.shape[1],)
    )


def project_back(values, weight):
    flat_rows = values.reshape(-1, values.shape[-1])
    result = lax.dot_general(
        flat_rows, weight, (((1,), (1,)), ((), ())), preferred_element_type=jnp.float32
    )
    return result.reshape(values.shape[:-1] + (weight.shape[0],))


def weight_grad(left_rows, right_rows):
    return lax.dot_general(
        left_rows.reshape(-1, left_rows.shape[-1]),
        right_rows.reshape(-1, right_rows.shape[-1]),
        (((0,), (0,)), ((), ())),
        preferred_element_type=jnp.float32,
    )


def layer_norm(values, gain, shift):
    centred = values - jnp.mean(values, axis=-1, keepdims=True)
    spread = jnp.mean(centred * centred, axis=-1, keepdims=True)
    inverse = lax.rsqrt(spread + epsilon)
    scaled = centred * inverse
    return (scaled * gain + shift, scaled, inverse)


def norm_back(grad_rows, scaled, inverse, gain):
    weighted = grad_rows * gain
    result = inverse * (
        weighted
        - jnp.mean(weighted, axis=-1, keepdims=True)
        - scaled * jnp.mean(weighted * scaled, axis=-1, keepdims=True)
    )
    flat_grad = grad_rows.reshape(-1, grad_rows.shape[-1])
    flat_scaled = scaled.reshape(-1, scaled.shape[-1])
    return (result, jnp.sum(flat_grad * flat_scaled, axis=0), jnp.sum(flat_grad, axis=0))


def dot(left, right, contract):
    return lax.dot_general(left, right, (contract, ((), ())), preferred_element_type=jnp.float32)


def ffn_body(rows_ref, grad_ref, expand_ref, reduce_ref, order_ref, out_ref, back_ref, rgrad_ref, egrad_ref, *, ratio):
    rows, grad = rows_ref[...], grad_ref[...]
    width = rows.shape[1]
    stacked = jnp.concatenate([reduce_ref[:, k * width : (k + 1) * width] for k in range(ratio)], axis=0)
    reduce = dot(order_ref[...], stacked, ((1,), (0,))).astype(jnp.bfloat16)
    expand = expand_ref[...]
    gate = dot(rows, expand, ((1,), (0,)))
    grad_hidden = dot(grad, reduce, ((1,), (1,)))
    share = 0.5 * (1.0 + lax.erf(gate * math.sqrt(0.5)))
    slope = share + gate * (jnp.exp(-0.5 * gate * gate) * (1.0 / math.sqrt(2.0 * math.pi)))
    hidden = (gate * share).astype(jnp.bfloat16)
    grad_gate = (grad_hidden * slope).astype(jnp.bfloat16)
    rgrad_ref[...] = dot(hidden, grad, ((0,), (0,))).astype(jnp.bfloat16)
    egrad_ref[...] = dot(rows, grad_gate, ((0,), (0,))).astype(jnp.bfloat16)
    first = pl.program_id(0) == 0
    @pl.when(first)
    def _():
        out_ref[...] = jnp.zeros_like(out_ref)
        back_ref[...] = jnp.zeros_like(back_ref)
    out_ref[...] += dot(hidden, reduce, ((1,), (0,)))
    back_ref[...] += dot(grad_gate, expand, ((1,), (1,)))


def ffn(rows, grad, others, per_device, hidden_width):
    count, width = rows.shape
    ratio = hidden_width // width
    part = TILE // ratio
    place = jnp.arange(TILE)
    chunk = per_device * ratio
    source = part * (place % chunk // per_device) + per_device * (place // chunk) + place % per_device
    order = (source[:, None] == place[None, :]).astype(jnp.bfloat16)
    whole = lambda shape: pl.BlockSpec(shape, lambda j: (0, 0))
    return pl.pallas_call(
        functools.partial(ffn_body, ratio=ratio),
        grid=(hidden_width // TILE,),
        in_specs=[
            whole((count, width)), whole((count, width)),
            pl.BlockSpec((width, TILE), lambda j: (0, hidden_width // TILE + j)),
            pl.BlockSpec((part, hidden_width), lambda j: (j, 0)),
            whole((TILE, TILE)),
        ],
        out_specs=[
            whole((count, width)), whole((count, width)),
            pl.BlockSpec((TILE, width), lambda j: (j, 0)),
            pl.BlockSpec((width, TILE), lambda j: (0, j)),
        ],
        out_shape=[
            jax.ShapeDtypeStruct((count, width), jnp.float32),
            jax.ShapeDtypeStruct((count, width), jnp.float32),
            jax.ShapeDtypeStruct((hidden_width, width), jnp.bfloat16),
            jax.ShapeDtypeStruct((width, hidden_width), jnp.bfloat16),
        ],
        compiler_params=pltpu.CompilerParams(dimension_semantics=("arbitrary",), vmem_limit_bytes=48 << 20),
        name="ffn",
    )(rows, grad, others, others, order)


def stack_heads(block):
    left = lax.broadcasted_iota(jnp.int32, block.shape, 1) < HEAD_DIM
    none = jnp.zeros_like(block)
    return jnp.concatenate([jnp.where(left, block, none), jnp.where(left, none, block)], axis=0)


def join_heads(stacked):
    count = stacked.shape[0] // 2
    left = lax.broadcasted_iota(jnp.int32, (count, LANES), 1) < HEAD_DIM
    return jnp.where(left, stacked[:count], stacked[count:])


def pair_probs(query, key, length):
    scores = dot(key, query, ((1,), (1,)))
    if length is not None:
        row = lax.broadcasted_iota(jnp.int32, scores.shape, 0)
        column = lax.broadcasted_iota(jnp.int32, scores.shape, 1) % (scores.shape[1] // 2)
        scores = jnp.where((row <= column) & (row < length), scores, -1e30)
    spread = jnp.exp(scores - jnp.max(scores, axis=0, keepdims=True))
    return spread * (1.0 / jnp.sum(spread, axis=0, keepdims=True))


def scaled(block):
    return block * jnp.asarray(1.0 / math.sqrt(HEAD_DIM), block.dtype)


def attend_body(table_ref, query_ref, key_ref, value_ref, out_ref, *, causal):
    length = table_ref[pl.program_id(0)] if causal else None
    for start in range(0, HEADS * HEAD_DIM, LANES):
        lanes = slice(start, start + LANES)
        query = stack_heads(scaled(query_ref[0, :, lanes]))
        probs = pair_probs(query, key_ref[0, :, lanes], length).astype(jnp.bfloat16)
        out_ref[0, :, lanes] = join_heads(dot(probs, value_ref[0, :, lanes], ((0,), (0,)))).astype(jnp.bfloat16)


def attend_back_body(table_ref, query_ref, key_ref, value_ref, grad_ref, query_grad_ref, pair_grad_ref, *, causal):
    length = table_ref[pl.program_id(0)] if causal else None
    width = HEADS * HEAD_DIM
    for start in range(0, width, LANES):
        lanes = slice(start, start + LANES)
        query = stack_heads(scaled(query_ref[0, :, lanes]))
        grad = stack_heads(grad_ref[0, :, lanes])
        key, value = key_ref[0, :, lanes], value_ref[0, :, lanes]
        probs = pair_probs(query, key, length)
        grad_probs = dot(value, grad, ((1,), (1,)))
        grad_scores = probs * (grad_probs - jnp.sum(grad_probs * probs, axis=0, keepdims=True))
        grad_scores = grad_scores.astype(jnp.bfloat16)
        back = lambda left, right: dot(left, right, ((1,), (0,))).astype(jnp.bfloat16)
        grad_query = scaled(join_heads(dot(grad_scores, key, ((0,), (0,))))).astype(jnp.bfloat16)
        grad_key, grad_value = back(grad_scores, query), back(probs.astype(jnp.bfloat16), grad)
        query_grad_ref[0, :, lanes] = grad_query
        if causal:
            query_grad_ref[0, :, slice(width + start, width + start + LANES)] = grad_key
            query_grad_ref[0, :, slice(2 * width + start, 2 * width + start + LANES)] = grad_value
        else:
            pair_grad_ref[0, :, lanes] = grad_key
            pair_grad_ref[0, :, slice(width + start, width + start + LANES)] = grad_value


def attention(body, table, arrays, outs, name, heavy, routed=False):
    width = HEADS * HEAD_DIM
    captions = arrays[0][0].shape[0]
    own = arrays[0][0].shape[1]

    def spec(rows, cols, at):
        if routed and rows != own:
            return pl.BlockSpec((1, rows, cols), lambda c, place: (place[c], 0, at))
        return pl.BlockSpec((1, rows, cols), lambda c, place: (c, 0, at))

    work = heavy * 2 * captions * arrays[0][0].shape[1] * arrays[1][0].shape[1] * width
    return pl.pallas_call(
        body,
        grid_spec=pltpu.PrefetchScalarGridSpec(
            num_scalar_prefetch=1,
            grid=(captions,),
            in_specs=[spec(array.shape[1], width, at) for array, at in arrays],
            out_specs=[spec(rows, cols, 0) for rows, cols in outs],
        ),
        out_shape=[jax.ShapeDtypeStruct((captions, rows, cols), jnp.bfloat16) for rows, cols in outs],
        compiler_params=pltpu.CompilerParams(dimension_semantics=("arbitrary",), vmem_limit_bytes=48 << 20),
        cost_estimate=pl.CostEstimate(flops=work, transcendentals=0, bytes_accessed=0),
        name=name,
    )(table, *(array for array, _ in arrays))


def self_forward(packed, lengths):
    rows, width = packed.shape[1], HEADS * HEAD_DIM
    return attention(functools.partial(attend_body, causal=True), lengths,
        [(packed, 0), (packed, 1), (packed, 2)], [(rows, width)], "self_attention", 2)[0]


def cross_forward(query_rows, pair, place):
    return attention(functools.partial(attend_body, causal=False), place,
        [(query_rows, 0), (pair, 0), (pair, 1)], [query_rows.shape[1:]], "cross_attention", 2, True)[0]


def self_body(*refs):
    attend_back_body(*refs, None, causal=True)


def self_backward(packed, grad_rows, lengths):
    return attention(self_body, lengths,
        [(packed, 0), (packed, 1), (packed, 2), (grad_rows, 0)], [packed.shape[1:]], "self_backward", 5)[0]


def cross_backward(query_rows, pair, grad_rows, place):
    return attention(functools.partial(attend_back_body, causal=False), place,
        [(query_rows, 0), (pair, 0), (pair, 1), (grad_rows, 0)],
        [query_rows.shape[1:], pair.shape[1:]], "cross_backward", 5, True)


def index_bits():
    found = []
    for axis in ("dp", "seq"):
        count = lax.axis_size(axis)
        found += [(axis, bit) for bit in reversed(range(count.bit_length() - 1))]
    return found


def swap_pairs(axis, bit):
    return [(i, i ^ (1 << bit)) for i in range(lax.axis_size(axis))]


def own_bit(axis, bit):
    return (lax.axis_index(axis) >> bit) & 1


def gather_order(flip):
    far = [("dp", bit) for bit in range(1, lax.axis_size("dp").bit_length() - 1)][::-1]
    near = [[("dp", 0)], [("seq", bit) for bit in range(1, lax.axis_size("seq").bit_length() - 1)]]
    if flip:
        near = near[::-1]
    return far + near[0] + near[1] + [("seq", 0)]


class Gather:
    def __init__(self, part, flip):
        bits = index_bits()
        self.own = [own_bit(*place) for place in bits]
        self.known = [1] * len(bits)
        self.shape = part.shape
        self.piece = part.reshape((1,) * len(bits) + part.shape)
        self.whole = jnp.zeros((2,) * len(bits) + part.shape, part.dtype)
        self.whole = self.put(self.piece, self.own)
        self.left = gather_order(flip)

    def put(self, piece, starts):
        return lax.dynamic_update_slice(self.whole, piece, starts + [0] * len(self.shape))

    def starts(self):
        return [0 if size == 2 else bit for size, bit in zip(self.known, self.own)]

    def step(self):
        place = self.left.pop(0)
        dim = index_bits().index(place)
        starts = self.starts()
        if self.piece is None:
            self.piece = lax.dynamic_slice(
                self.whole, starts + [0] * len(self.shape), self.known + list(self.shape)
            )
        other = lax.ppermute(self.piece, place[0], swap_pairs(*place))
        starts[dim] = 1 - self.own[dim]
        self.whole = self.put(other, starts)
        self.known[dim] = 2
        self.piece = None
        return other

    def rows(self):
        return self.whole.reshape((-1,) + self.shape[1:])


class Scatter:
    def __init__(self, whole, flip, span):
        bits = index_bits()
        self.rows = whole.shape[0] >> len(bits)
        self.tail = whole.shape[1:]
        self.state = whole.reshape((2,) * len(bits) + (self.rows,) + self.tail)
        order = gather_order(flip)
        far = [place for place in order[:-3]][::-1]
        pairs = [far[i : i + span] for i in range(0, len(far), span)]
        self.left = [[order[-1]], [order[-2]], [order[-3]]] + pairs

    def part(self, places, turn):
        part = self.state
        for place, flipped in zip(places, turn):
            dim = index_bits().index(place)
            part = lax.dynamic_slice_in_dim(part, own_bit(*place) ^ flipped, 1, dim)
        return part

    def step(self):
        places = self.left.pop(0)
        axis = places[0][0]
        total = self.part(places, [0] * len(places))
        for turn in list(itertools.product((0, 1), repeat=len(places)))[1:]:
            mask = sum(flipped << place[1] for place, flipped in zip(places, turn))
            pairs = [(i, i ^ mask) for i in range(lax.axis_size(axis))]
            total = total + lax.ppermute(self.part(places, turn), axis, pairs)
        self.state = total

    def join(self, other):
        self.state = jnp.concatenate([self.state, other.state], axis=-1)
        self.tail = self.state.shape[-1:]

    def finish(self):
        while self.left:
            self.step()
        return self.state.reshape((self.rows,) + self.tail).astype(jnp.float32)


def advance(scatters, *values):
    held = lax.optimization_barrier(tuple(one.state for one in scatters) + values)
    for one, state in zip(scatters, held):
        one.state = state
        if one.left:
            one.step()
    values = held[len(scatters) :]
    return values[0] if len(values) == 1 else values


def swap(rows, k):
    if not k:
        return rows
    return lax.ppermute(rows, "seq", [(i, i ^ k) for i in range(lax.axis_size("seq"))])


def lay_body(*refs):
    start = 0
    for ref in refs[:-1]:
        refs[-1][:, start : start + ref.shape[1]] = ref[...]
        start += ref.shape[1]


def lay_side_by_side(pieces):
    width = sum(piece.shape[1] for piece in pieces)
    return pl.pallas_call(
        lay_body,
        out_shape=jax.ShapeDtypeStruct((pieces[0].shape[0], width), pieces[0].dtype),
        name="lay_side_by_side",
    )(*pieces)


def put_body(table_ref, *refs):
    for k, ref in enumerate(refs[:-1]):

        @pl.when(pl.program_id(0) == k)
        def _():
            refs[-1][...] = ref[...]


def put_rows(pieces, table):
    shape = pieces[0].shape
    return pl.pallas_call(
        put_body,
        grid_spec=pltpu.PrefetchScalarGridSpec(
            num_scalar_prefetch=1,
            grid=(len(pieces),),
            in_specs=[pl.BlockSpec(shape, lambda k, at: (0, 0, 0)) for _ in pieces],
            out_specs=pl.BlockSpec(shape, lambda k, at: (at[k], 0, 0)),
        ),
        out_shape=jax.ShapeDtypeStruct((len(pieces),) + shape[1:], pieces[0].dtype),
        compiler_params=pltpu.CompilerParams(dimension_semantics=("arbitrary",)),
        cost_estimate=pl.CostEstimate(
            flops=0, transcendentals=0, bytes_accessed=4 * len(pieces) * shape[1] * shape[2]
        ),
        name="put_rows",
    )(table, *pieces)


def shards(
    caption_tokens,
    image_tokens,
    caption_lengths,
    caption_image,
    norm_gain,
    norm_bias,
    self_packed,
    self_output,
    cross_query,
    cross_pair,
    cross_output,
    expand_weight,
    reduce_weight,
    cotangent,
):
    captions, seq_len, model_width = caption_tokens.shape
    peer_count = lax.axis_size("seq")
    position = lax.axis_index("seq")

    owner = (caption_image // captions % peer_count).reshape(peer_count, captions)
    slot = (caption_image % captions).reshape(peer_count, captions)
    peers = jnp.arange(peer_count)
    mine = (peers == position).astype(jnp.int32)
    place = jnp.sum(owner * mine[:, None], axis=0) ^ position
    asked = jnp.sum(jnp.where(owner == position, slot, 0), axis=1)
    turned = (peers[:, None] ^ position) == peers[None, :]
    asked = jnp.sum(jnp.where(turned, asked[None, :], 0), axis=1)
    norm_columns = jnp.pad(jnp.concatenate([norm_gain, norm_bias], axis=1), ((0, 0), (0, 122)))
    rows = self_packed.shape[0]
    ratio = reduce_weight.shape[0] // rows
    reduce_blocks = [reduce_weight[k * rows : (k + 1) * rows] for k in range(ratio)]
    wide = lax.all_gather(
        lay_side_by_side(
            reduce_blocks + [expand_weight, cross_pair, cross_query, cross_output]
        ),
        ("dp", "seq"),
        axis=0,
        tiled=True,
    )
    first_group = Gather(
        jnp.concatenate([self_packed, self_output, norm_columns], axis=1), False
    )
    first_group.step()
    first_group.whole, asked, place = lax.optimization_barrier((first_group.whole, asked, place))
    first_group.step()
    wanted = [lax.dynamic_slice_in_dim(image_tokens, asked[k], 1) for k in range(peer_count)]
    first_group.whole, *wanted = lax.optimization_barrier((first_group.whole, *wanted))
    while len(first_group.left) > 1:
        came = first_group.step()
    wanted = lax.optimization_barrier((*wanted, came))[:-1]
    paired = [swap(row, k) for k, row in enumerate(wanted)]
    first_group.step()
    first_group = first_group.rows()
    packed_weight = first_group[:, : 3 * model_width]
    output_weight = first_group[:, 3 * model_width : 4 * model_width]
    norm_values = first_group[:, 4 * model_width : 4 * model_width + 6].astype(jnp.float32)
    norm_gains, norm_shifts = norm_values[:, :3], norm_values[:, 3:]
    hidden_width = expand_weight.shape[1]
    narrower = wide[:, 2 * hidden_width :]
    pair_weight = narrower[:, : 2 * model_width]
    query_weight = narrower[:, 2 * model_width : 3 * model_width]
    cross_weight = narrower[:, 3 * model_width :]

    live_rows = jnp.arange(seq_len)[None, :] < caption_lengths[:, None]
    inputs = caption_tokens.astype(jnp.float32)
    normed_full, scaled_one, inverse_one = layer_norm(inputs, norm_gains[:, 0], norm_shifts[:, 0])
    normed_one = normed_full.astype(jnp.bfloat16)
    packed = project(normed_one, packed_weight).astype(jnp.bfloat16)
    attended = self_forward(packed, caption_lengths)
    *paired, attended = lax.optimization_barrier((*paired, attended))
    paired = jnp.concatenate(paired)
    after_self = inputs + project(attended, output_weight)
    normed_full_two, scaled_two, inverse_two = layer_norm(
        after_self, norm_gains[:, 1], norm_shifts[:, 1]
    )
    normed_two = normed_full_two.astype(jnp.bfloat16)
    image_pair = project(paired, pair_weight).astype(jnp.bfloat16)
    query_rows = project(normed_two, query_weight).astype(jnp.bfloat16)
    mixed_rows = cross_forward(query_rows, image_pair, place)
    branch = project(mixed_rows, cross_weight).astype(jnp.bfloat16)
    after_cross = after_self + branch.astype(jnp.float32)
    normed_full_three, scaled_three, inverse_three = layer_norm(
        after_cross, norm_gains[:, 2], norm_shifts[:, 2]
    )
    normed_three = normed_full_three.astype(jnp.bfloat16)
    grad_out = jnp.where(live_rows[..., None], cotangent, jnp.zeros_like(cotangent))
    flat = lambda member: member.reshape(-1, model_width)
    forward, backward, reduce_part, expand_part = ffn(
        flat(normed_three), flat(grad_out), wide, rows, hidden_width
    )
    caption_out = jnp.where(
        live_rows[..., None], after_cross + forward.reshape(after_cross.shape), 0.0
    ).astype(jnp.bfloat16)

    narrow = lambda member: member.astype(jnp.bfloat16)
    reduce_sums = Scatter(reduce_part, True, 1)
    expand_sums = Scatter(expand_part, False, 1)
    reduce_sums.step()
    expand_sums.step()
    grad_norm_three, gain_three, shift_three = norm_back(
        backward.reshape(after_cross.shape), scaled_three, inverse_three, norm_gains[:, 2]
    )
    grad_second = grad_out.astype(jnp.float32) + grad_norm_three
    grad_branch = grad_second.astype(jnp.bfloat16)
    grad_cross_mixed = project_back(grad_branch, cross_weight).astype(jnp.bfloat16)
    grad_cross_mixed, grad_branch = advance(
        [reduce_sums, expand_sums], grad_cross_mixed, grad_branch
    )
    cross_output_grad = weight_grad(mixed_rows, grad_branch)
    grad_cross_rows, grad_pair = cross_backward(
        query_rows, image_pair, grad_cross_mixed, place
    )
    cross_pair_grad = weight_grad(paired, grad_pair)
    cross_sums = Scatter(
        narrow(jnp.concatenate([cross_pair_grad, cross_output_grad], axis=1)), True, 2
    )
    image_rows = project_back(grad_pair, pair_weight).astype(jnp.bfloat16)
    image_rows, grad_cross_rows = advance(
        [reduce_sums, expand_sums, cross_sums], image_rows, grad_cross_rows
    )
    cross_query_grad = weight_grad(normed_two, grad_cross_rows)
    grad_norm_two, gain_two, shift_two = norm_back(
        project_back(grad_cross_rows, query_weight).astype(jnp.bfloat16).astype(jnp.float32),
        scaled_two,
        inverse_two,
        norm_gains[:, 1],
    )
    grad_first = grad_second + grad_norm_two
    grad_self = grad_first.astype(jnp.bfloat16)
    self_output_grad = weight_grad(attended, grad_self)
    grad_self, image_rows = advance([reduce_sums, expand_sums, cross_sums], grad_self, image_rows)
    home = [swap(image_rows[k : k + 1], k) for k in range(peer_count)]
    grad_attended = project_back(grad_self, output_weight).astype(jnp.bfloat16)
    grad_packed = self_backward(packed, grad_attended, caption_lengths)
    grad_packed, *home = advance([reduce_sums, expand_sums, cross_sums], grad_packed, *home)
    self_packed_grad = weight_grad(normed_one, grad_packed)
    grad_norm_one, gain_one, shift_one = norm_back(
        project_back(grad_packed, packed_weight), scaled_one, inverse_one, norm_gains[:, 0]
    )
    caption_grad = (grad_first + grad_norm_one).astype(jnp.bfloat16)
    norm_sums = jnp.stack([gain_one, gain_two, gain_three, shift_one, shift_two, shift_three], axis=1)
    half = model_width // 2
    left = jnp.concatenate([cross_query_grad, self_output_grad, self_packed_grad[:, :half]], axis=1)
    right = jnp.concatenate(
        [self_packed_grad[:, half:], jnp.pad(norm_sums, ((0, 0), (0, 122)))], axis=1
    )
    left_sums = Scatter(narrow(left), True, 2)
    right_sums = Scatter(narrow(right), False, 2)
    left_sums.step()
    right_sums.step()
    groups = [cross_sums, reduce_sums, expand_sums, left_sums, right_sums]
    while len(left_sums.left) > 1:
        advance(groups)
    left_sums.join(right_sums)
    home = advance([left_sums], *home)
    image_grad = put_rows(list(home), asked)
    self_sums = left_sums.finish()
    reduce_grad, expand_grad = reduce_sums.finish(), expand_sums.finish()
    cross_sums = cross_sums.finish()
    last = 5 * model_width
    return (
        caption_out,
        caption_grad,
        image_grad,
        self_sums[:, last : last + 3],
        self_sums[:, last + 3 : last + 6],
        self_sums[:, 2 * model_width : last],
        self_sums[:, model_width : 2 * model_width],
        self_sums[:, :model_width],
        cross_sums[:, : 2 * model_width],
        cross_sums[:, 2 * model_width :],
        expand_grad,
        reduce_grad,
    )


def solution(mesh):
    placed = (
        P(("dp", "seq"), None, None),
        P(("dp", "seq"), None, None),
        P(("dp", "seq")),
        P("dp"),
        P(("dp", "seq"), None),
        P(("dp", "seq"), None),
        P(("dp", "seq"), None),
        P(("dp", "seq"), None),
        P(("dp", "seq"), None),
        P(("dp", "seq"), None),
        P(("dp", "seq"), None),
        P(("dp", "seq"), None),
        P(("dp", "seq"), None),
        P(("dp", "seq"), None, None),
    )
    return jax.shard_map(
        shards,
        mesh=mesh,
        in_specs=placed,
        out_specs=(
            P(("dp", "seq"), None, None),
            P(("dp", "seq"), None, None),
            P(("dp", "seq"), None, None),
            P(("dp", "seq"), None),
            P(("dp", "seq"), None),
            P(("dp", "seq"), None),
            P(("dp", "seq"), None),
            P(("dp", "seq"), None),
            P(("dp", "seq"), None),
            P(("dp", "seq"), None),
            P(("dp", "seq"), None),
            P(("dp", "seq"), None),
        ),
        check_vma=False,
    )
```

```python
import functools
import itertools
import math

import jax
import jax.numpy as jnp
from jax import lax
from jax.experimental import pallas as pl
from jax.experimental.pallas import tpu as pltpu
from jax.sharding import PartitionSpec as P

HEADS = 12
HEAD_DIM = 64


epsilon = 1e-05


TILE = 384
LANES = 128


def project(values, weight):
    flat_rows = values.reshape(-1, values.shape[-1])
    return jnp.dot(flat_rows, weight, preferred_element_type=jnp.float32).reshape(
        values.shape[:-1] + (weight.shape[1],)
    )


def project_back(values, weight):
    flat_rows = values.reshape(-1, values.shape[-1])
    result = lax.dot_general(
        flat_rows, weight, (((1,), (1,)), ((), ())), preferred_element_type=jnp.float32
    )
    return result.reshape(values.shape[:-1] + (weight.shape[0],))


def weight_grad(left_rows, right_rows):
    return lax.dot_general(
        left_rows.reshape(-1, left_rows.shape[-1]),
        right_rows.reshape(-1, right_rows.shape[-1]),
        (((0,), (0,)), ((), ())),
        preferred_element_type=jnp.float32,
    )


def layer_norm(values, gain, shift):
    centred = values - jnp.mean(values, axis=-1, keepdims=True)
    spread = jnp.mean(centred * centred, axis=-1, keepdims=True)
    inverse = lax.rsqrt(spread + epsilon)
    scaled = centred * inverse
    return (scaled * gain + shift, scaled, inverse)


def norm_back(grad_rows, scaled, inverse, gain):
    weighted = grad_rows * gain
    result = inverse * (
        weighted
        - jnp.mean(weighted, axis=-1, keepdims=True)
        - scaled * jnp.mean(weighted * scaled, axis=-1, keepdims=True)
    )
    flat_grad = grad_rows.reshape(-1, grad_rows.shape[-1])
    flat_scaled = scaled.reshape(-1, scaled.shape[-1])
    return (result, jnp.sum(flat_grad * flat_scaled, axis=0), jnp.sum(flat_grad, axis=0))


def dot(left, right, contract):
    return lax.dot_general(left, right, (contract, ((), ())), preferred_element_type=jnp.float32)


def alternate(whole, span):
    blocks = [whole[at : at + span] for at in range(0, whole.shape[0], span)]
    return [
        jnp.concatenate(blocks[which::2], axis=0).astype(jnp.bfloat16) for which in range(2)
    ]


def ffn_body(
    bit_ref, rows_ref, grad_ref, expand_ref, reduce_ref, order_ref, out_ref, back_ref, *sum_refs,
    ratio, span
):
    rows, grad = rows_ref[...], grad_ref[...]
    width = rows.shape[1]
    stacked = jnp.concatenate([reduce_ref[:, k * width : (k + 1) * width] for k in range(ratio)], axis=0)
    reduce = dot(order_ref[...], stacked, ((1,), (0,))).astype(jnp.bfloat16)
    expand = expand_ref[...]
    gate = dot(rows, expand, ((1,), (0,)))
    grad_hidden = dot(grad, reduce, ((1,), (1,)))
    share = 0.5 * (1.0 + lax.erf(gate * math.sqrt(0.5)))
    slope = share + gate * (jnp.exp(-0.5 * gate * gate) * (1.0 / math.sqrt(2.0 * math.pi)))
    hidden = (gate * share).astype(jnp.bfloat16)
    grad_gate = (grad_hidden * slope).astype(jnp.bfloat16)
    reduce_grad = dot(hidden, grad, ((0,), (0,)))
    expand_grad = dot(rows, grad_gate, ((0,), (0,)))
    if span:
        halves = [alternate(reduce_grad, span * ratio), alternate(expand_grad, span)]
        for own in range(2):

            @pl.when(bit_ref[0] == own)
            def _():
                for i, pair in enumerate(halves):
                    sum_refs[2 * i][...] = pair[own]
                    sum_refs[2 * i + 1][...] = pair[1 - own]

    else:
        sum_refs[0][...] = reduce_grad.astype(jnp.bfloat16)
        sum_refs[1][...] = expand_grad.astype(jnp.bfloat16)
    first = pl.program_id(0) == 0
    @pl.when(first)
    def _():
        out_ref[...] = jnp.zeros_like(out_ref)
        back_ref[...] = jnp.zeros_like(back_ref)
    out_ref[...] += dot(hidden, reduce, ((1,), (0,)))
    back_ref[...] += dot(grad_gate, expand, ((1,), (1,)))


def ffn(rows, grad, others, per_device, hidden_width):
    count, width = rows.shape
    ratio = hidden_width // width
    part = TILE // ratio
    place = jnp.arange(TILE)
    chunk = per_device * ratio
    source = part * (place % chunk // per_device) + per_device * (place // chunk) + place % per_device
    order = (source[:, None] == place[None, :]).astype(jnp.bfloat16)
    whole = lambda shape: pl.BlockSpec(shape, lambda j: (0, 0))
    span = per_device if per_device % 8 == 0 and chunk % 16 == 0 else 0
    copies = 2 if span else 1
    sums = []
    for shape, block, at in (
        ((hidden_width, width), (TILE, width), lambda j: (j, 0)),
        ((width, hidden_width), (width, TILE), lambda j: (0, j)),
    ):
        part_of = lambda size: (size[0] // copies, size[1])
        sums += copies * [
            (pl.BlockSpec(part_of(block), at), jax.ShapeDtypeStruct(part_of(shape), jnp.bfloat16))
        ]
    return pl.pallas_call(
        functools.partial(ffn_body, ratio=ratio, span=span),
        grid=(hidden_width // TILE,),
        in_specs=[
            pl.BlockSpec(memory_space=pltpu.SMEM),
            whole((count, width)),
            whole((count, width)),
            pl.BlockSpec((width, TILE), lambda j: (0, hidden_width // TILE + j)),
            pl.BlockSpec((part, hidden_width), lambda j: (j, 0)),
            whole((TILE, TILE)),
        ],
        out_specs=[whole((count, width)), whole((count, width))] + [spec for spec, _ in sums],
        out_shape=2 * [jax.ShapeDtypeStruct((count, width), jnp.float32)]
        + [shape for _, shape in sums],
        compiler_params=pltpu.CompilerParams(
            dimension_semantics=("arbitrary",), vmem_limit_bytes=48 << 20
        ),
        name="ffn",
    )(own_bit("seq", 0).astype(jnp.int32).reshape(1), rows, grad, others, others, order)


def stack_heads(block):
    left = lax.broadcasted_iota(jnp.int32, block.shape, 1) < HEAD_DIM
    none = jnp.zeros_like(block)
    return jnp.concatenate([jnp.where(left, block, none), jnp.where(left, none, block)], axis=0)


def join_heads(stacked):
    count = stacked.shape[0] // 2
    left = lax.broadcasted_iota(jnp.int32, (count, LANES), 1) < HEAD_DIM
    return jnp.where(left, stacked[:count], stacked[count:])


def pair_probs(query, key, length):
    scores = dot(key, query, ((1,), (1,)))
    if length is not None:
        row = lax.broadcasted_iota(jnp.int32, scores.shape, 0)
        column = lax.broadcasted_iota(jnp.int32, scores.shape, 1) % (scores.shape[1] // 2)
        scores = jnp.where((row <= column) & (row < length), scores, -1e30)
    spread = jnp.exp(scores - jnp.max(scores, axis=0, keepdims=True))
    return spread * (1.0 / jnp.sum(spread, axis=0, keepdims=True))


def scaled(block):
    return block * jnp.asarray(1.0 / math.sqrt(HEAD_DIM), block.dtype)


def attend_body(table_ref, query_ref, key_ref, value_ref, out_ref, *, causal):
    length = table_ref[pl.program_id(0)] if causal else None
    for start in range(0, HEADS * HEAD_DIM, LANES):
        lanes = slice(start, start + LANES)
        query = stack_heads(scaled(query_ref[0, :, lanes]))
        probs = pair_probs(query, key_ref[0, :, lanes], length).astype(jnp.bfloat16)
        out_ref[0, :, lanes] = join_heads(dot(probs, value_ref[0, :, lanes], ((0,), (0,)))).astype(jnp.bfloat16)


def attend_back_body(table_ref, query_ref, key_ref, value_ref, grad_ref, query_grad_ref, pair_grad_ref, *, causal):
    length = table_ref[pl.program_id(0)] if causal else None
    width = HEADS * HEAD_DIM
    for start in range(0, width, LANES):
        lanes = slice(start, start + LANES)
        query = stack_heads(scaled(query_ref[0, :, lanes]))
        grad = stack_heads(grad_ref[0, :, lanes])
        key, value = key_ref[0, :, lanes], value_ref[0, :, lanes]
        probs = pair_probs(query, key, length)
        grad_probs = dot(value, grad, ((1,), (1,)))
        grad_scores = probs * (grad_probs - jnp.sum(grad_probs * probs, axis=0, keepdims=True))
        grad_scores = grad_scores.astype(jnp.bfloat16)
        back = lambda left, right: dot(left, right, ((1,), (0,))).astype(jnp.bfloat16)
        grad_query = scaled(join_heads(dot(grad_scores, key, ((0,), (0,))))).astype(jnp.bfloat16)
        grad_key, grad_value = back(grad_scores, query), back(probs.astype(jnp.bfloat16), grad)
        query_grad_ref[0, :, lanes] = grad_query
        if causal:
            query_grad_ref[0, :, slice(width + start, width + start + LANES)] = grad_key
            query_grad_ref[0, :, slice(2 * width + start, 2 * width + start + LANES)] = grad_value
        else:
            pair_grad_ref[0, :, lanes] = grad_key
            pair_grad_ref[0, :, slice(width + start, width + start + LANES)] = grad_value


def attention(body, table, arrays, outs, name, heavy, routed=False):
    width = HEADS * HEAD_DIM
    captions = arrays[0][0].shape[0]
    own = arrays[0][0].shape[1]

    def spec(rows, cols, at):
        if routed and rows != own:
            return pl.BlockSpec((1, rows, cols), lambda c, place: (place[c], 0, at))
        return pl.BlockSpec((1, rows, cols), lambda c, place: (c, 0, at))

    work = heavy * 2 * captions * arrays[0][0].shape[1] * arrays[1][0].shape[1] * width
    return pl.pallas_call(
        body,
        grid_spec=pltpu.PrefetchScalarGridSpec(
            num_scalar_prefetch=1,
            grid=(captions,),
            in_specs=[spec(array.shape[1], width, at) for array, at in arrays],
            out_specs=[spec(rows, cols, 0) for rows, cols in outs],
        ),
        out_shape=[jax.ShapeDtypeStruct((captions, rows, cols), jnp.bfloat16) for rows, cols in outs],
        compiler_params=pltpu.CompilerParams(dimension_semantics=("arbitrary",), vmem_limit_bytes=48 << 20),
        cost_estimate=pl.CostEstimate(flops=work, transcendentals=0, bytes_accessed=0),
        name=name,
    )(table, *(array for array, _ in arrays))


def self_forward(packed, lengths):
    rows, width = packed.shape[1], HEADS * HEAD_DIM
    return attention(functools.partial(attend_body, causal=True), lengths,
        [(packed, 0), (packed, 1), (packed, 2)], [(rows, width)], "self_attention", 2)[0]


def cross_forward(query_rows, pair, place):
    return attention(functools.partial(attend_body, causal=False), place,
        [(query_rows, 0), (pair, 0), (pair, 1)], [query_rows.shape[1:]], "cross_attention", 2, True)[0]


def self_body(*refs):
    attend_back_body(*refs, None, causal=True)


def self_backward(packed, grad_rows, lengths):
    return attention(self_body, lengths,
        [(packed, 0), (packed, 1), (packed, 2), (grad_rows, 0)], [packed.shape[1:]], "self_backward", 5)[0]


def cross_backward(query_rows, pair, grad_rows, place):
    return attention(functools.partial(attend_back_body, causal=False), place,
        [(query_rows, 0), (pair, 0), (pair, 1), (grad_rows, 0)],
        [query_rows.shape[1:], pair.shape[1:]], "cross_backward", 5, True)


def index_bits():
    found = []
    for axis in ("dp", "seq"):
        count = lax.axis_size(axis)
        found += [(axis, bit) for bit in reversed(range(count.bit_length() - 1))]
    return found


def swap_pairs(axis, bit):
    return [(i, i ^ (1 << bit)) for i in range(lax.axis_size(axis))]


def own_bit(axis, bit):
    return (lax.axis_index(axis) >> bit) & 1


def gather_order(flip):
    far = [("dp", bit) for bit in range(1, lax.axis_size("dp").bit_length() - 1)][::-1]
    near = [[("dp", 0)], [("seq", bit) for bit in range(1, lax.axis_size("seq").bit_length() - 1)]]
    if flip:
        near = near[::-1]
    return far + near[0] + near[1] + [("seq", 0)]


class Gather:
    def __init__(self, part, flip):
        bits = index_bits()
        self.own = [own_bit(*place) for place in bits]
        self.known = [1] * len(bits)
        self.shape = part.shape
        self.piece = part.reshape((1,) * len(bits) + part.shape)
        self.whole = jnp.zeros((2,) * len(bits) + part.shape, part.dtype)
        self.whole = self.put(self.piece, self.own)
        self.left = gather_order(flip)

    def put(self, piece, starts):
        return lax.dynamic_update_slice(self.whole, piece, starts + [0] * len(self.shape))

    def starts(self):
        return [0 if size == 2 else bit for size, bit in zip(self.known, self.own)]

    def step(self):
        place = self.left.pop(0)
        dim = index_bits().index(place)
        starts = self.starts()
        if self.piece is None:
            self.piece = lax.dynamic_slice(
                self.whole, starts + [0] * len(self.shape), self.known + list(self.shape)
            )
        other = lax.ppermute(self.piece, place[0], swap_pairs(*place))
        starts[dim] = 1 - self.own[dim]
        self.whole = self.put(other, starts)
        self.known[dim] = 2
        self.piece = None
        return other

    def rows(self):
        return self.whole.reshape((-1,) + self.shape[1:])


class Scatter:
    def __init__(self, whole, flip, span):
        bits = index_bits()
        self.rows = whole.shape[0] >> len(bits)
        self.tail = whole.shape[1:]
        self.state = whole.reshape((2,) * len(bits) + (self.rows,) + self.tail)
        order = gather_order(flip)
        far = [place for place in order[:-3]][::-1]
        pairs = [far[i : i + span] for i in range(0, len(far), span)]
        self.left = [[order[-1]], [order[-2]], [order[-3]]] + pairs

    @classmethod
    def halved(cls, kept, given, flip, span):
        one = cls(jnp.concatenate([kept[:0], given[:0]]), flip, span)
        bits = len(index_bits())
        one.rows = kept.shape[0] >> (bits - 1)
        shape = (2,) * (bits - 1) + (1, one.rows) + one.tail
        place = one.left.pop(0)[0]
        other = lax.ppermute(given.reshape(shape), place[0], swap_pairs(*place))
        one.state = kept.reshape(shape) + other
        return one

    def part(self, places, turn):
        part = self.state
        for place, flipped in zip(places, turn):
            dim = index_bits().index(place)
            part = lax.dynamic_slice_in_dim(part, own_bit(*place) ^ flipped, 1, dim)
        return part

    def step(self):
        places = self.left.pop(0)
        axis = places[0][0]
        total = self.part(places, [0] * len(places))
        for turn in list(itertools.product((0, 1), repeat=len(places)))[1:]:
            mask = sum(flipped << place[1] for place, flipped in zip(places, turn))
            pairs = [(i, i ^ mask) for i in range(lax.axis_size(axis))]
            total = total + lax.ppermute(self.part(places, turn), axis, pairs)
        self.state = total

    def join(self, other):
        self.state = jnp.concatenate([self.state, other.state], axis=-1)
        self.tail = self.state.shape[-1:]

    def finish(self):
        while self.left:
            self.step()
        return self.state.reshape((self.rows,) + self.tail).astype(jnp.float32)


def advance(scatters, *values):
    held = lax.optimization_barrier(tuple(one.state for one in scatters) + values)
    for one, state in zip(scatters, held):
        one.state = state
        if one.left:
            one.step()
    values = held[len(scatters) :]
    return values[0] if len(values) == 1 else values


def swap(rows, k):
    if not k:
        return rows
    return lax.ppermute(rows, "seq", [(i, i ^ k) for i in range(lax.axis_size("seq"))])


def lay_body(*refs):
    start = 0
    for ref in refs[:-1]:
        refs[-1][:, start : start + ref.shape[1]] = ref[...]
        start += ref.shape[1]


def lay_side_by_side(pieces):
    width = sum(piece.shape[1] for piece in pieces)
    return pl.pallas_call(
        lay_body,
        out_shape=jax.ShapeDtypeStruct((pieces[0].shape[0], width), pieces[0].dtype),
        name="lay_side_by_side",
    )(*pieces)


def put_body(table_ref, *refs):
    for k, ref in enumerate(refs[:-1]):

        @pl.when(pl.program_id(0) == k)
        def _():
            refs[-1][...] = ref[...]


def put_rows(pieces, table):
    shape = pieces[0].shape
    return pl.pallas_call(
        put_body,
        grid_spec=pltpu.PrefetchScalarGridSpec(
            num_scalar_prefetch=1,
            grid=(len(pieces),),
            in_specs=[pl.BlockSpec(shape, lambda k, at: (0, 0, 0)) for _ in pieces],
            out_specs=pl.BlockSpec(shape, lambda k, at: (at[k], 0, 0)),
        ),
        out_shape=jax.ShapeDtypeStruct((len(pieces),) + shape[1:], pieces[0].dtype),
        compiler_params=pltpu.CompilerParams(dimension_semantics=("arbitrary",)),
        cost_estimate=pl.CostEstimate(
            flops=0, transcendentals=0, bytes_accessed=4 * len(pieces) * shape[1] * shape[2]
        ),
        name="put_rows",
    )(table, *pieces)


def shards(
    caption_tokens,
    image_tokens,
    caption_lengths,
    caption_image,
    norm_gain,
    norm_bias,
    self_packed,
    self_output,
    cross_query,
    cross_pair,
    cross_output,
    expand_weight,
    reduce_weight,
    cotangent,
):
    captions, seq_len, model_width = caption_tokens.shape
    peer_count = lax.axis_size("seq")
    position = lax.axis_index("seq")

    owner = (caption_image // captions % peer_count).reshape(peer_count, captions)
    slot = (caption_image % captions).reshape(peer_count, captions)
    peers = jnp.arange(peer_count)
    mine = (peers == position).astype(jnp.int32)
    place = jnp.sum(owner * mine[:, None], axis=0) ^ position
    asked = jnp.sum(jnp.where(owner == position, slot, 0), axis=1)
    turned = (peers[:, None] ^ position) == peers[None, :]
    asked = jnp.sum(jnp.where(turned, asked[None, :], 0), axis=1)
    norm_columns = jnp.pad(jnp.concatenate([norm_gain, norm_bias], axis=1), ((0, 0), (0, 122)))
    rows = self_packed.shape[0]
    ratio = reduce_weight.shape[0] // rows
    reduce_blocks = [reduce_weight[k * rows : (k + 1) * rows] for k in range(ratio)]
    wide = lax.all_gather(
        lay_side_by_side(
            reduce_blocks + [expand_weight, cross_pair, cross_query, cross_output]
        ),
        ("dp", "seq"),
        axis=0,
        tiled=True,
    )
    first_group = Gather(
        jnp.concatenate([self_packed, self_output, norm_columns], axis=1), False
    )
    first_group.step()
    first_group.whole, asked, place = lax.optimization_barrier((first_group.whole, asked, place))
    first_group.step()
    wanted = [lax.dynamic_slice_in_dim(image_tokens, asked[k], 1) for k in range(peer_count)]
    first_group.whole, *wanted = lax.optimization_barrier((first_group.whole, *wanted))
    while len(first_group.left) > 1:
        came = first_group.step()
    wanted = lax.optimization_barrier((*wanted, came))[:-1]
    paired = [swap(row, k) for k, row in enumerate(wanted)]
    first_group.step()
    first_group = first_group.rows()
    packed_weight = first_group[:, : 3 * model_width]
    output_weight = first_group[:, 3 * model_width : 4 * model_width]
    norm_values = first_group[:, 4 * model_width : 4 * model_width + 6].astype(jnp.float32)
    norm_gains, norm_shifts = norm_values[:, :3], norm_values[:, 3:]
    hidden_width = expand_weight.shape[1]
    narrower = wide[:, 2 * hidden_width :]
    pair_weight = narrower[:, : 2 * model_width]
    query_weight = narrower[:, 2 * model_width : 3 * model_width]
    cross_weight = narrower[:, 3 * model_width :]

    live_rows = jnp.arange(seq_len)[None, :] < caption_lengths[:, None]
    inputs = caption_tokens.astype(jnp.float32)
    normed_full, scaled_one, inverse_one = layer_norm(inputs, norm_gains[:, 0], norm_shifts[:, 0])
    normed_one = normed_full.astype(jnp.bfloat16)
    packed = project(normed_one, packed_weight).astype(jnp.bfloat16)
    attended = self_forward(packed, caption_lengths)
    *paired, attended = lax.optimization_barrier((*paired, attended))
    paired = jnp.concatenate(paired)
    after_self = inputs + project(attended, output_weight)
    normed_full_two, scaled_two, inverse_two = layer_norm(
        after_self, norm_gains[:, 1], norm_shifts[:, 1]
    )
    normed_two = normed_full_two.astype(jnp.bfloat16)
    image_pair = project(paired, pair_weight).astype(jnp.bfloat16)
    query_rows = project(normed_two, query_weight).astype(jnp.bfloat16)
    mixed_rows = cross_forward(query_rows, image_pair, place)
    branch = project(mixed_rows, cross_weight).astype(jnp.bfloat16)
    after_cross = after_self + branch.astype(jnp.float32)
    normed_full_three, scaled_three, inverse_three = layer_norm(
        after_cross, norm_gains[:, 2], norm_shifts[:, 2]
    )
    normed_three = normed_full_three.astype(jnp.bfloat16)
    grad_out = jnp.where(live_rows[..., None], cotangent, jnp.zeros_like(cotangent))
    flat = lambda member: member.reshape(-1, model_width)
    forward, backward, *parts = ffn(
        flat(normed_three), flat(grad_out), wide, rows, hidden_width
    )
    caption_out = jnp.where(
        live_rows[..., None], after_cross + forward.reshape(after_cross.shape), 0.0
    ).astype(jnp.bfloat16)

    narrow = lambda member: member.astype(jnp.bfloat16)
    if len(parts) == 4:
        reduce_sums = Scatter.halved(*parts[:2], True, 1)
        expand_sums = Scatter.halved(*parts[2:], False, 1)
    else:
        reduce_sums = Scatter(parts[0], True, 1)
        expand_sums = Scatter(parts[1], False, 1)
        reduce_sums.step()
        expand_sums.step()
    grad_norm_three, gain_three, shift_three = norm_back(
        backward.reshape(after_cross.shape), scaled_three, inverse_three, norm_gains[:, 2]
    )
    grad_second = grad_out.astype(jnp.float32) + grad_norm_three
    grad_branch = grad_second.astype(jnp.bfloat16)
    grad_cross_mixed = project_back(grad_branch, cross_weight).astype(jnp.bfloat16)
    grad_cross_mixed, grad_branch = advance(
        [reduce_sums, expand_sums], grad_cross_mixed, grad_branch
    )
    cross_output_grad = weight_grad(mixed_rows, grad_branch)
    grad_cross_rows, grad_pair = cross_backward(
        query_rows, image_pair, grad_cross_mixed, place
    )
    cross_pair_grad = weight_grad(paired, grad_pair)
    cross_sums = Scatter(
        narrow(jnp.concatenate([cross_pair_grad, cross_output_grad], axis=1)), True, 2
    )
    image_rows = project_back(grad_pair, pair_weight).astype(jnp.bfloat16)
    image_rows, grad_cross_rows = advance(
        [reduce_sums, expand_sums, cross_sums], image_rows, grad_cross_rows
    )
    cross_query_grad = weight_grad(normed_two, grad_cross_rows)
    grad_norm_two, gain_two, shift_two = norm_back(
        project_back(grad_cross_rows, query_weight).astype(jnp.bfloat16).astype(jnp.float32),
        scaled_two,
        inverse_two,
        norm_gains[:, 1],
    )
    grad_first = grad_second + grad_norm_two
    grad_self = grad_first.astype(jnp.bfloat16)
    self_output_grad = weight_grad(attended, grad_self)
    grad_self, image_rows = advance([reduce_sums, expand_sums, cross_sums], grad_self, image_rows)
    home = [swap(image_rows[k : k + 1], k) for k in range(peer_count)]
    grad_attended = project_back(grad_self, output_weight).astype(jnp.bfloat16)
    grad_packed = self_backward(packed, grad_attended, caption_lengths)
    grad_packed, *home = advance([reduce_sums, expand_sums, cross_sums], grad_packed, *home)
    self_packed_grad = weight_grad(normed_one, grad_packed)
    grad_norm_one, gain_one, shift_one = norm_back(
        project_back(grad_packed, packed_weight), scaled_one, inverse_one, norm_gains[:, 0]
    )
    caption_grad = (grad_first + grad_norm_one).astype(jnp.bfloat16)
    norm_sums = jnp.stack([gain_one, gain_two, gain_three, shift_one, shift_two, shift_three], axis=1)
    half = model_width // 2
    left = jnp.concatenate([cross_query_grad, self_output_grad, self_packed_grad[:, :half]], axis=1)
    right = jnp.concatenate(
        [self_packed_grad[:, half:], jnp.pad(norm_sums, ((0, 0), (0, 122)))], axis=1
    )
    left_sums = Scatter(narrow(left), True, 2)
    right_sums = Scatter(narrow(right), False, 2)
    left_sums.step()
    right_sums.step()
    groups = [cross_sums, reduce_sums, expand_sums, left_sums, right_sums]
    while len(left_sums.left) > 1:
        advance(groups)
    left_sums.join(right_sums)
    home = advance([left_sums], *home)
    image_grad = put_rows(list(home), asked)
    self_sums = left_sums.finish()
    reduce_grad, expand_grad = reduce_sums.finish(), expand_sums.finish()
    cross_sums = cross_sums.finish()
    last = 5 * model_width
    return (
        caption_out,
        caption_grad,
        image_grad,
        self_sums[:, last : last + 3],
        self_sums[:, last + 3 : last + 6],
        self_sums[:, 2 * model_width : last],
        self_sums[:, model_width : 2 * model_width],
        self_sums[:, :model_width],
        cross_sums[:, : 2 * model_width],
        cross_sums[:, 2 * model_width :],
        expand_grad,
        reduce_grad,
    )


def solution(mesh):
    placed = (
        P(("dp", "seq"), None, None),
        P(("dp", "seq"), None, None),
        P(("dp", "seq")),
        P("dp"),
        P(("dp", "seq"), None),
        P(("dp", "seq"), None),
        P(("dp", "seq"), None),
        P(("dp", "seq"), None),
        P(("dp", "seq"), None),
        P(("dp", "seq"), None),
        P(("dp", "seq"), None),
        P(("dp", "seq"), None),
        P(("dp", "seq"), None),
        P(("dp", "seq"), None, None),
    )
    return jax.shard_map(
        shards,
        mesh=mesh,
        in_specs=placed,
        out_specs=(
            P(("dp", "seq"), None, None),
            P(("dp", "seq"), None, None),
            P(("dp", "seq"), None, None),
            P(("dp", "seq"), None),
            P(("dp", "seq"), None),
            P(("dp", "seq"), None),
            P(("dp", "seq"), None),
            P(("dp", "seq"), None),
            P(("dp", "seq"), None),
            P(("dp", "seq"), None),
            P(("dp", "seq"), None),
            P(("dp", "seq"), None),
        ),
        check_vma=False,
    )
```

```python
import functools
import itertools
import math

import jax
import jax.numpy as jnp
from jax import lax
from jax.experimental import pallas as pl
from jax.experimental.pallas import tpu as pltpu
from jax.sharding import PartitionSpec as P

HEADS = 12
HEAD_DIM = 64


epsilon = 1e-05


TILE = 384
LANES = 128


def project(values, weight):
    flat_rows = values.reshape(-1, values.shape[-1])
    return jnp.dot(flat_rows, weight, preferred_element_type=jnp.float32).reshape(
        values.shape[:-1] + (weight.shape[1],)
    )


def project_back(values, weight):
    flat_rows = values.reshape(-1, values.shape[-1])
    result = lax.dot_general(
        flat_rows, weight, (((1,), (1,)), ((), ())), preferred_element_type=jnp.float32
    )
    return result.reshape(values.shape[:-1] + (weight.shape[0],))


def weight_grad(left_rows, right_rows):
    return lax.dot_general(
        left_rows.reshape(-1, left_rows.shape[-1]),
        right_rows.reshape(-1, right_rows.shape[-1]),
        (((0,), (0,)), ((), ())),
        preferred_element_type=jnp.float32,
    )


def layer_norm(values, gain, shift):
    centred = values - jnp.mean(values, axis=-1, keepdims=True)
    spread = jnp.mean(centred * centred, axis=-1, keepdims=True)
    inverse = lax.rsqrt(spread + epsilon)
    scaled = centred * inverse
    return (scaled * gain + shift, scaled, inverse)


def norm_back(grad_rows, scaled, inverse, gain):
    weighted = grad_rows * gain
    result = inverse * (
        weighted
        - jnp.mean(weighted, axis=-1, keepdims=True)
        - scaled * jnp.mean(weighted * scaled, axis=-1, keepdims=True)
    )
    flat_grad = grad_rows.reshape(-1, grad_rows.shape[-1])
    flat_scaled = scaled.reshape(-1, scaled.shape[-1])
    return (result, jnp.sum(flat_grad * flat_scaled, axis=0), jnp.sum(flat_grad, axis=0))


def dot(left, right, contract):
    return lax.dot_general(left, right, (contract, ((), ())), preferred_element_type=jnp.float32)


def alternate(whole, span):
    blocks = [whole[at : at + span] for at in range(0, whole.shape[0], span)]
    return [
        jnp.concatenate(blocks[which::2], axis=0).astype(jnp.bfloat16) for which in range(2)
    ]


def ffn_body(
    bit_ref, rows_ref, grad_ref, expand_ref, reduce_ref, order_ref, out_ref, back_ref, *sum_refs,
    ratio, span
):
    rows, grad = rows_ref[...], grad_ref[...]
    width = rows.shape[1]
    stacked = jnp.concatenate([reduce_ref[:, k * width : (k + 1) * width] for k in range(ratio)], axis=0)
    reduce = dot(order_ref[...], stacked, ((1,), (0,))).astype(jnp.bfloat16)
    expand = expand_ref[...]
    gate = dot(rows, expand, ((1,), (0,)))
    grad_hidden = dot(grad, reduce, ((1,), (1,)))
    share = 0.5 * (1.0 + lax.erf(gate * math.sqrt(0.5)))
    slope = share + gate * (jnp.exp(-0.5 * gate * gate) * (1.0 / math.sqrt(2.0 * math.pi)))
    hidden = (gate * share).astype(jnp.bfloat16)
    grad_gate = (grad_hidden * slope).astype(jnp.bfloat16)
    reduce_grad = dot(hidden, grad, ((0,), (0,)))
    expand_grad = dot(rows, grad_gate, ((0,), (0,)))
    if span:
        halves = [alternate(reduce_grad, span * ratio), alternate(expand_grad, span)]
        for own in range(2):

            @pl.when(bit_ref[0] == own)
            def _():
                for i, pair in enumerate(halves):
                    sum_refs[2 * i][...] = pair[own]
                    sum_refs[2 * i + 1][...] = pair[1 - own]

    else:
        sum_refs[0][...] = reduce_grad.astype(jnp.bfloat16)
        sum_refs[1][...] = expand_grad.astype(jnp.bfloat16)
    first = pl.program_id(0) == 0
    @pl.when(first)
    def _():
        out_ref[...] = jnp.zeros_like(out_ref)
        back_ref[...] = jnp.zeros_like(back_ref)
    out_ref[...] += dot(hidden, reduce, ((1,), (0,)))
    back_ref[...] += dot(grad_gate, expand, ((1,), (1,)))


def ffn(rows, grad, others, per_device, hidden_width):
    count, width = rows.shape
    ratio = hidden_width // width
    part = TILE // ratio
    place = jnp.arange(TILE)
    chunk = per_device * ratio
    source = part * (place % chunk // per_device) + per_device * (place // chunk) + place % per_device
    order = (source[:, None] == place[None, :]).astype(jnp.bfloat16)
    whole = lambda shape: pl.BlockSpec(shape, lambda j: (0, 0))
    span = per_device if per_device % 8 == 0 and chunk % 16 == 0 else 0
    copies = 2 if span else 1
    sums = []
    for shape, block, at in (
        ((hidden_width, width), (TILE, width), lambda j: (j, 0)),
        ((width, hidden_width), (width, TILE), lambda j: (0, j)),
    ):
        part_of = lambda size: (size[0] // copies, size[1])
        sums += copies * [
            (pl.BlockSpec(part_of(block), at), jax.ShapeDtypeStruct(part_of(shape), jnp.bfloat16))
        ]
    return pl.pallas_call(
        functools.partial(ffn_body, ratio=ratio, span=span),
        grid=(hidden_width // TILE,),
        in_specs=[
            pl.BlockSpec(memory_space=pltpu.SMEM),
            whole((count, width)),
            whole((count, width)),
            pl.BlockSpec((width, TILE), lambda j: (0, hidden_width // TILE + j)),
            pl.BlockSpec((part, hidden_width), lambda j: (j, 0)),
            whole((TILE, TILE)),
        ],
        out_specs=[whole((count, width)), whole((count, width))] + [spec for spec, _ in sums],
        out_shape=2 * [jax.ShapeDtypeStruct((count, width), jnp.float32)]
        + [shape for _, shape in sums],
        compiler_params=pltpu.CompilerParams(
            dimension_semantics=("arbitrary",), vmem_limit_bytes=48 << 20
        ),
        name="ffn",
    )(own_bit("seq", 0).astype(jnp.int32).reshape(1), rows, grad, others, others, order)


def stack_heads(block):
    left = lax.broadcasted_iota(jnp.int32, block.shape, 1) < HEAD_DIM
    none = jnp.zeros_like(block)
    return jnp.concatenate([jnp.where(left, block, none), jnp.where(left, none, block)], axis=0)


def join_heads(stacked):
    count = stacked.shape[0] // 2
    left = lax.broadcasted_iota(jnp.int32, (count, LANES), 1) < HEAD_DIM
    return jnp.where(left, stacked[:count], stacked[count:])


def pair_probs(query, key, length):
    scores = dot(key, query, ((1,), (1,)))
    if length is not None:
        row = lax.broadcasted_iota(jnp.int32, scores.shape, 0)
        column = lax.broadcasted_iota(jnp.int32, scores.shape, 1) % (scores.shape[1] // 2)
        scores = jnp.where((row <= column) & (row < length), scores, -1e30)
    spread = jnp.exp(scores - jnp.max(scores, axis=0, keepdims=True))
    return spread * (1.0 / jnp.sum(spread, axis=0, keepdims=True))


def scaled(block):
    return block * jnp.asarray(1.0 / math.sqrt(HEAD_DIM), block.dtype)


def attend_body(table_ref, query_ref, key_ref, value_ref, out_ref, *, causal):
    length = table_ref[pl.program_id(0)] if causal else None
    for start in range(0, HEADS * HEAD_DIM, LANES):
        lanes = slice(start, start + LANES)
        query = stack_heads(scaled(query_ref[0, :, lanes]))
        probs = pair_probs(query, key_ref[0, :, lanes], length).astype(jnp.bfloat16)
        out_ref[0, :, lanes] = join_heads(dot(probs, value_ref[0, :, lanes], ((0,), (0,)))).astype(jnp.bfloat16)


def attend_back_body(table_ref, query_ref, key_ref, value_ref, grad_ref, query_grad_ref, pair_grad_ref, *, causal):
    length = table_ref[pl.program_id(0)] if causal else None
    width = HEADS * HEAD_DIM
    for start in range(0, width, LANES):
        lanes = slice(start, start + LANES)
        query = stack_heads(scaled(query_ref[0, :, lanes]))
        grad = stack_heads(grad_ref[0, :, lanes])
        key, value = key_ref[0, :, lanes], value_ref[0, :, lanes]
        probs = pair_probs(query, key, length)
        grad_probs = dot(value, grad, ((1,), (1,)))
        grad_scores = probs * (grad_probs - jnp.sum(grad_probs * probs, axis=0, keepdims=True))
        grad_scores = grad_scores.astype(jnp.bfloat16)
        back = lambda left, right: dot(left, right, ((1,), (0,))).astype(jnp.bfloat16)
        grad_query = scaled(join_heads(dot(grad_scores, key, ((0,), (0,))))).astype(jnp.bfloat16)
        grad_key, grad_value = back(grad_scores, query), back(probs.astype(jnp.bfloat16), grad)
        query_grad_ref[0, :, lanes] = grad_query
        if causal:
            query_grad_ref[0, :, slice(width + start, width + start + LANES)] = grad_key
            query_grad_ref[0, :, slice(2 * width + start, 2 * width + start + LANES)] = grad_value
        else:
            pair_grad_ref[0, :, lanes] = grad_key
            pair_grad_ref[0, :, slice(width + start, width + start + LANES)] = grad_value


def attention(body, table, arrays, outs, name, heavy, routed=False):
    width = HEADS * HEAD_DIM
    captions = arrays[0][0].shape[0]
    own = arrays[0][0].shape[1]

    def spec(rows, cols, at):
        if routed and rows != own:
            return pl.BlockSpec((1, rows, cols), lambda c, place: (place[c], 0, at))
        return pl.BlockSpec((1, rows, cols), lambda c, place: (c, 0, at))

    work = heavy * 2 * captions * arrays[0][0].shape[1] * arrays[1][0].shape[1] * width
    return pl.pallas_call(
        body,
        grid_spec=pltpu.PrefetchScalarGridSpec(
            num_scalar_prefetch=1,
            grid=(captions,),
            in_specs=[spec(array.shape[1], width, at) for array, at in arrays],
            out_specs=[spec(rows, cols, 0) for rows, cols in outs],
        ),
        out_shape=[jax.ShapeDtypeStruct((captions, rows, cols), jnp.bfloat16) for rows, cols in outs],
        compiler_params=pltpu.CompilerParams(dimension_semantics=("arbitrary",), vmem_limit_bytes=48 << 20),
        cost_estimate=pl.CostEstimate(flops=work, transcendentals=0, bytes_accessed=0),
        name=name,
    )(table, *(array for array, _ in arrays))


def self_forward(packed, lengths):
    rows, width = packed.shape[1], HEADS * HEAD_DIM
    return attention(functools.partial(attend_body, causal=True), lengths,
        [(packed, 0), (packed, 1), (packed, 2)], [(rows, width)], "self_attention", 2)[0]


def cross_forward(query_rows, pair, place):
    return attention(functools.partial(attend_body, causal=False), place,
        [(query_rows, 0), (pair, 0), (pair, 1)], [query_rows.shape[1:]], "cross_attention", 2, True)[0]


def self_body(*refs):
    attend_back_body(*refs, None, causal=True)


def self_backward(packed, grad_rows, lengths):
    return attention(self_body, lengths,
        [(packed, 0), (packed, 1), (packed, 2), (grad_rows, 0)], [packed.shape[1:]], "self_backward", 5)[0]


def cross_backward(query_rows, pair, grad_rows, place):
    return attention(functools.partial(attend_back_body, causal=False), place,
        [(query_rows, 0), (pair, 0), (pair, 1), (grad_rows, 0)],
        [query_rows.shape[1:], pair.shape[1:]], "cross_backward", 5, True)


def index_bits():
    found = []
    for axis in ("dp", "seq"):
        count = lax.axis_size(axis)
        found += [(axis, bit) for bit in reversed(range(count.bit_length() - 1))]
    return found


def swap_pairs(axis, bit):
    return [(i, i ^ (1 << bit)) for i in range(lax.axis_size(axis))]


def own_bit(axis, bit):
    return (lax.axis_index(axis) >> bit) & 1


def gather_order(flip):
    far = [("dp", bit) for bit in range(1, lax.axis_size("dp").bit_length() - 1)][::-1]
    near = [[("dp", 0)], [("seq", bit) for bit in range(1, lax.axis_size("seq").bit_length() - 1)]]
    if flip:
        near = near[::-1]
    return far + near[0] + near[1] + [("seq", 0)]


class Gather:
    def __init__(self, part, flip):
        bits = index_bits()
        self.own = [own_bit(*place) for place in bits]
        self.known = [1] * len(bits)
        self.shape = part.shape
        self.piece = part.reshape((1,) * len(bits) + part.shape)
        self.whole = jnp.zeros((2,) * len(bits) + part.shape, part.dtype)
        self.whole = self.put(self.piece, self.own)
        self.left = gather_order(flip)

    def put(self, piece, starts):
        return lax.dynamic_update_slice(self.whole, piece, starts + [0] * len(self.shape))

    def starts(self):
        return [0 if size == 2 else bit for size, bit in zip(self.known, self.own)]

    def step(self):
        place = self.left.pop(0)
        dim = index_bits().index(place)
        starts = self.starts()
        if self.piece is None:
            self.piece = lax.dynamic_slice(
                self.whole, starts + [0] * len(self.shape), self.known + list(self.shape)
            )
        other = lax.ppermute(self.piece, place[0], swap_pairs(*place))
        starts[dim] = 1 - self.own[dim]
        self.whole = self.put(other, starts)
        self.known[dim] = 2
        self.piece = None
        return other

    def rows(self):
        return self.whole.reshape((-1,) + self.shape[1:])


class Scatter:
    def __init__(self, whole, flip, span):
        bits = index_bits()
        self.rows = whole.shape[0] >> len(bits)
        self.tail = whole.shape[1:]
        self.state = whole.reshape((2,) * len(bits) + (self.rows,) + self.tail)
        order = gather_order(flip)
        far = [place for place in order[:-3]][::-1]
        pairs = [far[i : i + span] for i in range(0, len(far), span)]
        self.left = [[order[-1]], [order[-2]], [order[-3]]] + pairs

    @classmethod
    def halved(cls, kept, given, flip, span):
        one = cls(jnp.concatenate([kept[:0], given[:0]]), flip, span)
        bits = len(index_bits())
        one.rows = kept.shape[0] >> (bits - 1)
        shape = (2,) * (bits - 1) + (1, one.rows) + one.tail
        place = one.left.pop(0)[0]
        other = lax.ppermute(given.reshape(shape), place[0], swap_pairs(*place))
        one.state = kept.reshape(shape) + other
        return one

    def part(self, places, turn):
        part = self.state
        for place, flipped in zip(places, turn):
            dim = index_bits().index(place)
            part = lax.dynamic_slice_in_dim(part, own_bit(*place) ^ flipped, 1, dim)
        return part

    def step(self):
        places = self.left.pop(0)
        axis = places[0][0]
        total = self.part(places, [0] * len(places))
        for turn in list(itertools.product((0, 1), repeat=len(places)))[1:]:
            mask = sum(flipped << place[1] for place, flipped in zip(places, turn))
            pairs = [(i, i ^ mask) for i in range(lax.axis_size(axis))]
            total = total + lax.ppermute(self.part(places, turn), axis, pairs)
        self.state = total

    def join(self, other):
        self.state = jnp.concatenate([self.state, other.state], axis=-1)
        self.tail = self.state.shape[-1:]

    def finish(self):
        while self.left:
            self.step()
        return self.state.reshape((self.rows,) + self.tail).astype(jnp.float32)


def advance(scatters, *values):
    held = lax.optimization_barrier(tuple(one.state for one in scatters) + values)
    for one, state in zip(scatters, held):
        one.state = state
        if one.left:
            one.step()
    values = held[len(scatters) :]
    return values[0] if len(values) == 1 else values


def swap(rows, k):
    if not k:
        return rows
    return lax.ppermute(rows, "seq", [(i, i ^ k) for i in range(lax.axis_size("seq"))])


def lay_body(*refs):
    start = 0
    for ref in refs[:-1]:
        refs[-1][:, start : start + ref.shape[1]] = ref[...]
        start += ref.shape[1]


def lay_side_by_side(pieces):
    width = sum(piece.shape[1] for piece in pieces)
    return pl.pallas_call(
        lay_body,
        out_shape=jax.ShapeDtypeStruct((pieces[0].shape[0], width), pieces[0].dtype),
        name="lay_side_by_side",
    )(*pieces)


def put_body(table_ref, *refs):
    for k, ref in enumerate(refs[:-1]):

        @pl.when(pl.program_id(0) == k)
        def _():
            refs[-1][...] = ref[...]


def put_rows(pieces, table):
    shape = pieces[0].shape
    return pl.pallas_call(
        put_body,
        grid_spec=pltpu.PrefetchScalarGridSpec(
            num_scalar_prefetch=1,
            grid=(len(pieces),),
            in_specs=[pl.BlockSpec(shape, lambda k, at: (0, 0, 0)) for _ in pieces],
            out_specs=pl.BlockSpec(shape, lambda k, at: (at[k], 0, 0)),
        ),
        out_shape=jax.ShapeDtypeStruct((len(pieces),) + shape[1:], pieces[0].dtype),
        compiler_params=pltpu.CompilerParams(dimension_semantics=("arbitrary",)),
        cost_estimate=pl.CostEstimate(
            flops=0, transcendentals=0, bytes_accessed=4 * len(pieces) * shape[1] * shape[2]
        ),
        name="put_rows",
    )(table, *pieces)


def shards(
    caption_tokens,
    image_tokens,
    caption_lengths,
    caption_image,
    norm_gain,
    norm_bias,
    self_packed,
    self_output,
    cross_query,
    cross_pair,
    cross_output,
    expand_weight,
    reduce_weight,
    cotangent,
):
    captions, seq_len, model_width = caption_tokens.shape
    peer_count = lax.axis_size("seq")
    position = lax.axis_index("seq")

    owner = (caption_image // captions % peer_count).reshape(peer_count, captions)
    slot = (caption_image % captions).reshape(peer_count, captions)
    peers = jnp.arange(peer_count)
    mine = (peers == position).astype(jnp.int32)
    place = jnp.sum(owner * mine[:, None], axis=0) ^ position
    asked = jnp.sum(jnp.where(owner == position, slot, 0), axis=1)
    turned = (peers[:, None] ^ position) == peers[None, :]
    asked = jnp.sum(jnp.where(turned, asked[None, :], 0), axis=1)
    norm_columns = jnp.pad(jnp.concatenate([norm_gain, norm_bias], axis=1), ((0, 0), (0, 122)))
    rows = self_packed.shape[0]
    ratio = reduce_weight.shape[0] // rows
    reduce_blocks = [reduce_weight[k * rows : (k + 1) * rows] for k in range(ratio)]
    wide = lax.all_gather(
        lay_side_by_side(
            reduce_blocks + [expand_weight, cross_pair, cross_query, cross_output]
        ),
        ("dp", "seq"),
        axis=0,
        tiled=True,
    )
    first_group = Gather(
        jnp.concatenate([self_packed, self_output, norm_columns], axis=1), False
    )
    first_group.step()
    first_group.whole, asked, place = lax.optimization_barrier((first_group.whole, asked, place))
    first_group.step()
    wanted = [lax.dynamic_slice_in_dim(image_tokens, asked[k], 1) for k in range(peer_count)]
    first_group.whole, *wanted = lax.optimization_barrier((first_group.whole, *wanted))
    while len(first_group.left) > 1:
        came = first_group.step()
    wanted = lax.optimization_barrier((*wanted, came))[:-1]
    paired = [swap(row, k) for k, row in enumerate(wanted)]
    first_group.step()
    first_group = first_group.rows()
    packed_weight = first_group[:, : 3 * model_width]
    output_weight = first_group[:, 3 * model_width : 4 * model_width]
    norm_values = first_group[:, 4 * model_width : 4 * model_width + 6].astype(jnp.float32)
    norm_gains, norm_shifts = norm_values[:, :3], norm_values[:, 3:]
    hidden_width = expand_weight.shape[1]
    narrower = wide[:, 2 * hidden_width :]
    pair_weight = narrower[:, : 2 * model_width]
    query_weight = narrower[:, 2 * model_width : 3 * model_width]
    cross_weight = narrower[:, 3 * model_width :]

    live_rows = jnp.arange(seq_len)[None, :] < caption_lengths[:, None]
    inputs = caption_tokens.astype(jnp.float32)
    normed_full, scaled_one, inverse_one = layer_norm(inputs, norm_gains[:, 0], norm_shifts[:, 0])
    normed_one = normed_full.astype(jnp.bfloat16)
    packed = project(normed_one, packed_weight).astype(jnp.bfloat16)
    attended = self_forward(packed, caption_lengths)
    *paired, attended = lax.optimization_barrier((*paired, attended))
    paired = jnp.concatenate(paired)
    after_self = inputs + project(attended, output_weight)
    normed_full_two, scaled_two, inverse_two = layer_norm(
        after_self, norm_gains[:, 1], norm_shifts[:, 1]
    )
    normed_two = normed_full_two.astype(jnp.bfloat16)
    image_pair = project(paired, pair_weight).astype(jnp.bfloat16)
    query_rows = project(normed_two, query_weight).astype(jnp.bfloat16)
    mixed_rows = cross_forward(query_rows, image_pair, place)
    branch = project(mixed_rows, cross_weight).astype(jnp.bfloat16)
    after_cross = after_self + branch.astype(jnp.float32)
    normed_full_three, scaled_three, inverse_three = layer_norm(
        after_cross, norm_gains[:, 2], norm_shifts[:, 2]
    )
    normed_three = normed_full_three.astype(jnp.bfloat16)
    grad_out = jnp.where(live_rows[..., None], cotangent, jnp.zeros_like(cotangent))
    flat = lambda member: member.reshape(-1, model_width)
    forward, backward, *parts = ffn(
        flat(normed_three), flat(grad_out), wide, rows, hidden_width
    )
    caption_out = jnp.where(
        live_rows[..., None], after_cross + forward.reshape(after_cross.shape), 0.0
    ).astype(jnp.bfloat16)

    narrow = lambda member: member.astype(jnp.bfloat16)
    if len(parts) == 4:
        reduce_sums = Scatter.halved(*parts[:2], True, 1)
        expand_sums = Scatter.halved(*parts[2:], False, 1)
    else:
        reduce_sums = Scatter(parts[0], True, 1)
        expand_sums = Scatter(parts[1], False, 1)
        reduce_sums.step()
        expand_sums.step()
    grad_norm_three, gain_three, shift_three = norm_back(
        backward.reshape(after_cross.shape), scaled_three, inverse_three, norm_gains[:, 2]
    )
    grad_second = grad_out.astype(jnp.float32) + grad_norm_three
    grad_branch = grad_second.astype(jnp.bfloat16)
    grad_cross_mixed = project_back(grad_branch, cross_weight).astype(jnp.bfloat16)
    grad_cross_mixed = advance([reduce_sums], grad_cross_mixed)
    grad_cross_mixed, grad_branch = advance([expand_sums], grad_cross_mixed, grad_branch)
    cross_output_grad = weight_grad(mixed_rows, grad_branch)
    grad_cross_rows, grad_pair = cross_backward(
        query_rows, image_pair, grad_cross_mixed, place
    )
    cross_pair_grad = weight_grad(paired, grad_pair)
    cross_sums = Scatter(
        narrow(jnp.concatenate([cross_pair_grad, cross_output_grad], axis=1)), True, 2
    )
    image_rows = project_back(grad_pair, pair_weight).astype(jnp.bfloat16)
    image_rows, grad_cross_rows = advance(
        [reduce_sums, expand_sums, cross_sums], image_rows, grad_cross_rows
    )
    cross_query_grad = weight_grad(normed_two, grad_cross_rows)
    grad_norm_two, gain_two, shift_two = norm_back(
        project_back(grad_cross_rows, query_weight).astype(jnp.bfloat16).astype(jnp.float32),
        scaled_two,
        inverse_two,
        norm_gains[:, 1],
    )
    grad_first = grad_second + grad_norm_two
    grad_self = grad_first.astype(jnp.bfloat16)
    self_output_grad = weight_grad(attended, grad_self)
    grad_self, image_rows = advance([reduce_sums, expand_sums, cross_sums], grad_self, image_rows)
    home = [swap(image_rows[k : k + 1], k) for k in range(peer_count)]
    grad_attended = project_back(grad_self, output_weight).astype(jnp.bfloat16)
    grad_packed = self_backward(packed, grad_attended, caption_lengths)
    grad_packed, *home = advance([reduce_sums, expand_sums, cross_sums], grad_packed, *home)
    self_packed_grad = weight_grad(normed_one, grad_packed)
    grad_norm_one, gain_one, shift_one = norm_back(
        project_back(grad_packed, packed_weight), scaled_one, inverse_one, norm_gains[:, 0]
    )
    caption_grad = (grad_first + grad_norm_one).astype(jnp.bfloat16)
    norm_sums = jnp.stack([gain_one, gain_two, gain_three, shift_one, shift_two, shift_three], axis=1)
    half = model_width // 2
    left = jnp.concatenate([cross_query_grad, self_output_grad, self_packed_grad[:, :half]], axis=1)
    right = jnp.concatenate(
        [self_packed_grad[:, half:], jnp.pad(norm_sums, ((0, 0), (0, 122)))], axis=1
    )
    left_sums = Scatter(narrow(left), True, 2)
    right_sums = Scatter(narrow(right), False, 2)
    left_sums.step()
    right_sums.step()
    groups = [cross_sums, reduce_sums, expand_sums, left_sums, right_sums]
    while len(left_sums.left) > 1:
        advance(groups)
    left_sums.join(right_sums)
    home = advance([left_sums], *home)
    image_grad = put_rows(list(home), asked)
    self_sums = left_sums.finish()
    reduce_grad, expand_grad = reduce_sums.finish(), expand_sums.finish()
    cross_sums = cross_sums.finish()
    last = 5 * model_width
    return (
        caption_out,
        caption_grad,
        image_grad,
        self_sums[:, last : last + 3],
        self_sums[:, last + 3 : last + 6],
        self_sums[:, 2 * model_width : last],
        self_sums[:, model_width : 2 * model_width],
        self_sums[:, :model_width],
        cross_sums[:, : 2 * model_width],
        cross_sums[:, 2 * model_width :],
        expand_grad,
        reduce_grad,
    )


def solution(mesh):
    placed = (
        P(("dp", "seq"), None, None),
        P(("dp", "seq"), None, None),
        P(("dp", "seq")),
        P("dp"),
        P(("dp", "seq"), None),
        P(("dp", "seq"), None),
        P(("dp", "seq"), None),
        P(("dp", "seq"), None),
        P(("dp", "seq"), None),
        P(("dp", "seq"), None),
        P(("dp", "seq"), None),
        P(("dp", "seq"), None),
        P(("dp", "seq"), None),
        P(("dp", "seq"), None, None),
    )
    return jax.shard_map(
        shards,
        mesh=mesh,
        in_specs=placed,
        out_specs=(
            P(("dp", "seq"), None, None),
            P(("dp", "seq"), None, None),
            P(("dp", "seq"), None, None),
            P(("dp", "seq"), None),
            P(("dp", "seq"), None),
            P(("dp", "seq"), None),
            P(("dp", "seq"), None),
            P(("dp", "seq"), None),
            P(("dp", "seq"), None),
            P(("dp", "seq"), None),
            P(("dp", "seq"), None),
            P(("dp", "seq"), None),
        ),
        check_vma=False,
    )
```
